32 devices in a mesh: gx: 2 (over x), gy: 4 (over y, core), gz: 4 (over z).
Axes of the slice: x: 2, y: 2, z: 4, core: 2. Of those that a mesh axis runs over, the one named last changes fastest.
Arguments:
- volume: float32 [32, 32, 1024], P('gz', 'gx', 'gy'), may hold values from -10 to 10
Outputs:
- diffused: float32 [32, 32, 1024], P('gz', 'gx', 'gy')
The draws below stay inside these ranges and needn't reach their ends.
All inputs are finite; a program needn't handle non-finite values.
Results may differ from the reference program's by a relative error of at most 0.0003.
Values sent between devices are 32-bit elements; how exact they have to be, the bound alone decides.
No kernel may reach another device: no remote copies, remote signals or barrier semaphores. Data moves between devices by JAX's collectives and lax.ppermute only.
A program may use at most 64 MiB of HBM per device.

```python
import math
import jax
import jax.numpy as jnp
from jax import lax

CZ = 8
CX = 16
NZ = 32
NX = 32
NY = 1024


def smooth_field(key, term_count):
    keys = jax.random.split(key, 4)
    directions = jax.random.normal(keys[0], (term_count, 3), jnp.float32)
    directions = directions / jnp.sqrt(jnp.sum(directions * directions, axis=1, keepdims=True) + 1e-06)
    wavelengths = jax.random.uniform(keys[1], (term_count,), jnp.float32, 40.0, 160.0)
    phases = jax.random.uniform(keys[2], (term_count,), jnp.float32, 0.0, 2.0 * math.pi)
    weights = jax.random.normal(keys[3], (term_count,), jnp.float32)
    z_pos = jnp.arange(NZ, dtype=jnp.float32)[:, None, None]
    x_pos = jnp.arange(NX, dtype=jnp.float32)[None, :, None]
    y_pos = jnp.arange(NY, dtype=jnp.float32)[None, None, :]
    field = jnp.zeros((NZ, NX, NY), jnp.float32)
    for term in range(term_count):
        rate = 2.0 * math.pi / wavelengths[term]
        angle = rate * (directions[term, 0] * z_pos + directions[term, 1] * x_pos + directions[term, 2] * y_pos) + phases[term]
        field = field + weights[term] * jnp.cos(angle)
    return field / math.sqrt(0.5 * term_count)


def draw_volume(key, part):
    keys = jax.random.split(key, 3)
    region = 1.5 * jnp.tanh(3.0 * smooth_field(keys[0], 6))
    loudness = 0.5 + 1.5 * jax.nn.sigmoid(2.0 * smooth_field(keys[1], 4))
    noise = jnp.clip(jax.random.normal(keys[2], (NZ, NX, NY), jnp.float32), -4.0, 4.0)
    values = region + loudness * noise
    return values.astype(jnp.float32)


def setup_inputs(seed: int = 0) -> dict:
    key_of = jax.random.split(jax.random.key(seed), 2)
    volume = draw_volume(jax.random.fold_in(key_of[1], 71), 0)
    return {"volume": volume}


kernel_taps = (0.41111229, 0.8007374, 1.0, 0.8007374, 0.41111229)
time_step = 3000.0
contrast = 0.1


def blur_valid(values, first_dim):
    weight_sum = sum(kernel_taps)
    for axis_dim in range(first_dim, first_dim + 3):
        out_size = values.shape[axis_dim] - 4
        blurred = (kernel_taps[0] / weight_sum) * lax.slice_in_dim(values, 0, out_size, axis=axis_dim)
        for offset in range(1, 5):
            blurred = blurred + (kernel_taps[offset] / weight_sum) * lax.slice_in_dim(values, offset, offset + out_size, axis=axis_dim)
        values = blurred
    return values


def gradients(values, first_dim):
    result = []
    for axis_dim in range(first_dim, first_dim + 3):
        cropped = values
        for other_dim in range(first_dim, first_dim + 3):
            if other_dim != axis_dim:
                cropped = lax.slice_in_dim(cropped, 1, cropped.shape[other_dim] - 1, axis=other_dim)
        length = cropped.shape[axis_dim] - 2
        forward = lax.slice_in_dim(cropped, 2, length + 2, axis=axis_dim)
        behind = lax.slice_in_dim(cropped, 0, length, axis=axis_dim)
        result.append((forward - behind) * 0.5)
    return result


def shifted(values, stride, axis_dim, fill_value):
    length = values.shape[axis_dim]
    if abs(stride) >= length:
        return jnp.full(values.shape, fill_value, values.dtype)
    pad_shape = list(values.shape)
    pad_shape[axis_dim] = abs(stride)
    padding = jnp.full(tuple(pad_shape), fill_value, values.dtype)
    if stride > 0:
        return jnp.concatenate([padding, lax.slice_in_dim(values, 0, length - stride, axis=axis_dim)], axis=axis_dim)
    return jnp.concatenate([lax.slice_in_dim(values, -stride, length, axis=axis_dim), padding], axis=axis_dim)


def every_other(values, first_row, axis_dim):
    return lax.slice_in_dim(values, first_row, values.shape[axis_dim], stride=2, axis=axis_dim)


def append_row(values, fill_value, axis_dim):
    row_shape = list(values.shape)
    row_shape[axis_dim] = 1
    return jnp.concatenate([values, jnp.full(tuple(row_shape), fill_value, values.dtype)], axis=axis_dim)


def reduce_solve(sub_diag, main_diag, super_diag, right_sides, axis_dim):
    length = main_diag.shape[axis_dim]
    if length == 1:
        return [right_side / main_diag for right_side in right_sides]
    if length % 2 == 1:
        sub_diag = append_row(sub_diag, 0.0, axis_dim)
        main_diag = append_row(main_diag, 1.0, axis_dim)
        super_diag = append_row(super_diag, 0.0, axis_dim)
        right_sides = [append_row(right_side, 0.0, axis_dim) for right_side in right_sides]
    even_sub = every_other(sub_diag, 0, axis_dim)
    odd_sub = every_other(sub_diag, 1, axis_dim)
    even_main = every_other(main_diag, 0, axis_dim)
    odd_main = every_other(main_diag, 1, axis_dim)
    even_super = every_other(super_diag, 0, axis_dim)
    odd_super = every_other(super_diag, 1, axis_dim)
    even_sides = [every_other(right_side, 0, axis_dim) for right_side in right_sides]
    odd_sides = [every_other(right_side, 1, axis_dim) for right_side in right_sides]
    lower_factor = -even_sub / shifted(odd_main, 1, axis_dim, 1.0)
    upper_factor = -even_super / odd_main
    reduced = reduce_solve(
        lower_factor * shifted(odd_sub, 1, axis_dim, 0.0),
        even_main + lower_factor * shifted(odd_super, 1, axis_dim, 0.0) + upper_factor * odd_sub,
        upper_factor * odd_super,
        [even_side + lower_factor * shifted(odd_side, 1, axis_dim, 0.0) + upper_factor * odd_side for even_side, odd_side in zip(even_sides, odd_sides)],
        axis_dim)
    result = []
    for even_part, odd_side in zip(reduced, odd_sides):
        odd_part = (odd_side - odd_sub * even_part - odd_super * shifted(even_part, -1, axis_dim, 0.0)) / odd_main
        joined = jnp.stack([even_part, odd_part], axis=axis_dim + 1)
        joined_shape = list(even_part.shape)
        joined_shape[axis_dim] = 2 * joined_shape[axis_dim]
        result.append(lax.slice_in_dim(joined.reshape(tuple(joined_shape)), 0, length, axis=axis_dim))
    return result


def inside_grid(squares, offsets, totals):
    full_shape = squares[0].shape
    inside_mask = None
    for axis_dim in range(3):
        global_index = offsets[axis_dim] + lax.broadcasted_iota(jnp.int32, full_shape, axis_dim)
        within = (global_index >= 0) & (global_index < totals[axis_dim])
        inside_mask = within if inside_mask is None else inside_mask & within
    return [jnp.where(inside_mask, square, 0.0) for square in squares]


def face_pairs(diffusivity, axis_dim, offset, total):
    cropped = diffusivity
    for other_dim in range(3):
        if other_dim != axis_dim:
            cropped = lax.slice_in_dim(cropped, 1, cropped.shape[other_dim] - 1, axis=other_dim)
    length = cropped.shape[axis_dim] - 2
    centre = lax.slice_in_dim(cropped, 1, length + 1, axis=axis_dim)
    following = lax.slice_in_dim(cropped, 2, length + 2, axis=axis_dim)
    before = lax.slice_in_dim(cropped, 0, length, axis=axis_dim)
    face_up = (centre + following) * 0.5
    face_down = (before + centre) * 0.5
    global_index = offset + lax.broadcasted_iota(jnp.int32, face_up.shape, axis_dim)
    face_up = jnp.where(global_index < total - 1, face_up, 0.0)
    face_down = jnp.where(global_index > 0, face_down, 0.0)
    return face_up, face_down


def line_system(values, face_up, face_down, axis_dim, stiffness):
    return reduce_solve(-stiffness * face_down, 1.0 + stiffness * (face_down + face_up), -stiffness * face_up, [values], axis_dim)[0]


def reference(volume):
    stiffness = 3.0 * time_step
    full_z, full_x, full_y = volume.shape
    padded = jnp.pad(volume, 6)

    def slab_work(slab_index):
        first_row = slab_index * CZ
        window = lax.dynamic_slice_in_dim(padded, first_row, CZ + 12, axis=0)
        blurred = blur_valid(window, 0)
        squares = inside_grid([slope * slope for slope in gradients(blurred, 0)], (first_row - 3, -3, -3), (full_z, full_x, full_y))
        diffusivity = [1.0 / (1.0 + blur_valid(square, 0) / (contrast * contrast)) for square in squares]
        up_z, down_z = face_pairs(diffusivity[0], 0, first_row, full_z)
        up_x, down_x = face_pairs(diffusivity[1], 1, 0, full_x)
        up_y, down_y = face_pairs(diffusivity[2], 2, 0, full_y)
        values = lax.dynamic_slice_in_dim(volume, first_row, CZ, axis=0)
        solved_x = line_system(values, up_x, down_x, 1, stiffness)
        solved_y = line_system(values, up_y, down_y, 2, stiffness)
        return solved_x + solved_y, up_z

    partial_sum, face_z = lax.map(slab_work, jnp.arange(full_z // CZ, dtype=jnp.int32))
    partial_sum = partial_sum.reshape((full_z, full_x, full_y))
    face_z = face_z.reshape((full_z, full_x, full_y))

    def column_work(slab_index):
        first_row = slab_index * CX
        values = lax.dynamic_slice_in_dim(volume, first_row, CX, axis=1)
        face_up = lax.dynamic_slice_in_dim(face_z, first_row, CX, axis=1)
        face_down = shifted(face_up, 1, 0, 0.0)
        return line_system(values, face_up, face_down, 0, stiffness)

    solved_z = lax.map(column_work, jnp.arange(full_x // CX, dtype=jnp.int32))
    solved_z = jnp.moveaxis(solved_z, 0, 1).reshape((full_z, full_x, full_y))
    return (partial_sum + solved_z) / 3.0
```

```python
import functools

import jax
import jax.numpy as jnp
from jax import lax
from jax.experimental import pallas as pl
from jax.experimental.pallas import tpu as pltpu
from jax.sharding import PartitionSpec as P

kernel_taps = (0.41111229, 0.8007374, 1.0, 0.8007374, 0.41111229)
time_step = 3000.0
contrast = 0.1
stiffness = 3.0 * time_step
halo = 6
lanes = 128
edge = 8
VMEM = pl.BlockSpec(memory_space=pltpu.VMEM)


def taps(scale=1.0):
    total = sum(kernel_taps)
    return tuple(scale * tap / total for tap in kernel_taps[:3])


def five(k, a, b, c, d, e):
    return k[0] * (a + e) + k[1] * (b + d) + k[2] * c


def lane_shift(tiles, k, wanted):
    count = len(tiles)
    rolled = [pltpu.roll(t, (-k) % lanes, axis=1) for t in tiles]
    lane = lax.broadcasted_iota(jnp.int32, tiles[0].shape, 1)
    out = []
    for t in wanted:
        if k > 0:
            out.append(jnp.where(lane < lanes - k, rolled[t], rolled[(t + 1) % count]))
        else:
            out.append(jnp.where(lane >= -k, rolled[t], rolled[(t - 1) % count]))
    return out


def lane_blur(k, tiles, wanted):
    s = {o: lane_shift(tiles, o, wanted) for o in (-2, -1, 1, 2)}
    return [five(k, s[-2][i], s[-1][i], tiles[t], s[1][i], s[2][i]) for i, t in enumerate(wanted)]


def merge(low, high):
    a0, an, g00, g0n, gnn, c = low
    b0, bn, h00, h0n, hnn, e = high
    w = c / (1.0 + c * (gnn + h00))
    flux = w * (b0 - an)
    by_left = w * g0n
    by_right = w * h0n
    joined = (a0 + g0n * flux, bn - h0n * flux, g00 - g0n * by_left, by_left * h0n, hnn - h0n * by_right, e)
    return joined, (flux, by_left, by_right)


def pick(upper, own, other):
    low = tuple(jnp.where(upper, o, m) for m, o in zip(own, other))
    high = tuple(jnp.where(upper, m, o) for m, o in zip(own, other))
    return low, high


def last_message(upper, seg):
    a0, an, g00, g0n, gnn, c = seg
    return (jnp.where(upper, a0, an), jnp.where(upper, g00, c / (1.0 + c * gnn)))


def bit_of(position, level):
    return (position // (2**level)) % 2 == 1


def climb(position, own, received):
    coefs = []
    for level, other in enumerate(received):
        low, high = pick(bit_of(position, level), own, other)
        own, coef = merge(low, high)
        coefs.append(coef)
    return own, coefs


def end_fluxes(position, own, received, final):
    seg, coefs = climb(position, own, received)
    top = len(received)
    upper = bit_of(position, top)
    mine = last_message(upper, seg)
    (low_a, low_y), (high_a, high_g) = pick(upper, mine, final)
    flux = low_y * (high_a - low_a) / (1.0 + low_y * high_g)
    left = jnp.where(upper, -flux, 0.0)
    right = jnp.where(upper, 0.0, flux)
    for level in reversed(range(top)):
        const, by_left, by_right = coefs[level]
        flux = const + by_right * right - by_left * left
        upper = bit_of(position, level)
        left, right = jnp.where(upper, -flux, left), jnp.where(upper, right, flux)
    return left, right


def eliminate(v, c, count, keep):
    a0 = an = v(0)
    g00 = g0n = gnn = jnp.ones_like(an)
    for i in range(count - 1):
        face = c(i)
        w = face / (1.0 + face * (gnn + 1.0))
        following = v(i + 1)
        d = following - an
        keep(i, w, d, g0n)
        flux = w * d
        a0 = a0 + g0n * flux
        an = following - flux
        hw = g0n * w
        g00 = g00 - g0n * hw
        g0n = hw
        gnn = 1.0 - w
    return a0, an, g00, g0n, gnn, c(count - 1)


def substitute(factors, count, left, right, emit):
    above = right
    for i in reversed(range(count - 1)):
        w, d, h = factors(i)
        flux = w * (d + above - h * left)
        emit(i + 1, above - flux)
        above = flux
    emit(0, above + left)


def strip_kernel(dims, swap, *refs):
    nz, nx, ny = dims
    if swap:
        zlo, v, zhi, xr, first, last = refs
        at_x = lax.axis_index("gx")
        keep_lo = jnp.where(at_x == 1, 1.0, 0.0)
        keep_hi = jnp.where(at_x == 0, 1.0, 0.0)
    else:
        zlo, v, zhi, xlo, xhi, first, last = refs
    width = nx + 2 * edge
    per = lanes // width

    def row(z, t):
        cols = slice(t * lanes, (t + 1) * lanes)
        if z < halo:
            mid = zlo[nz - halo + z, :, cols]
        elif z < halo + nz:
            mid = v[z - halo, :, cols]
        else:
            mid = zhi[z - halo - nz, :, cols]
        if swap:
            side = xr[z, :, cols]
            return [side * keep_lo, mid, side * keep_hi]
        return [xlo[z, :, cols], mid, xhi[z, :, cols]]

    for t, out, begin in ((0, first, 0), (ny // lanes - 1, last, lanes - edge)):
        for chunk in range((nz + 2 * halo) // per):
            rows = []
            for z in range(per):
                rows += row(chunk * per + z, t)
            turned = jnp.concatenate(rows, axis=0).T
            out[:, chunk * lanes:(chunk + 1) * lanes] = turned[begin:begin + edge, :]


def main_kernel(dims, counts, swap, *refs):
    nz, nx, ny = dims
    nt = ny // lanes
    own = tuple(range(nt))
    every = tuple(range(nt + 1))
    lines = nz * nx
    if swap:
        zlo, v, zhi, xr, yl, yr = refs[:6]
        refs = refs[6:]
    else:
        zlo, v, zhi, xlo, xhi, yl, yr = refs[:7]
        refs = refs[7:]
    (fz, fx, fy, cy_out, send_z, send_x, send_y,
     wh, zp, bb, t1, dxs, vs, cz, cxs, cys, ct, vt) = refs
    at_z, at_x, at_y = lax.axis_index("gz"), lax.axis_index("gx"), lax.axis_index("gy")
    width = nx + 2 * edge
    rows_b = nx + 8
    per = lanes // width
    k = taps()
    kt = taps(0.25 / (contrast * contrast))
    if swap:
        keep_lo = jnp.where(at_x == 1, 1.0, 0.0)
        keep_hi = jnp.where(at_x == 0, 1.0, 0.0)

    gap = jnp.zeros((lanes - 2 * edge, lanes), jnp.float32)
    for chunk in range((nz + 2 * halo) // per):
        cols = slice(chunk * lanes, (chunk + 1) * lanes)
        turned = jnp.concatenate([yr[:, cols], gap, yl[:, cols]], axis=0).T
        for z in range(per):
            wh[chunk * per + z] = turned[z * width:(z + 1) * width, :]

    def centre(z, t):
        cols = slice(t * lanes, (t + 1) * lanes)
        if z < halo:
            return zlo[nz - halo + z, :, cols]
        if z < halo + nz:
            return v[z - halo, :, cols]
        return zhi[z - halo - nz, :, cols]

    def z_blur(load, store, count, weights):
        window = [load(i) for i in range(4)]
        for i in range(count):
            window.append(load(i + 4))
            store(i, five(weights, *window))
            window.pop(0)

    nb = nz + 8
    for t in own:
        cols = slice(t * lanes, (t + 1) * lanes)

        def put(rows, scale=None, t=t):
            def store(i, value):
                zp[t, i, rows, :] = value if scale is None else value * scale
            return store

        z_blur(lambda z: centre(z, t), put(slice(edge, edge + nx)), nb, k)
        if swap:
            def both(i, value):
                zp[t, i, 0:edge, :] = value * keep_lo
                zp[t, i, edge + nx:width, :] = value * keep_hi
            z_blur(lambda z: xr[z, :, cols], both, nb, k)
        else:
            z_blur(lambda z: xlo[z, :, cols], put(slice(0, edge)), nb, k)
            z_blur(lambda z: xhi[z, :, cols], put(slice(edge + nx, width)), nb, k)

    def put_h(i, value):
        zp[nt, i] = value
    z_blur(lambda z: wh[z], put_h, nb, k)

    blank = jnp.zeros((edge, lanes), jnp.float32)
    for z in range(nb):
        along_x = [five(k, *[zp[t, z, 2 + o:2 + o + rows_b, :] for o in range(5)]) for t in every]
        done = lane_blur(k, along_x, every)
        for t in every:
            bb[t, z, 0:edge, :] = blank
            bb[t, z, edge:edge + rows_b, :] = done[t]
            bb[t, z, edge + rows_b:, :] = blank

    xi = at_x * nx + lax.broadcasted_iota(jnp.int32, (rows_b, lanes), 0) - 4
    x_in = (xi >= 0) & (xi < nx * counts[1])
    lane = lax.broadcasted_iota(jnp.int32, (rows_b, lanes), 1)
    not_first = (at_y > 0).astype(jnp.float32)
    not_last = (at_y < counts[2] - 1).astype(jnp.float32)
    y_in = jnp.where(lane < lanes // 2, not_last, not_first)
    x_mask = jnp.where(x_in, 1.0, 0.0)
    masks = [x_mask] * nt + [x_mask * y_in]

    def z_mask(z, value):
        if 0 <= z < nz:
            return value
        inside = (at_z > 0) if z < 0 else (at_z < counts[0] - 1)
        return value * inside.astype(jnp.float32)

    def tensor(square, count):
        for t in every:
            window = [square(t, z) for z in range(-2, 2)]
            for i in range(count):
                window.append(square(t, i + 2))
                t1[t, i, 0:rows_b, :] = five(kt, *window)
                window.pop(0)

    def finish(z, first_row, rows, wanted):
        along_x = [five(k, *[t1[t, z, first_row + o:first_row + o + rows, :] for o in range(5)]) for t in every]
        return [1.0 / (1.0 + value) for value in lane_blur(k, along_x, wanted)]

    for t in every:
        for z in range(nz + 1):
            t1[t, z, rows_b:, :] = blank

    def square_z(t, z):
        slope = bb[t, z + 5, edge:edge + rows_b, :] - bb[t, z + 3, edge:edge + rows_b, :]
        return z_mask(z, slope * slope * masks[t])

    tensor(square_z, nz + 1)
    before = None
    for z in range(nz + 1):
        here = finish(z, 2, nx, own)
        if before is not None:
            scale = 0.5 * stiffness
            if z == nz:
                scale = jnp.where(at_z < counts[0] - 1, scale, 0.0)
            for t in own:
                cz[z - 1, :, t * lanes:(t + 1) * lanes] = (before[t] + here[t]) * scale
        before = here

    def keep_z(i, w, d, h):
        fz[0, i], fz[1, i], fz[2, i] = w, d, h

    seg = eliminate(lambda i: v[i], lambda i: cz[i], nz, keep_z)
    for i, value in enumerate(seg if counts[0] > 2 else last_message(bit_of(at_z, 0), seg)):
        send_z[i] = value

    def square_x(t, z):
        slope = bb[t, z + 4, edge + 1:edge + 1 + rows_b, :] - bb[t, z + 4, edge - 1:edge - 1 + rows_b, :]
        return z_mask(z, slope * slope * masks[t])

    tensor(square_x, nz)
    for z in range(nz):
        here = finish(z, 2, rows_b, own)
        for t in own:
            dxs[t, z * rows_b:(z + 1) * rows_b, :] = here[t]
            vs[t, z * nx:(z + 1) * nx, :] = v[z, :, t * lanes:(t + 1) * lanes]
    for t in own:
        cols = slice(t * lanes, (t + 1) * lanes)
        here = dxs[t, pl.ds(0, nz, stride=rows_b), :]
        for x in range(nx):
            following = dxs[t, pl.ds(x + 1, nz, stride=rows_b), :]
            scale = 0.5 * stiffness
            if x == nx - 1:
                scale = jnp.where(at_x < counts[1] - 1, scale, 0.0)
            cxs[0, x, :, cols] = (here + following) * scale
            cxs[1, x, :, cols] = vs[t, pl.ds(x, nz, stride=nx), :]
            here = following

    def keep_x(i, w, d, h):
        fx[0, i], fx[1, i], fx[2, i] = w, d, h

    seg = eliminate(lambda i: cxs[1, i], lambda i: cxs[0, i], nx, keep_x)
    for i, value in enumerate(seg if counts[1] > 2 else last_message(bit_of(at_x, 0), seg)):
        send_x[i] = value

    def square_y_layer(z):
        tiles = [bb[t, z + 4, edge:edge + rows_b, :] for t in every]
        up, down = lane_shift(tiles, 1, every), lane_shift(tiles, -1, every)
        out = []
        for t in every:
            slope = up[t] - down[t]
            out.append(z_mask(z, slope * slope * masks[t]))
        return out

    window = [square_y_layer(z) for z in range(-2, 2)]
    for z in range(nz):
        window.append(square_y_layer(z + 2))
        for t in every:
            t1[t, z, 0:rows_b, :] = five(kt, *[layer[t] for layer in window])
        window.pop(0)
    for z in range(nz):
        here = finish(z, 2, nx, every)
        following = lane_shift(here, 1, own)
        for t in own:
            cys[t, z * nx:(z + 1) * nx, :] = (here[t] + following[t]) * (0.5 * stiffness)
    for t in own:
        ct[t * lanes:(t + 1) * lanes, :] = cys[t].T
        vt[t * lanes:(t + 1) * lanes, :] = vs[t].T
    closing = jnp.where(at_y < counts[2] - 1, 1.0, 0.0)
    ct[ny - 1:ny, :] = ct[ny - 1:ny, :] * closing

    steps = ny // 16
    segs = []
    for half in range(2):
        def at(ref, i, half=half):
            return ref[pl.ds(half * steps + i, 8, stride=2 * steps), :]

        def keep_y(i, w, d, h, half=half):
            fy[0, i, half], fy[1, i, half], fy[2, i, half] = w, d, h

        segs.append(eliminate(functools.partial(at, vt), functools.partial(at, ct), steps, keep_y))
    seg, coef = merge(segs[0], segs[1])
    for i in range(3):
        cy_out[0, i] = coef[i]
    for level in range(3):
        other = tuple(pltpu.roll(value, 8 - 2**level, axis=0) for value in seg)
        seg, coef = merge(seg, other)
        for i in range(3):
            cy_out[level + 1, i] = coef[i]
    seg = seg if counts[2] > 2 else last_message(bit_of(at_y, 0), seg)
    for i, value in enumerate(seg):
        send_y[i:i + 1, :] = value[0:1, :]


def summary(ref, axis, count):
    if axis == 2:
        return tuple(ref[i:i + 1, :] for i in range(count))
    return tuple(ref[i] for i in range(count))


def merge_kernel(level, counts, depths, axes, *refs):
    refs = list(refs)
    groups = [[refs.pop(0) for _ in range(level + 2)] for _ in axes]
    for axis, group, out in zip(axes, groups, refs):
        position = lax.axis_index(("gz", "gx", "gy")[axis])
        own, *received = [summary(ref, axis, 6) for ref in group]
        seg, _ = climb(position, own, received)
        if depths[axis] == level + 2:
            seg = last_message(bit_of(position, level + 1), seg)
        for i, value in enumerate(seg):
            if axis == 2:
                out[i:i + 1, :] = value
            else:
                out[i] = value


def last_kernel(dims, depths, *refs):
    nz, nx, ny = dims
    nt = ny // lanes
    refs = list(refs)
    v, fz, fx, fy, cy = [refs.pop(0) for _ in range(5)]
    groups = [[refs.pop(0) for _ in range(depths[axis] + 1)] for axis in range(3)]
    out, acc, st, sx = refs
    fluxes = []
    for axis, group in enumerate(groups):
        position = lax.axis_index(("gz", "gx", "gy")[axis])
        if depths[axis] == 1:
            upper = bit_of(position, 0)
            mine, final = [summary(ref, axis, 2) for ref in group]
            (low_a, low_y), (high_a, high_g) = pick(upper, mine, final)
            flux = low_y * (high_a - low_a) / (1.0 + low_y * high_g)
            fluxes.append((jnp.where(upper, -flux, 0.0), jnp.where(upper, 0.0, flux)))
        else:
            own, *received = [summary(ref, axis, 6) for ref in group[:-1]]
            fluxes.append(end_fluxes(position, own, received, summary(group[-1], axis, 2)))

    left, right = fluxes[2]
    left = jnp.broadcast_to(left, (8, lanes))
    right = jnp.broadcast_to(right, (8, lanes))
    sub = lax.broadcasted_iota(jnp.int32, (8, lanes), 0)
    for level in (2, 1, 0):
        stride = 2**level
        const, by_left, by_right = [cy[level + 1, i] for i in range(3)]
        flux = const + by_right * right - by_left * left
        lower = sub % (2 * stride) == 0
        left, right = (jnp.where(lower, left, -pltpu.roll(flux, stride, axis=0)),
                       jnp.where(lower, flux, pltpu.roll(right, stride, axis=0)))
    flux = cy[0, 0] + cy[0, 2] * right - cy[0, 1] * left
    steps = ny // 16
    for half, (a, b) in enumerate(((left, flux), (-flux, right))):
        def factors(i, half=half):
            return fy[0, i, half], fy[1, i, half], fy[2, i, half]

        def emit(i, value, half=half):
            st[pl.ds(half * steps + i, 8, stride=2 * steps), :] = value

        substitute(factors, steps, a, b, emit)

    def emit_x(i, value):
        for t in range(nt):
            sx[t, pl.ds(i, nz, stride=nx), :] = value[:, t * lanes:(t + 1) * lanes]

    substitute(lambda i: (fx[0, i], fx[1, i], fx[2, i]), nx, *fluxes[1], emit_x)

    def emit_z(i, value):
        acc[i] = value

    substitute(lambda i: (fz[0, i], fz[1, i], fz[2, i]), nz, *fluxes[0], emit_z)
    for t in range(nt):
        cols = slice(t * lanes, (t + 1) * lanes)
        turned = st[cols, :].T
        for z in range(nz):
            rows = slice(z * nx, (z + 1) * nx)
            total = acc[z, :, cols] + sx[t, rows, :] + turned[rows, :]
            out[z, :, cols] = v[z, :, cols] + total * (1.0 / 3.0)


def shift(value, axis, step):
    n = lax.axis_size(axis)
    return lax.ppermute(value, axis, [(i, i + step) for i in range(n) if 0 <= i + step < n])


def swap_bit(value, axis, level):
    n = lax.axis_size(axis)
    return lax.ppermute(value, axis, [(i, i ^ (2**level)) for i in range(n)])


def body(volume):
    dims = volume.shape
    nz, nx, ny = dims
    nt = ny // lanes
    names = ("gz", "gx", "gy")
    counts = tuple(lax.axis_size(name) for name in names)
    depths = tuple(count.bit_length() - 1 for count in counts)
    assert all(2**d == n and d >= 1 for d, n in zip(depths, counts))
    assert nz == 8 and nz * nx == lanes and nx >= 8
    swap = counts[1] == 2
    f32 = lambda *shape: jax.ShapeDtypeStruct(shape, jnp.float32)
    scratch = lambda *shape: pltpu.VMEM(shape, jnp.float32)
    call = functools.partial(pl.pallas_call)

    zlo = shift(volume, "gz", 1)
    zhi = shift(volume, "gz", -1)
    tall = jnp.concatenate([zlo[nz - halo:], volume, zhi[:halo]], axis=0)
    low_rows, high_rows = tall[:, :edge], tall[:, nx - edge:]
    if swap:
        sides = [swap_bit(jnp.where(lax.axis_index("gx") == 0, high_rows, low_rows), "gx", 0)]
    else:
        sides = [shift(high_rows, "gx", 1), shift(low_rows, "gx", -1)]
    high = nz + 2 * halo
    width = nx + 2 * edge
    flat = high * width
    first, last = call(
        functools.partial(strip_kernel, dims, swap),
        out_shape=[f32(edge, flat)] * 2,
        in_specs=[VMEM] * (3 + len(sides)), out_specs=[VMEM] * 2,
    )(zlo, volume, zhi, *sides)
    yl = shift(last, "gy", 1)
    yr = shift(first, "gy", -1)

    steps = ny // 16
    send_shape = lambda d: 6 if d > 1 else 2
    rows_b = nx + 8
    fz, fx, fy, cy, send_z, send_x, send_y = call(
        functools.partial(main_kernel, dims, counts, swap),
        out_shape=[f32(3, nz - 1, nx, ny), f32(3, nx - 1, nz, ny), f32(3, steps - 1, 2, 8, lanes), f32(4, 3, 8, lanes),
                   f32(send_shape(depths[0]), nx, ny), f32(send_shape(depths[1]), nz, ny), f32(8, lanes)],
        in_specs=[VMEM] * (5 + len(sides)), out_specs=[VMEM] * 7,
        scratch_shapes=[scratch(high, width, lanes), scratch(nt + 1, nz + 8, width, lanes),
                        scratch(nt + 1, nz + 8, rows_b + 2 * edge, lanes), scratch(nt + 1, nz + 1, rows_b + 8, lanes),
                        scratch(nt, nz * rows_b, lanes), scratch(nt, lanes, lanes), scratch(nz, nx, ny),
                        scratch(2, nx, nz, ny), scratch(nt, lanes, lanes), scratch(ny, lanes), scratch(ny, lanes)],
    )(zlo, volume, zhi, *sides, yl, yr)

    groups = [[send_z], [send_x], [send_y]]
    message = [send_z, send_x, send_y]
    for level in range(max(depths)):
        for axis in range(3):
            if level < depths[axis]:
                groups[axis].append(swap_bit(message[axis], names[axis], level))
        axes = [axis for axis in range(3) if depths[axis] > level + 1]
        if axes:
            shapes = []
            for axis in axes:
                count = 2 if depths[axis] == level + 2 else 6
                shapes.append(f32(8, lanes) if axis == 2 else f32(count, *((nx, ny) if axis == 0 else (nz, ny))))
            sent = call(
                functools.partial(merge_kernel, level, counts, depths, axes),
                out_shape=shapes,
                in_specs=[VMEM] * (len(axes) * (level + 2)), out_specs=[VMEM] * len(axes),
            )(*[ref for axis in axes for ref in groups[axis]])
            for axis, value in zip(axes, sent):
                message[axis] = value
    return call(
        functools.partial(last_kernel, dims, depths),
        out_shape=f32(*dims),
        in_specs=[VMEM] * (5 + sum(len(g) for g in groups)), out_specs=VMEM,
        scratch_shapes=[scratch(*dims), scratch(ny, lanes), scratch(nt, lanes, lanes)],
    )(volume, fz, fx, fy, cy, *groups[0], *groups[1], *groups[2])


def solution(mesh):
    return jax.shard_map(
        body,
        mesh=mesh,
        in_specs=(P("gz", "gx", "gy"),),
        out_specs=P("gz", "gx", "gy"),
        check_vma=False,
    )
```

```python
import functools

import jax
import jax.numpy as jnp
from jax import lax
from jax.experimental import pallas as pl
from jax.experimental.pallas import tpu as pltpu
from jax.sharding import PartitionSpec as P

kernel_taps = (0.41111229, 0.8007374, 1.0, 0.8007374, 0.41111229)
time_step = 3000.0
contrast = 0.1
stiffness = 3.0 * time_step
halo = 6
lanes = 128
edge = 8
VMEM = pl.BlockSpec(memory_space=pltpu.VMEM)


def taps(scale=1.0):
    total = sum(kernel_taps)
    return tuple(scale * tap / total for tap in kernel_taps[:3])


def five(k, a, b, c, d, e):
    return k[0] * (a + e) + k[1] * (b + d) + k[2] * c


def lane_shift(tiles, k, wanted):
    count = len(tiles)
    rolled = [pltpu.roll(t, (-k) % lanes, axis=1) for t in tiles]
    lane = lax.broadcasted_iota(jnp.int32, tiles[0].shape, 1)
    out = []
    for t in wanted:
        if k > 0:
            out.append(jnp.where(lane < lanes - k, rolled[t], rolled[(t + 1) % count]))
        else:
            out.append(jnp.where(lane >= -k, rolled[t], rolled[(t - 1) % count]))
    return out


def lane_blur(k, tiles, wanted):
    s = {o: lane_shift(tiles, o, wanted) for o in (-2, -1, 1, 2)}
    return [five(k, s[-2][i], s[-1][i], tiles[t], s[1][i], s[2][i]) for i, t in enumerate(wanted)]


def merge(low, high):
    a0, an, g00, g0n, gnn, c = low
    b0, bn, h00, h0n, hnn, e = high
    w = c / (1.0 + c * (gnn + h00))
    flux = w * (b0 - an)
    by_left = w * g0n
    by_right = w * h0n
    joined = (a0 + g0n * flux, bn - h0n * flux, g00 - g0n * by_left, by_left * h0n, hnn - h0n * by_right, e)
    return joined, (flux, by_left, by_right)


def pick(upper, own, other):
    low = tuple(jnp.where(upper, o, m) for m, o in zip(own, other))
    high = tuple(jnp.where(upper, m, o) for m, o in zip(own, other))
    return low, high


def last_message(upper, seg):
    a0, an, g00, g0n, gnn, c = seg
    return (jnp.where(upper, a0, an), jnp.where(upper, g00, c / (1.0 + c * gnn)))


def bit_of(position, level):
    return (position // (2**level)) % 2 == 1


def climb(position, own, received):
    coefs = []
    for level, other in enumerate(received):
        low, high = pick(bit_of(position, level), own, other)
        own, coef = merge(low, high)
        coefs.append(coef)
    return own, coefs


def end_fluxes(position, own, received, final):
    seg, coefs = climb(position, own, received)
    top = len(received)
    upper = bit_of(position, top)
    mine = last_message(upper, seg)
    (low_a, low_y), (high_a, high_g) = pick(upper, mine, final)
    flux = low_y * (high_a - low_a) / (1.0 + low_y * high_g)
    left = jnp.where(upper, -flux, 0.0)
    right = jnp.where(upper, 0.0, flux)
    for level in reversed(range(top)):
        const, by_left, by_right = coefs[level]
        flux = const + by_right * right - by_left * left
        upper = bit_of(position, level)
        left, right = jnp.where(upper, -flux, left), jnp.where(upper, right, flux)
    return left, right


def eliminate(v, c, count, keep):
    a0 = an = v(0)
    g00 = g0n = gnn = jnp.ones_like(an)
    for i in range(count - 1):
        face = c(i)
        w = face / (1.0 + face * (gnn + 1.0))
        following = v(i + 1)
        d = following - an
        keep(i, w, d, g0n)
        flux = w * d
        a0 = a0 + g0n * flux
        an = following - flux
        hw = g0n * w
        g00 = g00 - g0n * hw
        g0n = hw
        gnn = 1.0 - w
    return a0, an, g00, g0n, gnn, c(count - 1)


def substitute(factors, count, left, right, emit):
    above = right
    for i in reversed(range(count - 1)):
        w, d, h = factors(i)
        flux = w * (d + above - h * left)
        emit(i + 1, above - flux)
        above = flux
    emit(0, above + left)


def strip_kernel(dims, swap, *refs):
    nz, nx, ny = dims
    if swap:
        zlo, v, zhi, xr, first, last = refs
        at_x = lax.axis_index("gx")
        keep_lo = jnp.where(at_x == 1, 1.0, 0.0)
        keep_hi = jnp.where(at_x == 0, 1.0, 0.0)
    else:
        zlo, v, zhi, xlo, xhi, first, last = refs
    width = nx + 2 * edge
    per = lanes // width

    def row(z, t):
        cols = slice(t * lanes, (t + 1) * lanes)
        if z < halo:
            mid = zlo[nz - halo + z, :, cols]
        elif z < halo + nz:
            mid = v[z - halo, :, cols]
        else:
            mid = zhi[z - halo - nz, :, cols]
        if swap:
            side = xr[z, :, cols]
            return [side * keep_lo, mid, side * keep_hi]
        return [xlo[z, :, cols], mid, xhi[z, :, cols]]

    for t, out, begin in ((0, first, 0), (ny // lanes - 1, last, lanes - edge)):
        for chunk in range((nz + 2 * halo) // per):
            rows = []
            for z in range(per):
                rows += row(chunk * per + z, t)
            turned = jnp.concatenate(rows, axis=0).T
            out[:, chunk * lanes:(chunk + 1) * lanes] = turned[begin:begin + edge, :]


def main_kernel(dims, counts, swap, *refs):
    nz, nx, ny = dims
    nt = ny // lanes
    own = tuple(range(nt))
    every = tuple(range(nt + 1))
    lines = nz * nx
    if swap:
        zlo, v, zhi, xr, yl, yr = refs[:6]
        refs = refs[6:]
    else:
        zlo, v, zhi, xlo, xhi, yl, yr = refs[:7]
        refs = refs[7:]
    (fz, fx, fy, cy_out, send_z, send_x, send_y,
     wh, zp, bb, t1, dxs, vs, cz, cxs, cys, ct, vt) = refs
    at_z, at_x, at_y = lax.axis_index("gz"), lax.axis_index("gx"), lax.axis_index("gy")
    width = nx + 2 * edge
    rows_b = nx + 8
    per = lanes // width
    k = taps()
    kt = taps(0.25 / (contrast * contrast))
    if swap:
        keep_lo = jnp.where(at_x == 1, 1.0, 0.0)
        keep_hi = jnp.where(at_x == 0, 1.0, 0.0)

    gap = jnp.zeros((lanes - 2 * edge, lanes), jnp.float32)
    for chunk in range((nz + 2 * halo) // per):
        cols = slice(chunk * lanes, (chunk + 1) * lanes)
        turned = jnp.concatenate([yr[:, cols], gap, yl[:, cols]], axis=0).T
        for z in range(per):
            wh[chunk * per + z] = turned[z * width:(z + 1) * width, :]

    def centre(z, t):
        cols = slice(t * lanes, (t + 1) * lanes)
        if z < halo:
            return zlo[nz - halo + z, :, cols]
        if z < halo + nz:
            return v[z - halo, :, cols]
        return zhi[z - halo - nz, :, cols]

    def z_blur(load, store, count, weights):
        window = [load(i) for i in range(4)]
        for i in range(count):
            window.append(load(i + 4))
            store(i, five(weights, *window))
            window.pop(0)

    nb = nz + 8
    for t in own:
        cols = slice(t * lanes, (t + 1) * lanes)

        def put(rows, scale=None, t=t):
            def store(i, value):
                zp[t, i, rows, :] = value if scale is None else value * scale
            return store

        z_blur(lambda z: centre(z, t), put(slice(edge, edge + nx)), nb, k)
        if swap:
            def both(i, value):
                zp[t, i, 0:edge, :] = value * keep_lo
                zp[t, i, edge + nx:width, :] = value * keep_hi
            z_blur(lambda z: xr[z, :, cols], both, nb, k)
        else:
            z_blur(lambda z: xlo[z, :, cols], put(slice(0, edge)), nb, k)
            z_blur(lambda z: xhi[z, :, cols], put(slice(edge + nx, width)), nb, k)

    def put_h(i, value):
        zp[nt, i] = value
    z_blur(lambda z: wh[z], put_h, nb, k)

    blank = jnp.zeros((edge, lanes), jnp.float32)
    for z in range(nb):
        along_x = [five(k, *[zp[t, z, 2 + o:2 + o + rows_b, :] for o in range(5)]) for t in every]
        done = lane_blur(k, along_x, every)
        for t in every:
            bb[t, z, 0:edge, :] = blank
            bb[t, z, edge:edge + rows_b, :] = done[t]
            bb[t, z, edge + rows_b:, :] = blank

    xi = at_x * nx + lax.broadcasted_iota(jnp.int32, (rows_b, lanes), 0) - 4
    x_in = (xi >= 0) & (xi < nx * counts[1])
    lane = lax.broadcasted_iota(jnp.int32, (rows_b, lanes), 1)
    not_first = (at_y > 0).astype(jnp.float32)
    not_last = (at_y < counts[2] - 1).astype(jnp.float32)
    y_in = jnp.where(lane < lanes // 2, not_last, not_first)
    x_mask = jnp.where(x_in, 1.0, 0.0)
    masks = [x_mask] * nt + [x_mask * y_in]

    def z_mask(z, value):
        if 0 <= z < nz:
            return value
        inside = (at_z > 0) if z < 0 else (at_z < counts[0] - 1)
        return value * inside.astype(jnp.float32)

    def tensor(square, count):
        for t in every:
            window = [square(t, z) for z in range(-2, 2)]
            for i in range(count):
                window.append(square(t, i + 2))
                t1[t, i, 0:rows_b, :] = five(kt, *window)
                window.pop(0)

    def finish(z, first_row, rows, wanted):
        along_x = [five(k, *[t1[t, z, first_row + o:first_row + o + rows, :] for o in range(5)]) for t in every]
        return [1.0 / (1.0 + value) for value in lane_blur(k, along_x, wanted)]

    for t in every:
        for z in range(nz + 1):
            t1[t, z, rows_b:, :] = blank

    def square_z(t, z):
        slope = bb[t, z + 5, edge:edge + rows_b, :] - bb[t, z + 3, edge:edge + rows_b, :]
        return z_mask(z, slope * slope * masks[t])

    tensor(square_z, nz + 1)
    before = None
    for z in range(nz + 1):
        here = finish(z, 2, nx, own)
        if before is not None:
            scale = 0.5 * stiffness
            if z == nz:
                scale = jnp.where(at_z < counts[0] - 1, scale, 0.0)
            for t in own:
                cz[z - 1, :, t * lanes:(t + 1) * lanes] = (before[t] + here[t]) * scale
        before = here

    def keep_z(i, w, d, h):
        fz[0, i], fz[1, i], fz[2, i] = w, d, h

    seg = eliminate(lambda i: v[i], lambda i: cz[i], nz, keep_z)
    for i, value in enumerate(seg if counts[0] > 2 else last_message(bit_of(at_z, 0), seg)):
        send_z[i] = value

    def square_x(t, z):
        slope = bb[t, z + 4, edge + 1:edge + 1 + rows_b, :] - bb[t, z + 4, edge - 1:edge - 1 + rows_b, :]
        return z_mask(z, slope * slope * masks[t])

    tensor(square_x, nz)
    for z in range(nz):
        here = finish(z, 2, rows_b, own)
        for t in own:
            dxs[t, z * rows_b:(z + 1) * rows_b, :] = here[t]
            vs[t, z * nx:(z + 1) * nx, :] = v[z, :, t * lanes:(t + 1) * lanes]
    for t in own:
        cols = slice(t * lanes, (t + 1) * lanes)
        here = dxs[t, pl.ds(0, nz, stride=rows_b), :]
        for x in range(nx):
            following = dxs[t, pl.ds(x + 1, nz, stride=rows_b), :]
            scale = 0.5 * stiffness
            if x == nx - 1:
                scale = jnp.where(at_x < counts[1] - 1, scale, 0.0)
            cxs[0, x, :, cols] = (here + following) * scale
            cxs[1, x, :, cols] = vs[t, pl.ds(x, nz, stride=nx), :]
            here = following

    def keep_x(i, w, d, h):
        fx[0, i], fx[1, i], fx[2, i] = w, d, h

    seg = eliminate(lambda i: cxs[1, i], lambda i: cxs[0, i], nx, keep_x)
    for i, value in enumerate(seg if counts[1] > 2 else last_message(bit_of(at_x, 0), seg)):
        send_x[i] = value

    def square_y_layer(z):
        tiles = [bb[t, z + 4, edge:edge + rows_b, :] for t in every]
        up, down = lane_shift(tiles, 1, every), lane_shift(tiles, -1, every)
        out = []
        for t in every:
            slope = up[t] - down[t]
            out.append(z_mask(z, slope * slope * masks[t]))
        return out

    window = [square_y_layer(z) for z in range(-2, 2)]
    for z in range(nz):
        window.append(square_y_layer(z + 2))
        for t in every:
            t1[t, z, 0:rows_b, :] = five(kt, *[layer[t] for layer in window])
        window.pop(0)
    for z in range(nz):
        here = finish(z, 2, nx, every)
        following = lane_shift(here, 1, own)
        for t in own:
            cys[t, z * nx:(z + 1) * nx, :] = (here[t] + following[t]) * (0.5 * stiffness)
    for t in own:
        ct[t * lanes:(t + 1) * lanes, :] = cys[t].T
        vt[t * lanes:(t + 1) * lanes, :] = vs[t].T
    closing = jnp.where(at_y < counts[2] - 1, 1.0, 0.0)
    ct[ny - 1:ny, :] = ct[ny - 1:ny, :] * closing

    steps = ny // 16
    segs = []
    for half in range(2):
        def at(ref, i, half=half):
            return ref[pl.ds(half * steps + i, 8, stride=2 * steps), :]

        def keep_y(i, w, d, h, half=half):
            fy[0, i, half], fy[1, i, half], fy[2, i, half] = w, d, h

        segs.append(eliminate(functools.partial(at, vt), functools.partial(at, ct), steps, keep_y))
    seg, coef = merge(segs[0], segs[1])
    for i in range(3):
        cy_out[0, i] = coef[i]
    for level in range(3):
        other = tuple(pltpu.roll(value, 8 - 2**level, axis=0) for value in seg)
        seg, coef = merge(seg, other)
        for i in range(3):
            cy_out[level + 1, i] = coef[i]
    seg = seg if counts[2] > 2 else last_message(bit_of(at_y, 0), seg)
    for i, value in enumerate(seg):
        send_y[i:i + 1, :] = value[0:1, :]


def summary(ref, axis, count):
    if axis == 2:
        return tuple(ref[i:i + 1, :] for i in range(count))
    return tuple(ref[i] for i in range(count))


def merge_kernel(level, counts, depths, axes, *refs):
    refs = list(refs)
    groups = [[refs.pop(0) for _ in range(level + 2)] for _ in axes]
    for axis, group, out in zip(axes, groups, refs):
        position = lax.axis_index(("gz", "gx", "gy")[axis])
        own, *received = [summary(ref, axis, 6) for ref in group]
        seg, _ = climb(position, own, received)
        if depths[axis] == level + 2:
            seg = last_message(bit_of(position, level + 1), seg)
        for i, value in enumerate(seg):
            if axis == 2:
                out[i:i + 1, :] = value
            else:
                out[i] = value


def last_kernel(dims, depths, *refs):
    nz, nx, ny = dims
    nt = ny // lanes
    refs = list(refs)
    v, fz, fx, fy, cy = [refs.pop(0) for _ in range(5)]
    groups = [[refs.pop(0) for _ in range(depths[axis] + 1)] for axis in range(3)]
    out, acc, st, sx = refs
    fluxes = []
    for axis, group in enumerate(groups):
        position = lax.axis_index(("gz", "gx", "gy")[axis])
        if depths[axis] == 1:
            upper = bit_of(position, 0)
            mine, final = [summary(ref, axis, 2) for ref in group]
            (low_a, low_y), (high_a, high_g) = pick(upper, mine, final)
            flux = low_y * (high_a - low_a) / (1.0 + low_y * high_g)
            fluxes.append((jnp.where(upper, -flux, 0.0), jnp.where(upper, 0.0, flux)))
        else:
            own, *received = [summary(ref, axis, 6) for ref in group[:-1]]
            fluxes.append(end_fluxes(position, own, received, summary(group[-1], axis, 2)))

    left, right = fluxes[2]
    left = jnp.broadcast_to(left, (8, lanes))
    right = jnp.broadcast_to(right, (8, lanes))
    sub = lax.broadcasted_iota(jnp.int32, (8, lanes), 0)
    for level in (2, 1, 0):
        stride = 2**level
        const, by_left, by_right = [cy[level + 1, i] for i in range(3)]
        flux = const + by_right * right - by_left * left
        lower = sub % (2 * stride) == 0
        left, right = (jnp.where(lower, left, -pltpu.roll(flux, stride, axis=0)),
                       jnp.where(lower, flux, pltpu.roll(right, stride, axis=0)))
    flux = cy[0, 0] + cy[0, 2] * right - cy[0, 1] * left
    steps = ny // 16
    for half, (a, b) in enumerate(((left, flux), (-flux, right))):
        def factors(i, half=half):
            return fy[0, i, half], fy[1, i, half], fy[2, i, half]

        def emit(i, value, half=half):
            st[pl.ds(half * steps + i, 8, stride=2 * steps), :] = value

        substitute(factors, steps, a, b, emit)

    def emit_x(i, value):
        for t in range(nt):
            sx[t, pl.ds(i, nz, stride=nx), :] = value[:, t * lanes:(t + 1) * lanes]

    substitute(lambda i: (fx[0, i], fx[1, i], fx[2, i]), nx, *fluxes[1], emit_x)

    def emit_z(i, value):
        acc[i] = value

    substitute(lambda i: (fz[0, i], fz[1, i], fz[2, i]), nz, *fluxes[0], emit_z)
    for t in range(nt):
        cols = slice(t * lanes, (t + 1) * lanes)
        turned = st[cols, :].T
        for z in range(nz):
            rows = slice(z * nx, (z + 1) * nx)
            total = acc[z, :, cols] + sx[t, rows, :] + turned[rows, :]
            out[z, :, cols] = v[z, :, cols] + total * (1.0 / 3.0)


def shift(value, axis, step):
    n = lax.axis_size(axis)
    return lax.ppermute(value, axis, [(i, i + step) for i in range(n) if 0 <= i + step < n])


def swap_bit(value, axis, level):
    n = lax.axis_size(axis)
    return lax.ppermute(value, axis, [(i, i ^ (2**level)) for i in range(n)])


def body(volume):
    dims = volume.shape
    nz, nx, ny = dims
    nt = ny // lanes
    names = ("gz", "gx", "gy")
    counts = tuple(lax.axis_size(name) for name in names)
    depths = tuple(count.bit_length() - 1 for count in counts)
    assert all(2**d == n and d >= 1 for d, n in zip(depths, counts))
    assert nz == 8 and nz * nx == lanes and nx >= 8
    swap = counts[1] == 2
    f32 = lambda *shape: jax.ShapeDtypeStruct(shape, jnp.float32)
    scratch = lambda *shape: pltpu.VMEM(shape, jnp.float32)
    call = functools.partial(pl.pallas_call, compiler_params=pltpu.CompilerParams(vmem_limit_bytes=16 * 2**20))

    zlo = shift(volume, "gz", 1)
    zhi = shift(volume, "gz", -1)
    tall = jnp.concatenate([zlo[nz - halo:], volume, zhi[:halo]], axis=0)
    low_rows, high_rows = tall[:, :edge], tall[:, nx - edge:]
    if swap:
        sides = [swap_bit(jnp.where(lax.axis_index("gx") == 0, high_rows, low_rows), "gx", 0)]
    else:
        sides = [shift(high_rows, "gx", 1), shift(low_rows, "gx", -1)]
    high = nz + 2 * halo
    width = nx + 2 * edge
    flat = high * width
    first, last = call(
        functools.partial(strip_kernel, dims, swap),
        out_shape=[f32(edge, flat)] * 2,
        in_specs=[VMEM] * (3 + len(sides)), out_specs=[VMEM] * 2,
    )(zlo, volume, zhi, *sides)
    yl = shift(last, "gy", 1)
    yr = shift(first, "gy", -1)

    steps = ny // 16
    send_shape = lambda d: 6 if d > 1 else 2
    rows_b = nx + 8
    fz, fx, fy, cy, send_z, send_x, send_y = call(
        functools.partial(main_kernel, dims, counts, swap),
        out_shape=[f32(3, nz - 1, nx, ny), f32(3, nx - 1, nz, ny), f32(3, steps - 1, 2, 8, lanes), f32(4, 3, 8, lanes),
                   f32(send_shape(depths[0]), nx, ny), f32(send_shape(depths[1]), nz, ny), f32(8, lanes)],
        in_specs=[VMEM] * (5 + len(sides)), out_specs=[VMEM] * 7,
        scratch_shapes=[scratch(high, width, lanes), scratch(nt + 1, nz + 8, width, lanes),
                        scratch(nt + 1, nz + 8, rows_b + 2 * edge, lanes), scratch(nt + 1, nz + 1, rows_b + 8, lanes),
                        scratch(nt, nz * rows_b, lanes), scratch(nt, lanes, lanes), scratch(nz, nx, ny),
                        scratch(2, nx, nz, ny), scratch(nt, lanes, lanes), scratch(ny, lanes), scratch(ny, lanes)],
    )(zlo, volume, zhi, *sides, yl, yr)

    groups = [[send_z], [send_x], [send_y]]
    message = [send_z, send_x, send_y]
    for level in range(max(depths)):
        for axis in range(3):
            if level < depths[axis]:
                groups[axis].append(swap_bit(message[axis], names[axis], level))
        axes = [axis for axis in range(3) if depths[axis] > level + 1]
        if axes:
            shapes = []
            for axis in axes:
                count = 2 if depths[axis] == level + 2 else 6
                shapes.append(f32(8, lanes) if axis == 2 else f32(count, *((nx, ny) if axis == 0 else (nz, ny))))
            sent = call(
                functools.partial(merge_kernel, level, counts, depths, axes),
                out_shape=shapes,
                in_specs=[VMEM] * (len(axes) * (level + 2)), out_specs=[VMEM] * len(axes),
            )(*[ref for axis in axes for ref in groups[axis]])
            for axis, value in zip(axes, sent):
                message[axis] = value
    return call(
        functools.partial(last_kernel, dims, depths),
        out_shape=f32(*dims),
        in_specs=[VMEM] * (5 + sum(len(g) for g in groups)), out_specs=VMEM,
        scratch_shapes=[scratch(*dims), scratch(ny, lanes), scratch(nt, lanes, lanes)],
    )(volume, fz, fx, fy, cy, *groups[0], *groups[1], *groups[2])


def solution(mesh):
    return jax.shard_map(
        body,
        mesh=mesh,
        in_specs=(P("gz", "gx", "gy"),),
        out_specs=P("gz", "gx", "gy"),
        check_vma=False,
    )
```

```python
import functools

import jax
import jax.numpy as jnp
from jax import lax
from jax.experimental import pallas as pl
from jax.experimental.pallas import tpu as pltpu
from jax.sharding import PartitionSpec as P

kernel_taps = (0.41111229, 0.8007374, 1.0, 0.8007374, 0.41111229)
time_step = 3000.0
contrast = 0.1
stiffness = 3.0 * time_step
halo = 6
lanes = 128
edge = 8
VMEM = pl.BlockSpec(memory_space=pltpu.VMEM)


def taps(scale=1.0):
    total = sum(kernel_taps)
    return tuple(scale * tap / total for tap in kernel_taps[:3])


def five(k, a, b, c, d, e):
    return k[0] * (a + e) + k[1] * (b + d) + k[2] * c


def lane_shift(tiles, k, wanted):
    count = len(tiles)
    rolled = [pltpu.roll(t, (-k) % lanes, axis=1) for t in tiles]
    lane = lax.broadcasted_iota(jnp.int32, tiles[0].shape, 1)
    out = []
    for t in wanted:
        if k > 0:
            out.append(jnp.where(lane < lanes - k, rolled[t], rolled[(t + 1) % count]))
        else:
            out.append(jnp.where(lane >= -k, rolled[t], rolled[(t - 1) % count]))
    return out


def lane_blur(k, tiles, wanted):
    s = {o: lane_shift(tiles, o, wanted) for o in (-2, -1, 1, 2)}
    return [five(k, s[-2][i], s[-1][i], tiles[t], s[1][i], s[2][i]) for i, t in enumerate(wanted)]


def merge(low, high):
    a0, an, g00, g0n, gnn, c = low
    b0, bn, h00, h0n, hnn, e = high
    w = c / (1.0 + c * (gnn + h00))
    flux = w * (b0 - an)
    by_left = w * g0n
    by_right = w * h0n
    joined = (a0 + g0n * flux, bn - h0n * flux, g00 - g0n * by_left, by_left * h0n, hnn - h0n * by_right, e)
    return joined, (flux, by_left, by_right)


def pick(upper, own, other):
    low = tuple(jnp.where(upper, o, m) for m, o in zip(own, other))
    high = tuple(jnp.where(upper, m, o) for m, o in zip(own, other))
    return low, high


def last_message(upper, seg):
    a0, an, g00, g0n, gnn, c = seg
    return (jnp.where(upper, a0, an), jnp.where(upper, g00, c / (1.0 + c * gnn)))


def bit_of(position, level):
    return (position // (2**level)) % 2 == 1


def climb(position, own, received):
    coefs = []
    for level, other in enumerate(received):
        low, high = pick(bit_of(position, level), own, other)
        own, coef = merge(low, high)
        coefs.append(coef)
    return own, coefs


def end_fluxes(position, own, received, final):
    seg, coefs = climb(position, own, received)
    top = len(received)
    upper = bit_of(position, top)
    mine = last_message(upper, seg)
    (low_a, low_y), (high_a, high_g) = pick(upper, mine, final)
    flux = low_y * (high_a - low_a) / (1.0 + low_y * high_g)
    left = jnp.where(upper, -flux, 0.0)
    right = jnp.where(upper, 0.0, flux)
    for level in reversed(range(top)):
        const, by_left, by_right = coefs[level]
        flux = const + by_right * right - by_left * left
        upper = bit_of(position, level)
        left, right = jnp.where(upper, -flux, left), jnp.where(upper, right, flux)
    return left, right


def eliminate(v, c, count, keep):
    a0 = an = v(0)
    g00 = g0n = gnn = jnp.ones_like(an)
    for i in range(count - 1):
        face = c(i)
        w = face / (1.0 + face * (gnn + 1.0))
        following = v(i + 1)
        d = following - an
        keep(i, w, d, g0n)
        flux = w * d
        a0 = a0 + g0n * flux
        an = following - flux
        hw = g0n * w
        g00 = g00 - g0n * hw
        g0n = hw
        gnn = 1.0 - w
    return a0, an, g00, g0n, gnn, c(count - 1)


def substitute(factors, count, left, right, emit):
    above = right
    for i in reversed(range(count - 1)):
        w, d, h = factors(i)
        flux = w * (d + above - h * left)
        emit(i + 1, above - flux)
        above = flux
    emit(0, above + left)


def cut(t):
    return slice(t * lanes, (t + 1) * lanes)


def z_blur(load, store, count, weights):
    window = [load(i) for i in range(4)]
    for i in range(count):
        window.append(load(i + 4))
        store(i, five(weights, *window))
        window.pop(0)


def neighbours(position, refs, load):
    odd = position % 2 == 1
    first = load(refs[0])
    second = load(refs[1]) if len(refs) > 1 else jnp.zeros_like(first)
    return jnp.where(odd, first, second), jnp.where(odd, second, first)


def z_kernel(dims, pairs, *refs):
    nz, nx, ny = dims
    v, zr = refs[0], refs[1:1 + pairs[0]]
    out, *sends = refs[1 + pairs[0]:]
    at_z, at_x = lax.axis_index("gz"), lax.axis_index("gx")
    odd_x = at_x % 2 == 1
    for t in range(ny // lanes):
        cols = cut(t)
        below, above = {}, {}
        for z in range(halo):
            odd = at_z % 2 == 1
            first_top, first_low = zr[0][nz - halo + z, :, cols], zr[0][z, :, cols]
            if len(zr) > 1:
                second_top, second_low = zr[1][nz - halo + z, :, cols], zr[1][z, :, cols]
            else:
                second_top = second_low = jnp.zeros_like(first_low)
            below[z] = jnp.where(odd, first_top, second_top)
            above[z] = jnp.where(odd, second_low, first_low)

        def load(z):
            if z < halo:
                return below[z]
            return v[z - halo, :, cols] if z < halo + nz else above[z - halo - nz]

        def store(i, value):
            out[t, i] = value
            low, high = value[:halo], value[nx - halo:]
            rows = slice(i * halo, (i + 1) * halo)
            sends[0][rows, cols] = jnp.where(odd_x, low, high)
            if len(sends) > 1:
                sends[1][rows, cols] = jnp.where(odd_x, high, low)

        z_blur(load, store, nz + 8, taps())


def x_kernel(dims, pairs, *refs):
    nz, nx, ny = dims
    zb, xr = refs[0], refs[1:1 + pairs[1]]
    out, *rest = refs[1 + pairs[1]:]
    sends, wide = rest[:-1], rest[-1]
    at_x, at_y = lax.axis_index("gx"), lax.axis_index("gy")
    nt, nb, rows_b = ny // lanes, nz + 8, nx + 8
    k = taps()
    for t in range(nt):
        for i in range(nb):
            rows = slice(i * halo, (i + 1) * halo)
            low, high = neighbours(at_x, xr, lambda ref: ref[rows, cut(t)])
            wide[i, edge - halo:edge, :] = low
            wide[i, edge:edge + nx, :] = zb[t, i]
            wide[i, edge + nx:edge + nx + halo, :] = high
        for i in range(nb):
            out[t, i] = five(k, *[wide[i, 2 + o:2 + o + rows_b, :] for o in range(5)])
    odd_y = at_y % 2 == 1
    flat = lambda t, chunk: out.at[t].reshape(nb * rows_b, lanes)[chunk * lanes:(chunk + 1) * lanes, :]
    for chunk in range(nb * rows_b // lanes):
        first = flat(0, chunk).T[:edge, :]
        last = flat(nt - 1, chunk).T[lanes - edge:, :]
        sends[0][:, cut(chunk)] = jnp.where(odd_y, first, last)
        if len(sends) > 1:
            sends[1][:, cut(chunk)] = jnp.where(odd_y, last, first)


def grid_masks(dims, counts):
    nz, nx, ny = dims
    nt = ny // lanes
    at_z, at_x, at_y = lax.axis_index("gz"), lax.axis_index("gx"), lax.axis_index("gy")
    rows_b = nx + 8
    xi = at_x * nx + lax.broadcasted_iota(jnp.int32, (rows_b, lanes), 0) - 4
    x_mask = jnp.where((xi >= 0) & (xi < nx * counts[1]), 1.0, 0.0)
    lane = lax.broadcasted_iota(jnp.int32, (rows_b, lanes), 1)
    not_first = (at_y > 0).astype(jnp.float32)
    not_last = (at_y < counts[2] - 1).astype(jnp.float32)
    masks = [x_mask] * nt + [x_mask * jnp.where(lane < lanes // 2, not_last, not_first)]

    def z_mask(z, value):
        if 0 <= z < nz:
            return value
        inside = (at_z > 0) if z < 0 else (at_z < counts[0] - 1)
        return value * inside.astype(jnp.float32)

    return masks, z_mask


def tensor(t1, every, rows_b, square, count):
    kt = taps(0.25 / (contrast * contrast))
    for t in every:
        window = [square(t, z) for z in range(-2, 2)]
        for i in range(count):
            window.append(square(t, i + 2))
            t1[t, i, 0:rows_b, :] = five(kt, *window)
            window.pop(0)


def finish(t1, every, z, rows, wanted):
    k = taps()
    along_x = [five(k, *[t1[t, z, 2 + o:2 + o + rows, :] for o in range(5)]) for t in every]
    return [1.0 / (1.0 + value) for value in lane_blur(k, along_x, wanted)]


def main_kernel(dims, counts, pairs, *refs):
    nz, nx, ny = dims
    nt = ny // lanes
    own, every = tuple(range(nt)), tuple(range(nt + 1))
    v, xb, yr = refs[0], refs[1], refs[2:2 + pairs[2]]
    bb, fz, send_z, wh, t1, cz = refs[2 + pairs[2]:]
    at_z, at_y = lax.axis_index("gz"), lax.axis_index("gy")
    nb, rows_b = nz + 8, nx + 8
    k = taps()

    gap = jnp.zeros((lanes - 2 * edge, lanes), jnp.float32)
    for chunk in range(nb * rows_b // lanes):
        low, high = neighbours(at_y, yr, lambda ref: ref[:, cut(chunk)])
        wh[chunk * lanes:(chunk + 1) * lanes, :] = jnp.concatenate([high, gap, low], axis=0).T

    blank = jnp.zeros((edge, lanes), jnp.float32)
    for z in range(nb):
        tiles = [xb[t, z] for t in own] + [wh[z * rows_b:(z + 1) * rows_b, :]]
        done = lane_blur(k, tiles, every)
        for t in every:
            bb[t, z, 0:edge, :] = blank
            bb[t, z, edge:edge + rows_b, :] = done[t]
            bb[t, z, edge + rows_b:, :] = blank

    masks, z_mask = grid_masks(dims, counts)

    def square_z(t, z):
        slope = bb[t, z + 5, edge:edge + rows_b, :] - bb[t, z + 3, edge:edge + rows_b, :]
        return z_mask(z, slope * slope * masks[t])

    tensor(t1, every, rows_b, square_z, nz + 1)
    before = None
    for z in range(nz + 1):
        here = finish(t1, every, z, nx, own)
        if before is not None:
            scale = 0.5 * stiffness
            if z == nz:
                scale = jnp.where(at_z < counts[0] - 1, scale, 0.0)
            for t in own:
                cz[z - 1, :, cut(t)] = (before[t] + here[t]) * scale
        before = here

    def keep_z(i, w, d, h):
        fz[0, i], fz[1, i], fz[2, i] = w, d, h

    seg = eliminate(lambda i: v[i], lambda i: cz[i], nz, keep_z)
    for i, value in enumerate(seg if counts[0] > 2 else last_message(bit_of(at_z, 0), seg)):
        send_z[i] = value


def side_kernel(dims, counts, *refs):
    nz, nx, ny = dims
    nt = ny // lanes
    own, every = tuple(range(nt)), tuple(range(nt + 1))
    v, bb, fx, fy, cy_out, send_x, send_y, t1, dxs, vs, cxs, cys, ct, vt = refs
    at_x, at_y = lax.axis_index("gx"), lax.axis_index("gy")
    rows_b = nx + 8
    masks, z_mask = grid_masks(dims, counts)
    kt = taps(0.25 / (contrast * contrast))
    blank = jnp.zeros((edge, lanes), jnp.float32)
    for t in every:
        for z in range(nz):
            t1[t, z, rows_b:, :] = blank

    def square_x(t, z):
        slope = bb[t, z + 4, edge + 1:edge + 1 + rows_b, :] - bb[t, z + 4, edge - 1:edge - 1 + rows_b, :]
        return z_mask(z, slope * slope * masks[t])

    tensor(t1, every, rows_b, square_x, nz)
    for z in range(nz):
        here = finish(t1, every, z, rows_b, own)
        for t in own:
            dxs[t, z * rows_b:(z + 1) * rows_b, :] = here[t]
            vs[t, z * nx:(z + 1) * nx, :] = v[z, :, cut(t)]
    for t in own:
        here = dxs[t, pl.ds(0, nz, stride=rows_b), :]
        for x in range(nx):
            following = dxs[t, pl.ds(x + 1, nz, stride=rows_b), :]
            scale = 0.5 * stiffness
            if x == nx - 1:
                scale = jnp.where(at_x < counts[1] - 1, scale, 0.0)
            cxs[0, x, :, cut(t)] = (here + following) * scale
            cxs[1, x, :, cut(t)] = vs[t, pl.ds(x, nz, stride=nx), :]
            here = following

    def keep_x(i, w, d, h):
        fx[0, i], fx[1, i], fx[2, i] = w, d, h

    seg = eliminate(lambda i: cxs[1, i], lambda i: cxs[0, i], nx, keep_x)
    for i, value in enumerate(seg if counts[1] > 2 else last_message(bit_of(at_x, 0), seg)):
        send_x[i] = value

    def square_y_layer(z):
        tiles = [bb[t, z + 4, edge:edge + rows_b, :] for t in every]
        up, down = lane_shift(tiles, 1, every), lane_shift(tiles, -1, every)
        out = []
        for t in every:
            slope = up[t] - down[t]
            out.append(z_mask(z, slope * slope * masks[t]))
        return out

    window = [square_y_layer(z) for z in range(-2, 2)]
    for z in range(nz):
        window.append(square_y_layer(z + 2))
        for t in every:
            t1[t, z, 0:rows_b, :] = five(kt, *[layer[t] for layer in window])
        window.pop(0)
    for z in range(nz):
        here = finish(t1, every, z, nx, every)
        following = lane_shift(here, 1, own)
        for t in own:
            cys[t, z * nx:(z + 1) * nx, :] = (here[t] + following[t]) * (0.5 * stiffness)
    for t in own:
        ct[t * lanes:(t + 1) * lanes, :] = cys[t].T
        vt[t * lanes:(t + 1) * lanes, :] = vs[t].T
    closing = jnp.where(at_y < counts[2] - 1, 1.0, 0.0)
    ct[ny - 1:ny, :] = ct[ny - 1:ny, :] * closing

    steps = ny // 16
    segs = []
    for half in range(2):
        def at(ref, i, half=half):
            return ref[pl.ds(half * steps + i, 8, stride=2 * steps), :]

        def keep_y(i, w, d, h, half=half):
            fy[0, i, half], fy[1, i, half], fy[2, i, half] = w, d, h

        segs.append(eliminate(functools.partial(at, vt), functools.partial(at, ct), steps, keep_y))
    seg, coef = merge(segs[0], segs[1])
    for i in range(3):
        cy_out[0, i] = coef[i]
    for level in range(3):
        other = tuple(pltpu.roll(value, 8 - 2**level, axis=0) for value in seg)
        seg, coef = merge(seg, other)
        for i in range(3):
            cy_out[level + 1, i] = coef[i]
    seg = seg if counts[2] > 2 else last_message(bit_of(at_y, 0), seg)
    for i, value in enumerate(seg):
        send_y[i:i + 1, :] = value[0:1, :]


def summary(ref, axis, count):
    if axis == 2:
        return tuple(ref[i:i + 1, :] for i in range(count))
    return tuple(ref[i] for i in range(count))


def merge_kernel(level, counts, depths, axes, *refs):
    refs = list(refs)
    groups = [[refs.pop(0) for _ in range(level + 2)] for _ in axes]
    for axis, group, out in zip(axes, groups, refs):
        position = lax.axis_index(("gz", "gx", "gy")[axis])
        own, *received = [summary(ref, axis, 6) for ref in group]
        seg, _ = climb(position, own, received)
        if depths[axis] == level + 2:
            seg = last_message(bit_of(position, level + 1), seg)
        for i, value in enumerate(seg):
            if axis == 2:
                out[i:i + 1, :] = value
            else:
                out[i] = value


def last_kernel(dims, depths, *refs):
    nz, nx, ny = dims
    nt = ny // lanes
    refs = list(refs)
    v, fz, fx, fy, cy = [refs.pop(0) for _ in range(5)]
    groups = [[refs.pop(0) for _ in range(depths[axis] + 1)] for axis in range(3)]
    out, acc, st, sx = refs
    fluxes = []
    for axis, group in enumerate(groups):
        position = lax.axis_index(("gz", "gx", "gy")[axis])
        if depths[axis] == 1:
            upper = bit_of(position, 0)
            mine, final = [summary(ref, axis, 2) for ref in group]
            (low_a, low_y), (high_a, high_g) = pick(upper, mine, final)
            flux = low_y * (high_a - low_a) / (1.0 + low_y * high_g)
            fluxes.append((jnp.where(upper, -flux, 0.0), jnp.where(upper, 0.0, flux)))
        else:
            own, *received = [summary(ref, axis, 6) for ref in group[:-1]]
            fluxes.append(end_fluxes(position, own, received, summary(group[-1], axis, 2)))

    left, right = fluxes[2]
    left = jnp.broadcast_to(left, (8, lanes))
    right = jnp.broadcast_to(right, (8, lanes))
    sub = lax.broadcasted_iota(jnp.int32, (8, lanes), 0)
    for level in (2, 1, 0):
        stride = 2**level
        const, by_left, by_right = [cy[level + 1, i] for i in range(3)]
        flux = const + by_right * right - by_left * left
        lower = sub % (2 * stride) == 0
        left, right = (jnp.where(lower, left, -pltpu.roll(flux, stride, axis=0)),
                       jnp.where(lower, flux, pltpu.roll(right, stride, axis=0)))
    flux = cy[0, 0] + cy[0, 2] * right - cy[0, 1] * left
    steps = ny // 16
    for half, (a, b) in enumerate(((left, flux), (-flux, right))):
        def factors(i, half=half):
            return fy[0, i, half], fy[1, i, half], fy[2, i, half]

        def emit(i, value, half=half):
            st[pl.ds(half * steps + i, 8, stride=2 * steps), :] = value

        substitute(factors, steps, a, b, emit)

    def emit_x(i, value):
        for t in range(nt):
            sx[t, pl.ds(i, nz, stride=nx), :] = value[:, t * lanes:(t + 1) * lanes]

    substitute(lambda i: (fx[0, i], fx[1, i], fx[2, i]), nx, *fluxes[1], emit_x)

    def emit_z(i, value):
        acc[i] = value

    substitute(lambda i: (fz[0, i], fz[1, i], fz[2, i]), nz, *fluxes[0], emit_z)
    for t in range(nt):
        cols = slice(t * lanes, (t + 1) * lanes)
        turned = st[cols, :].T
        for z in range(nz):
            rows = slice(z * nx, (z + 1) * nx)
            total = acc[z, :, cols] + sx[t, rows, :] + turned[rows, :]
            out[z, :, cols] = v[z, :, cols] + total * (1.0 / 3.0)


def swap_bit(value, axis, level):
    n = lax.axis_size(axis)
    return lax.ppermute(value, axis, [(i, i ^ (2**level)) for i in range(n)])


def swap_pairs(values, axis):
    n = lax.axis_size(axis)
    out = []
    for start, value in enumerate(values):
        lows = range(start, n - 1, 2)
        out.append(lax.ppermute(value, axis, [(i, i + 1) for i in lows] + [(i + 1, i) for i in lows]))
    return out


def body(volume):
    dims = volume.shape
    nz, nx, ny = dims
    nt = ny // lanes
    names = ("gz", "gx", "gy")
    counts = tuple(lax.axis_size(name) for name in names)
    depths = tuple(count.bit_length() - 1 for count in counts)
    pairs = tuple(1 if count == 2 else 2 for count in counts)
    nb, rows_b = nz + 8, nx + 8
    assert all(2**d == n and d >= 1 for d, n in zip(depths, counts))
    assert nz == 8 and nz * nx == lanes and nx >= 8 and nb * rows_b % lanes == 0
    f32 = lambda *shape: jax.ShapeDtypeStruct(shape, jnp.float32)
    scratch = lambda *shape: pltpu.VMEM(shape, jnp.float32)

    def call(kernel, out_shape, scratch_shapes, *args):
        return pl.pallas_call(
            kernel, out_shape=out_shape, in_specs=[VMEM] * len(args), out_specs=[VMEM] * len(out_shape),
            scratch_shapes=scratch_shapes,
            compiler_params=pltpu.CompilerParams(vmem_limit_bytes=16 * 2**20),
        )(*args)

    z_received = swap_pairs([volume] * pairs[0], "gz")
    blurred_z, *x_sends = call(
        functools.partial(z_kernel, dims, pairs),
        [f32(nt, nb, nx, lanes)] + [f32(nb * halo, ny)] * pairs[1], [], volume, *z_received)
    x_received = swap_pairs(x_sends, "gx")
    blurred_x, *y_sends = call(
        functools.partial(x_kernel, dims, pairs),
        [f32(nt, nb, rows_b, lanes)] + [f32(edge, nb * rows_b)] * pairs[2],
        [scratch(nb, nx + 2 * edge, lanes)], blurred_z, *x_received)
    y_received = swap_pairs(y_sends, "gy")

    steps = ny // 16
    send_shape = lambda d: 6 if d > 1 else 2
    bb, fz, send_z = call(
        functools.partial(main_kernel, dims, counts, pairs),
        [f32(nt + 1, nb, rows_b + 2 * edge, lanes), f32(3, nz - 1, nx, ny), f32(send_shape(depths[0]), nx, ny)],
        [scratch(nb * rows_b, lanes), scratch(nt + 1, nz + 1, rows_b + 8, lanes), scratch(nz, nx, ny)],
        volume, blurred_x, *y_received)
    fx, fy, cy, send_x, send_y = call(
        functools.partial(side_kernel, dims, counts),
        [f32(3, nx - 1, nz, ny), f32(3, steps - 1, 2, 8, lanes), f32(4, 3, 8, lanes),
         f32(send_shape(depths[1]), nz, ny), f32(8, lanes)],
        [scratch(nt + 1, nz, rows_b + 8, lanes), scratch(nt, nz * rows_b, lanes), scratch(nt, lanes, lanes),
         scratch(2, nx, nz, ny), scratch(nt, lanes, lanes), scratch(ny, lanes), scratch(ny, lanes)],
        volume, bb)

    groups = [[send_z], [send_x], [send_y]]
    message = [send_z, send_x, send_y]
    for level in range(max(depths)):
        for axis in range(3):
            if level < depths[axis]:
                groups[axis].append(swap_bit(message[axis], names[axis], level))
        axes = [axis for axis in range(3) if depths[axis] > level + 1]
        if axes:
            shapes = []
            for axis in axes:
                count = 2 if depths[axis] == level + 2 else 6
                shapes.append(f32(8, lanes) if axis == 2 else f32(count, *((nx, ny) if axis == 0 else (nz, ny))))
            sent = call(functools.partial(merge_kernel, level, counts, depths, axes), shapes, [],
                        *[ref for axis in axes for ref in groups[axis]])
            for axis, value in zip(axes, sent):
                message[axis] = value
    return call(
        functools.partial(last_kernel, dims, depths), [f32(*dims)],
        [scratch(*dims), scratch(ny, lanes), scratch(nt, lanes, lanes)],
        volume, fz, fx, fy, cy, *groups[0], *groups[1], *groups[2])[0]


def solution(mesh):
    return jax.shard_map(
        body,
        mesh=mesh,
        in_specs=(P("gz", "gx", "gy"),),
        out_specs=P("gz", "gx", "gy"),
        check_vma=False,
    )
```

```python
import functools

import jax
import jax.numpy as jnp
from jax import lax
from jax.experimental import pallas as pl
from jax.experimental.pallas import tpu as pltpu
from jax.sharding import PartitionSpec as P

kernel_taps = (0.41111229, 0.8007374, 1.0, 0.8007374, 0.41111229)
time_step = 3000.0
contrast = 0.1
stiffness = 3.0 * time_step
halo = 6
lanes = 128
edge = 8
VMEM = pl.BlockSpec(memory_space=pltpu.VMEM)


def taps(scale=1.0):
    total = sum(kernel_taps)
    return tuple(scale * tap / total for tap in kernel_taps[:3])


def five(k, a, b, c, d, e):
    return k[0] * (a + e) + k[1] * (b + d) + k[2] * c


def lane_shift(tiles, k, wanted):
    count = len(tiles)
    rolled = [pltpu.roll(t, (-k) % lanes, axis=1) for t in tiles]
    lane = lax.broadcasted_iota(jnp.int32, tiles[0].shape, 1)
    out = []
    for t in wanted:
        if k > 0:
            out.append(jnp.where(lane < lanes - k, rolled[t], rolled[(t + 1) % count]))
        else:
            out.append(jnp.where(lane >= -k, rolled[t], rolled[(t - 1) % count]))
    return out


def lane_blur(k, tiles, wanted):
    s = {o: lane_shift(tiles, o, wanted) for o in (-2, -1, 1, 2)}
    return [five(k, s[-2][i], s[-1][i], tiles[t], s[1][i], s[2][i]) for i, t in enumerate(wanted)]


def merge(low, high):
    a0, an, g00, g0n, gnn, c = low
    b0, bn, h00, h0n, hnn, e = high
    w = c / (1.0 + c * (gnn + h00))
    flux = w * (b0 - an)
    by_left = w * g0n
    by_right = w * h0n
    joined = (a0 + g0n * flux, bn - h0n * flux, g00 - g0n * by_left, by_left * h0n, hnn - h0n * by_right, e)
    return joined, (flux, by_left, by_right)


def pick(upper, own, other):
    low = tuple(jnp.where(upper, o, m) for m, o in zip(own, other))
    high = tuple(jnp.where(upper, m, o) for m, o in zip(own, other))
    return low, high


def last_message(upper, seg):
    a0, an, g00, g0n, gnn, c = seg
    return (jnp.where(upper, a0, an), jnp.where(upper, g00, c / (1.0 + c * gnn)))


def bit_of(position, level):
    return (position // (2**level)) % 2 == 1


def climb(position, own, received):
    coefs = []
    for level, other in enumerate(received):
        low, high = pick(bit_of(position, level), own, other)
        own, coef = merge(low, high)
        coefs.append(coef)
    return own, coefs


def end_fluxes(position, own, received, final):
    seg, coefs = climb(position, own, received)
    top = len(received)
    upper = bit_of(position, top)
    mine = last_message(upper, seg)
    (low_a, low_y), (high_a, high_g) = pick(upper, mine, final)
    flux = low_y * (high_a - low_a) / (1.0 + low_y * high_g)
    left = jnp.where(upper, -flux, 0.0)
    right = jnp.where(upper, 0.0, flux)
    for level in reversed(range(top)):
        const, by_left, by_right = coefs[level]
        flux = const + by_right * right - by_left * left
        upper = bit_of(position, level)
        left, right = jnp.where(upper, -flux, left), jnp.where(upper, right, flux)
    return left, right


def eliminate(v, c, count, keep):
    a0 = an = v(0)
    g00 = g0n = gnn = jnp.ones_like(an)
    for i in range(count - 1):
        face = c(i)
        w = face / (1.0 + face * (gnn + 1.0))
        following = v(i + 1)
        d = following - an
        keep(i, w, d, g0n)
        flux = w * d
        a0 = a0 + g0n * flux
        an = following - flux
        hw = g0n * w
        g00 = g00 - g0n * hw
        g0n = hw
        gnn = 1.0 - w
    return a0, an, g00, g0n, gnn, c(count - 1)


def substitute(factors, count, left, right, emit):
    above = right
    for i in reversed(range(count - 1)):
        w, d, h = factors(i)
        flux = w * (d + above - h * left)
        emit(i + 1, above - flux)
        above = flux
    emit(0, above + left)


def cut(t):
    return slice(t * lanes, (t + 1) * lanes)


def z_blur(load, store, count, weights):
    window = [load(i) for i in range(4)]
    for i in range(count):
        window.append(load(i + 4))
        store(i, five(weights, *window))
        window.pop(0)


def neighbours(position, refs, load):
    odd = position % 2 == 1
    first = load(refs[0])
    second = load(refs[1]) if len(refs) > 1 else jnp.zeros_like(first)
    return jnp.where(odd, first, second), jnp.where(odd, second, first)


def z_kernel(dims, pairs, *refs):
    nz, nx, ny = dims
    nt, nb = ny // lanes, nz + 8
    v, zr = refs[0], refs[1:1 + pairs[0]]
    out, *sends = refs[1 + pairs[0]:]
    x_sends, y_sends = sends[:pairs[1]], sends[pairs[1]:pairs[1] + pairs[2]]
    corner_sends = sends[pairs[1] + pairs[2]:]
    odd_z = lax.axis_index("gz") % 2 == 1
    odd_x = lax.axis_index("gx") % 2 == 1
    odd_y = lax.axis_index("gy") % 2 == 1
    for t in range(nt):
        cols = cut(t)
        below, above = {}, {}
        for z in range(halo):
            first_top, first_low = zr[0][nz - halo + z, :, cols], zr[0][z, :, cols]
            if len(zr) > 1:
                second_top, second_low = zr[1][nz - halo + z, :, cols], zr[1][z, :, cols]
            else:
                second_top = second_low = jnp.zeros_like(first_low)
            below[z] = jnp.where(odd_z, first_top, second_top)
            above[z] = jnp.where(odd_z, second_low, first_low)

        def load(z):
            if z < halo:
                return below[z]
            return v[z - halo, :, cols] if z < halo + nz else above[z - halo - nz]

        def store(i, value):
            out[t, i] = value
            low, high = value[:halo], value[nx - halo:]
            rows = slice(i * halo, (i + 1) * halo)
            x_sends[0][rows, cols] = jnp.where(odd_x, low, high)
            if len(x_sends) > 1:
                x_sends[1][rows, cols] = jnp.where(odd_x, high, low)

        z_blur(load, store, nb, taps())

    def strips(first_tile, last_tile, targets):
        first = first_tile.T[:edge, :]
        last = last_tile.T[lanes - edge:, :]
        for f, target in enumerate(targets):
            ref, cols = target
            ref[:, cols] = jnp.where(odd_y, last, first) if f else jnp.where(odd_y, first, last)

    per = lanes // nx
    for chunk in range(nb // per):
        tiles = [out[t, chunk * per:(chunk + 1) * per].reshape(lanes, lanes) for t in (0, nt - 1)]
        strips(*tiles, [(ref, cut(chunk)) for ref in y_sends])
    pad = jnp.zeros((lanes - nb * halo, lanes), jnp.float32)
    for e, ref in enumerate(x_sends):
        tiles = [jnp.concatenate([ref[:, cut(t)], pad], axis=0) for t in (0, nt - 1)]
        strips(*tiles, [(corner, slice(None)) for corner in corner_sends[e * pairs[2]:(e + 1) * pairs[2]]])


def grid_masks(dims, counts):
    nz, nx, ny = dims
    nt = ny // lanes
    at_z, at_x, at_y = lax.axis_index("gz"), lax.axis_index("gx"), lax.axis_index("gy")
    rows_b = nx + 8
    xi = at_x * nx + lax.broadcasted_iota(jnp.int32, (rows_b, lanes), 0) - 4
    x_mask = jnp.where((xi >= 0) & (xi < nx * counts[1]), 1.0, 0.0)
    lane = lax.broadcasted_iota(jnp.int32, (rows_b, lanes), 1)
    not_first = (at_y > 0).astype(jnp.float32)
    not_last = (at_y < counts[2] - 1).astype(jnp.float32)
    masks = [x_mask] * nt + [x_mask * jnp.where(lane < lanes // 2, not_last, not_first)]

    def z_mask(z, value):
        if 0 <= z < nz:
            return value
        inside = (at_z > 0) if z < 0 else (at_z < counts[0] - 1)
        return value * inside.astype(jnp.float32)

    return masks, z_mask


def tensor(t1, every, rows_b, square, count):
    kt = taps(0.25 / (contrast * contrast))
    for t in every:
        window = [square(t, z) for z in range(-2, 2)]
        for i in range(count):
            window.append(square(t, i + 2))
            t1[t, i, 0:rows_b, :] = five(kt, *window)
            window.pop(0)


def finish(t1, every, z, rows, wanted):
    k = taps()
    along_x = [five(k, *[t1[t, z, 2 + o:2 + o + rows, :] for o in range(5)]) for t in every]
    return [1.0 / (1.0 + value) for value in lane_blur(k, along_x, wanted)]


def main_kernel(dims, counts, pairs, *refs):
    nz, nx, ny = dims
    nt = ny // lanes
    own, every = tuple(range(nt)), tuple(range(nt + 1))
    refs = list(refs)
    v, zb = refs.pop(0), refs.pop(0)
    xr = [refs.pop(0) for _ in range(pairs[1])]
    yr = [refs.pop(0) for _ in range(pairs[2])]
    corners = [[refs.pop(0) for _ in range(pairs[2])] for _ in range(pairs[1])]
    bb, fz, send_z, wide, t1, cz = refs
    at_z, at_x, at_y = lax.axis_index("gz"), lax.axis_index("gx"), lax.axis_index("gy")
    nb, rows_b = nz + 8, nx + 8
    k = taps()

    gap = jnp.zeros((lanes - 2 * edge, lanes), jnp.float32)

    def halo_tile(received, cols):
        low, high = neighbours(at_y, received, lambda ref: ref[:, cols])
        return jnp.concatenate([high, gap, low], axis=0).T

    def sides(t, load, sources):
        for i in range(nb):
            rows = slice(i * halo, (i + 1) * halo)
            low, high = neighbours(at_x, sources, lambda source: load(source, rows))
            wide[t, i, edge - halo:edge, :] = low
            wide[t, i, edge + nx:edge + nx + halo, :] = high

    for t in own:
        sides(t, lambda ref, rows: ref[rows, cut(t)], xr)
        for i in range(nb):
            wide[t, i, edge:edge + nx, :] = zb[t, i]
    sides(nt, lambda tile, rows: tile[rows, :], [halo_tile(group, slice(None)) for group in corners])
    per = lanes // nx
    for chunk in range(nb // per):
        turned = halo_tile(yr, cut(chunk))
        for i in range(per):
            wide[nt, chunk * per + i, edge:edge + nx, :] = turned[i * nx:(i + 1) * nx, :]

    blank = jnp.zeros((edge, lanes), jnp.float32)
    for z in range(nb):
        along_x = [five(k, *[wide[t, z, 2 + o:2 + o + rows_b, :] for o in range(5)]) for t in every]
        done = lane_blur(k, along_x, every)
        for t in every:
            bb[t, z, 0:edge, :] = blank
            bb[t, z, edge:edge + rows_b, :] = done[t]
            bb[t, z, edge + rows_b:, :] = blank

    masks, z_mask = grid_masks(dims, counts)

    def square_z(t, z):
        slope = bb[t, z + 5, edge:edge + rows_b, :] - bb[t, z + 3, edge:edge + rows_b, :]
        return z_mask(z, slope * slope * masks[t])

    tensor(t1, every, rows_b, square_z, nz + 1)
    before = None
    for z in range(nz + 1):
        here = finish(t1, every, z, nx, own)
        if before is not None:
            scale = 0.5 * stiffness
            if z == nz:
                scale = jnp.where(at_z < counts[0] - 1, scale, 0.0)
            for t in own:
                cz[z - 1, :, cut(t)] = (before[t] + here[t]) * scale
        before = here

    def keep_z(i, w, d, h):
        fz[0, i], fz[1, i], fz[2, i] = w, d, h

    seg = eliminate(lambda i: v[i], lambda i: cz[i], nz, keep_z)
    for i, value in enumerate(seg if counts[0] > 2 else last_message(bit_of(at_z, 0), seg)):
        send_z[i] = value


def side_kernel(dims, counts, *refs):
    nz, nx, ny = dims
    nt = ny // lanes
    own, every = tuple(range(nt)), tuple(range(nt + 1))
    v, bb, fx, fy, cy_out, send_x, send_y, t1, dxs, vs, cxs, cys, ct, vt = refs
    at_x, at_y = lax.axis_index("gx"), lax.axis_index("gy")
    rows_b = nx + 8
    masks, z_mask = grid_masks(dims, counts)
    kt = taps(0.25 / (contrast * contrast))
    blank = jnp.zeros((edge, lanes), jnp.float32)
    for t in every:
        for z in range(nz):
            t1[t, z, rows_b:, :] = blank

    def square_x(t, z):
        slope = bb[t, z + 4, edge + 1:edge + 1 + rows_b, :] - bb[t, z + 4, edge - 1:edge - 1 + rows_b, :]
        return z_mask(z, slope * slope * masks[t])

    tensor(t1, every, rows_b, square_x, nz)
    for z in range(nz):
        here = finish(t1, every, z, rows_b, own)
        for t in own:
            dxs[t, z * rows_b:(z + 1) * rows_b, :] = here[t]
            vs[t, z * nx:(z + 1) * nx, :] = v[z, :, cut(t)]
    for t in own:
        here = dxs[t, pl.ds(0, nz, stride=rows_b), :]
        for x in range(nx):
            following = dxs[t, pl.ds(x + 1, nz, stride=rows_b), :]
            scale = 0.5 * stiffness
            if x == nx - 1:
                scale = jnp.where(at_x < counts[1] - 1, scale, 0.0)
            cxs[0, x, :, cut(t)] = (here + following) * scale
            cxs[1, x, :, cut(t)] = vs[t, pl.ds(x, nz, stride=nx), :]
            here = following

    def keep_x(i, w, d, h):
        fx[0, i], fx[1, i], fx[2, i] = w, d, h

    seg = eliminate(lambda i: cxs[1, i], lambda i: cxs[0, i], nx, keep_x)
    for i, value in enumerate(seg if counts[1] > 2 else last_message(bit_of(at_x, 0), seg)):
        send_x[i] = value

    def square_y_layer(z):
        tiles = [bb[t, z + 4, edge:edge + rows_b, :] for t in every]
        up, down = lane_shift(tiles, 1, every), lane_shift(tiles, -1, every)
        out = []
        for t in every:
            slope = up[t] - down[t]
            out.append(z_mask(z, slope * slope * masks[t]))
        return out

    window = [square_y_layer(z) for z in range(-2, 2)]
    for z in range(nz):
        window.append(square_y_layer(z + 2))
        for t in every:
            t1[t, z, 0:rows_b, :] = five(kt, *[layer[t] for layer in window])
        window.pop(0)
    for z in range(nz):
        here = finish(t1, every, z, nx, every)
        following = lane_shift(here, 1, own)
        for t in own:
            cys[t, z * nx:(z + 1) * nx, :] = (here[t] + following[t]) * (0.5 * stiffness)
    for t in own:
        ct[t * lanes:(t + 1) * lanes, :] = cys[t].T
        vt[t * lanes:(t + 1) * lanes, :] = vs[t].T
    closing = jnp.where(at_y < counts[2] - 1, 1.0, 0.0)
    ct[ny - 1:ny, :] = ct[ny - 1:ny, :] * closing

    steps = ny // 16
    segs = []
    for half in range(2):
        def at(ref, i, half=half):
            return ref[pl.ds(half * steps + i, 8, stride=2 * steps), :]

        def keep_y(i, w, d, h, half=half):
            fy[0, i, half], fy[1, i, half], fy[2, i, half] = w, d, h

        segs.append(eliminate(functools.partial(at, vt), functools.partial(at, ct), steps, keep_y))
    seg, coef = merge(segs[0], segs[1])
    for i in range(3):
        cy_out[0, i] = coef[i]
    for level in range(3):
        other = tuple(pltpu.roll(value, 8 - 2**level, axis=0) for value in seg)
        seg, coef = merge(seg, other)
        for i in range(3):
            cy_out[level + 1, i] = coef[i]
    seg = seg if counts[2] > 2 else last_message(bit_of(at_y, 0), seg)
    for i, value in enumerate(seg):
        send_y[i:i + 1, :] = value[0:1, :]


def summary(ref, axis, count):
    if axis == 2:
        return tuple(ref[i:i + 1, :] for i in range(count))
    return tuple(ref[i] for i in range(count))


def merge_kernel(level, counts, depths, axes, *refs):
    refs = list(refs)
    groups = [[refs.pop(0) for _ in range(level + 2)] for _ in axes]
    for axis, group, out in zip(axes, groups, refs):
        position = lax.axis_index(("gz", "gx", "gy")[axis])
        own, *received = [summary(ref, axis, 6) for ref in group]
        seg, _ = climb(position, own, received)
        if depths[axis] == level + 2:
            seg = last_message(bit_of(position, level + 1), seg)
        for i, value in enumerate(seg):
            if axis == 2:
                out[i:i + 1, :] = value
            else:
                out[i] = value


def last_kernel(dims, depths, *refs):
    nz, nx, ny = dims
    nt = ny // lanes
    refs = list(refs)
    v, fz, fx, fy, cy = [refs.pop(0) for _ in range(5)]
    groups = [[refs.pop(0) for _ in range(depths[axis] + 1)] for axis in range(3)]
    out, acc, st, sx = refs
    fluxes = []
    for axis, group in enumerate(groups):
        position = lax.axis_index(("gz", "gx", "gy")[axis])
        if depths[axis] == 1:
            upper = bit_of(position, 0)
            mine, final = [summary(ref, axis, 2) for ref in group]
            (low_a, low_y), (high_a, high_g) = pick(upper, mine, final)
            flux = low_y * (high_a - low_a) / (1.0 + low_y * high_g)
            fluxes.append((jnp.where(upper, -flux, 0.0), jnp.where(upper, 0.0, flux)))
        else:
            own, *received = [summary(ref, axis, 6) for ref in group[:-1]]
            fluxes.append(end_fluxes(position, own, received, summary(group[-1], axis, 2)))

    left, right = fluxes[2]
    left = jnp.broadcast_to(left, (8, lanes))
    right = jnp.broadcast_to(right, (8, lanes))
    sub = lax.broadcasted_iota(jnp.int32, (8, lanes), 0)
    for level in (2, 1, 0):
        stride = 2**level
        const, by_left, by_right = [cy[level + 1, i] for i in range(3)]
        flux = const + by_right * right - by_left * left
        lower = sub % (2 * stride) == 0
        left, right = (jnp.where(lower, left, -pltpu.roll(flux, stride, axis=0)),
                       jnp.where(lower, flux, pltpu.roll(right, stride, axis=0)))
    flux = cy[0, 0] + cy[0, 2] * right - cy[0, 1] * left
    steps = ny // 16
    for half, (a, b) in enumerate(((left, flux), (-flux, right))):
        def factors(i, half=half):
            return fy[0, i, half], fy[1, i, half], fy[2, i, half]

        def emit(i, value, half=half):
            st[pl.ds(half * steps + i, 8, stride=2 * steps), :] = value

        substitute(factors, steps, a, b, emit)

    def emit_x(i, value):
        for t in range(nt):
            sx[t, pl.ds(i, nz, stride=nx), :] = value[:, t * lanes:(t + 1) * lanes]

    substitute(lambda i: (fx[0, i], fx[1, i], fx[2, i]), nx, *fluxes[1], emit_x)

    def emit_z(i, value):
        acc[i] = value

    substitute(lambda i: (fz[0, i], fz[1, i], fz[2, i]), nz, *fluxes[0], emit_z)
    for t in range(nt):
        cols = slice(t * lanes, (t + 1) * lanes)
        turned = st[cols, :].T
        for z in range(nz):
            rows = slice(z * nx, (z + 1) * nx)
            total = acc[z, :, cols] + sx[t, rows, :] + turned[rows, :]
            out[z, :, cols] = v[z, :, cols] + total * (1.0 / 3.0)


def swap_bit(value, axis, level):
    n = lax.axis_size(axis)
    return lax.ppermute(value, axis, [(i, i ^ (2**level)) for i in range(n)])


def pairs_of(n, start):
    lows = range(start, n - 1, 2)
    return [(i, i + 1) for i in lows] + [(i + 1, i) for i in lows]


def swap_pair(value, axis, start):
    return lax.ppermute(value, axis, pairs_of(lax.axis_size(axis), start))


def swap_corner(value, x_start, y_start):
    nx, ny = lax.axis_size("gx"), lax.axis_size("gy")
    moves = [(a * ny + c, b * ny + d) for a, b in pairs_of(nx, x_start) for c, d in pairs_of(ny, y_start)]
    return lax.ppermute(value, ("gx", "gy"), moves)


def body(volume):
    dims = volume.shape
    nz, nx, ny = dims
    nt = ny // lanes
    names = ("gz", "gx", "gy")
    counts = tuple(lax.axis_size(name) for name in names)
    depths = tuple(count.bit_length() - 1 for count in counts)
    pairs = tuple(1 if count == 2 else 2 for count in counts)
    nb, rows_b = nz + 8, nx + 8
    assert all(2**d == n and d >= 1 for d, n in zip(depths, counts))
    assert nz == 8 and nz * nx == lanes and nx >= 8 and nb * nx % lanes == 0 and nb * halo <= lanes
    f32 = lambda *shape: jax.ShapeDtypeStruct(shape, jnp.float32)
    scratch = lambda *shape: pltpu.VMEM(shape, jnp.float32)

    def call(kernel, out_shape, scratch_shapes, *args):
        return pl.pallas_call(
            kernel, out_shape=out_shape, in_specs=[VMEM] * len(args), out_specs=[VMEM] * len(out_shape),
            scratch_shapes=scratch_shapes,
            compiler_params=pltpu.CompilerParams(vmem_limit_bytes=16 * 2**20),
        )(*args)

    z_received = [swap_pair(volume, "gz", e) for e in range(pairs[0])]
    ex, ey = range(pairs[1]), range(pairs[2])
    blurred_z, *sends = call(
        functools.partial(z_kernel, dims, pairs),
        [f32(nt, nb, nx, lanes)] + [f32(nb * halo, ny) for e in ex] + [f32(edge, nb * nx) for f in ey]
        + [f32(edge, lanes) for e in ex for f in ey], [], volume, *z_received)
    x_received = [swap_pair(sends[e], "gx", e) for e in ex]
    y_received = [swap_pair(sends[pairs[1] + f], "gy", f) for f in reversed(ey)][::-1]
    corners = [swap_corner(sends[pairs[1] + pairs[2] + e * pairs[2] + f], e, f) for e in ex for f in ey]

    steps = ny // 16
    send_shape = lambda d: 6 if d > 1 else 2
    bb, fz, send_z = call(
        functools.partial(main_kernel, dims, counts, pairs),
        [f32(nt + 1, nb, rows_b + 2 * edge, lanes), f32(3, nz - 1, nx, ny), f32(send_shape(depths[0]), nx, ny)],
        [scratch(nt + 1, nb, nx + 2 * edge, lanes), scratch(nt + 1, nz + 1, rows_b + 8, lanes), scratch(nz, nx, ny)],
        volume, blurred_z, *x_received, *y_received, *corners)
    fx, fy, cy, send_x, send_y = call(
        functools.partial(side_kernel, dims, counts),
        [f32(3, nx - 1, nz, ny), f32(3, steps - 1, 2, 8, lanes), f32(4, 3, 8, lanes),
         f32(send_shape(depths[1]), nz, ny), f32(8, lanes)],
        [scratch(nt + 1, nz, rows_b + 8, lanes), scratch(nt, nz * rows_b, lanes), scratch(nt, lanes, lanes),
         scratch(2, nx, nz, ny), scratch(nt, lanes, lanes), scratch(ny, lanes), scratch(ny, lanes)],
        volume, bb)

    groups = [[send_z], [send_x], [send_y]]
    message = [send_z, send_x, send_y]
    for level in range(max(depths)):
        for axis in range(3):
            if level < depths[axis]:
                groups[axis].append(swap_bit(message[axis], names[axis], level))
        axes = [axis for axis in range(3) if depths[axis] > level + 1]
        if axes:
            shapes = []
            for axis in axes:
                count = 2 if depths[axis] == level + 2 else 6
                shapes.append(f32(8, lanes) if axis == 2 else f32(count, *((nx, ny) if axis == 0 else (nz, ny))))
            sent = call(functools.partial(merge_kernel, level, counts, depths, axes), shapes, [],
                        *[ref for axis in axes for ref in groups[axis]])
            for axis, value in zip(axes, sent):
                message[axis] = value
    return call(
        functools.partial(last_kernel, dims, depths), [f32(*dims)],
        [scratch(*dims), scratch(ny, lanes), scratch(nt, lanes, lanes)],
        volume, fz, fx, fy, cy, *groups[0], *groups[1], *groups[2])[0]


def solution(mesh):
    return jax.shard_map(
        body,
        mesh=mesh,
        in_specs=(P("gz", "gx", "gy"),),
        out_specs=P("gz", "gx", "gy"),
        check_vma=False,
    )
```

```python
import functools
import itertools

import jax
import jax.numpy as jnp
from jax import lax
from jax.experimental import pallas as pl
from jax.experimental.pallas import tpu as pltpu
from jax.sharding import PartitionSpec as P


kernel_taps = (0.41111229, 0.8007374, 1.0, 0.8007374, 0.41111229)
time_step = 3000.0
contrast = 0.1
stiffness = 3.0 * time_step
halo = 6
lanes = 128
edge = 8
VMEM = pl.BlockSpec(memory_space=pltpu.VMEM)


def taps(scale=1.0):
    total = sum(kernel_taps)
    return tuple(scale * tap / total for tap in kernel_taps[:3])


def five(k, a, b, c, d, e):
    return k[0] * (a + e) + k[1] * (b + d) + k[2] * c


def lane_shift(tiles, k, wanted):
    count = len(tiles)
    rolled = [pltpu.roll(t, (-k) % lanes, axis=1) for t in tiles]
    lane = lax.broadcasted_iota(jnp.int32, tiles[0].shape, 1)
    out = []
    for t in wanted:
        if k > 0:
            out.append(jnp.where(lane < lanes - k, rolled[t], rolled[(t + 1) % count]))
        else:
            out.append(jnp.where(lane >= -k, rolled[t], rolled[(t - 1) % count]))
    return out


def lane_blur(k, tiles, wanted):
    s = {o: lane_shift(tiles, o, wanted) for o in (-2, -1, 1, 2)}
    return [five(k, s[-2][i], s[-1][i], tiles[t], s[1][i], s[2][i]) for i, t in enumerate(wanted)]


def merge(low, high):
    a0, an, g00, g0n, gnn, c = low
    b0, bn, h00, h0n, hnn, e = high
    w = c / (1.0 + c * (gnn + h00))
    flux = w * (b0 - an)
    by_left = w * g0n
    by_right = w * h0n
    joined = (a0 + g0n * flux, bn - h0n * flux, g00 - g0n * by_left, by_left * h0n, hnn - h0n * by_right, e)
    return joined, (flux, by_left, by_right)


def pick(upper, own, other):
    low = tuple(jnp.where(upper, o, m) for m, o in zip(own, other))
    high = tuple(jnp.where(upper, m, o) for m, o in zip(own, other))
    return low, high


def last_message(upper, seg):
    a0, an, g00, _, gnn, c = seg
    return (jnp.where(upper, a0, an), jnp.where(upper, g00, c / (1.0 + c * gnn)))


def bit_of(position, level):
    return (position // (2**level)) % 2 == 1


def climb(position, own, received):
    coefs = []
    for level, other in enumerate(received):
        low, high = pick(bit_of(position, level), own, other)
        own, coef = merge(low, high)
        coefs.append(coef)
    return own, coefs


def end_fluxes(position, own, received, final):
    seg, coefs = climb(position, own, received)
    top = len(received)
    upper = bit_of(position, top)
    mine = last_message(upper, seg)
    (low_a, low_y), (high_a, high_g) = pick(upper, mine, final)
    flux = low_y * (high_a - low_a) / (1.0 + low_y * high_g)
    left = jnp.where(upper, -flux, 0.0)
    right = jnp.where(upper, 0.0, flux)
    for level in reversed(range(top)):
        const, by_left, by_right = coefs[level]
        flux = const + by_right * right - by_left * left
        upper = bit_of(position, level)
        left, right = jnp.where(upper, -flux, left), jnp.where(upper, right, flux)
    return left, right


def eliminate(v, c, count, keep):
    a0 = an = v(0)
    g00 = g0n = gnn = jnp.ones_like(an)
    for i in range(count - 1):
        face = c(i)
        w = face / (1.0 + face * (gnn + 1.0))
        following = v(i + 1)
        d = following - an
        keep(i, w, d, g0n)
        flux = w * d
        a0 = a0 + g0n * flux
        an = following - flux
        hw = g0n * w
        g00 = g00 - g0n * hw
        g0n = hw
        gnn = 1.0 - w
    return a0, an, g00, g0n, gnn, c(count - 1)


def substitute(factors, count, left, right, emit):
    above = right
    for i in reversed(range(count - 1)):
        w, d, h = factors(i)
        flux = w * (d + above - h * left)
        emit(i + 1, above - flux)
        above = flux
    emit(0, above + left)


def cut(t):
    return slice(t * lanes, (t + 1) * lanes)


def z_blur(load, store, count, weights):
    window = [load(i) for i in range(4)]
    for i in range(count):
        window.append(load(i + 4))
        store(i, five(weights, *window))
        window.pop(0)


def neighbours(position, count, refs, load):
    odd = position % 2 == 1
    first = load(refs[0])
    if len(refs) > 1:
        end = (position == 0) | (position == count - 1)
        second = jnp.where(end, 0.0, load(refs[1]))
    else:
        second = jnp.zeros_like(first)
    return jnp.where(odd, first, second), jnp.where(odd, second, first)


def open_kernel(dims, volume, kept, *sends):
    nz = dims[0]
    odd = lax.axis_index("gz") % 2 == 1
    for z in range(nz):
        kept[z] = volume[z]
    for z in range(halo):
        low, high = volume[z], volume[nz - halo + z]
        sends[0][z] = jnp.where(odd, low, high)
        if len(sends) > 1:
            sends[1][z] = jnp.where(odd, high, low)


def z_kernel(dims, counts, pairs, *refs):
    nz, nx, ny = dims
    nt, nb = ny // lanes, nz + 8
    v, zr = refs[0], refs[1:1 + pairs[0]]
    out, *sends = refs[1 + pairs[0]:]
    x_sends, y_sends = sends[:pairs[1]], sends[pairs[1]:pairs[1] + pairs[2]]
    corner_sends = sends[pairs[1] + pairs[2]:]
    at_z = lax.axis_index("gz")
    odd_x = lax.axis_index("gx") % 2 == 1
    odd_y = lax.axis_index("gy") % 2 == 1
    for t in range(nt):
        cols = cut(t)
        below = [neighbours(at_z, counts[0], zr, lambda ref: ref[z, :, cols])[0] for z in range(halo)]
        above = [neighbours(at_z, counts[0], zr, lambda ref: ref[z, :, cols])[1] for z in range(halo)]

        def load(z):
            if z < halo:
                return below[z]
            return v[z - halo, :, cols] if z < halo + nz else above[z - halo - nz]

        def store(i, value):
            out[t, i] = value
            low, high = value[:halo], value[nx - halo:]
            rows = slice(i * halo, (i + 1) * halo)
            x_sends[0][rows, cols] = jnp.where(odd_x, low, high)
            if len(x_sends) > 1:
                x_sends[1][rows, cols] = jnp.where(odd_x, high, low)

        z_blur(load, store, nb, taps())

    def strips(first_tile, last_tile, targets):
        first = first_tile.T[:edge, :]
        last = last_tile.T[lanes - edge:, :]
        for f, target in enumerate(targets):
            ref, cols = target
            ref[:, cols] = jnp.where(odd_y, last, first) if f else jnp.where(odd_y, first, last)

    per = lanes // nx
    for chunk in range(nb // per):
        tiles = [out[t, chunk * per:(chunk + 1) * per].reshape(lanes, lanes) for t in (0, nt - 1)]
        strips(*tiles, [(ref, cut(chunk)) for ref in y_sends])
    pad = jnp.zeros((lanes - nb * halo, lanes), jnp.float32)
    for e, ref in enumerate(x_sends):
        tiles = [jnp.concatenate([ref[:, cut(t)], pad], axis=0) for t in (0, nt - 1)]
        strips(*tiles, [(corner, slice(None)) for corner in corner_sends[e * pairs[2]:(e + 1) * pairs[2]]])


def grid_masks(dims, counts):
    nz, nx, ny = dims
    nt = ny // lanes
    at_z, at_x, at_y = lax.axis_index("gz"), lax.axis_index("gx"), lax.axis_index("gy")
    rows_b = nx + 8
    xi = at_x * nx + lax.broadcasted_iota(jnp.int32, (rows_b, lanes), 0) - 4
    x_mask = jnp.where((xi >= 0) & (xi < nx * counts[1]), 1.0, 0.0)
    lane = lax.broadcasted_iota(jnp.int32, (rows_b, lanes), 1)
    not_first = (at_y > 0).astype(jnp.float32)
    not_last = (at_y < counts[2] - 1).astype(jnp.float32)
    masks = [x_mask] * nt + [x_mask * jnp.where(lane < lanes // 2, not_last, not_first)]

    def z_mask(z, value):
        if 0 <= z < nz:
            return value
        inside = (at_z > 0) if z < 0 else (at_z < counts[0] - 1)
        return value * inside.astype(jnp.float32)

    return masks, z_mask


def tensor(t1, every, rows_b, square, count):
    kt = taps(0.25 / (contrast * contrast))
    for t in every:
        window = [square(t, z) for z in range(-2, 2)]
        for i in range(count):
            window.append(square(t, i + 2))
            t1[t, i, 0:rows_b, :] = five(kt, *window)
            window.pop(0)


def finish(t1, every, z, rows, wanted):
    k = taps()
    along_x = [five(k, *[t1[t, z, 2 + o:2 + o + rows, :] for o in range(5)]) for t in every]
    return [1.0 / (1.0 + value) for value in lane_blur(k, along_x, wanted)]


def main_kernel(dims, counts, pairs, *refs):
    nz, nx, ny = dims
    nt = ny // lanes
    own, every = tuple(range(nt)), tuple(range(nt + 1))
    refs = list(refs)
    v, zb = refs.pop(0), refs.pop(0)
    xr = [refs.pop(0) for _ in range(pairs[1])]
    yr = [refs.pop(0) for _ in range(pairs[2])]
    corners = [[refs.pop(0) for _ in range(pairs[2])] for _ in range(pairs[1])]
    bb, fz, send_z, wide, t1, cz = refs
    at_z, at_x, at_y = lax.axis_index("gz"), lax.axis_index("gx"), lax.axis_index("gy")
    nb, rows_b = nz + 8, nx + 8
    k = taps()

    gap = jnp.zeros((lanes - 2 * edge, lanes), jnp.float32)

    def halo_tile(received, cols):
        low, high = neighbours(at_y, counts[2], received, lambda ref: ref[:, cols])
        return jnp.concatenate([high, gap, low], axis=0).T

    def sides(t, load, sources):
        for i in range(nb):
            rows = slice(i * halo, (i + 1) * halo)
            low, high = neighbours(at_x, counts[1], sources, lambda source: load(source, rows))
            wide[t, i, edge - halo:edge, :] = low
            wide[t, i, edge + nx:edge + nx + halo, :] = high

    for t in own:
        sides(t, lambda ref, rows: ref[rows, cut(t)], xr)
        for i in range(nb):
            wide[t, i, edge:edge + nx, :] = zb[t, i]
    sides(nt, lambda tile, rows: tile[rows, :], [halo_tile(group, slice(None)) for group in corners])
    per = lanes // nx
    for chunk in range(nb // per):
        turned = halo_tile(yr, cut(chunk))
        for i in range(per):
            wide[nt, chunk * per + i, edge:edge + nx, :] = turned[i * nx:(i + 1) * nx, :]

    blank = jnp.zeros((edge, lanes), jnp.float32)
    for z in range(nb):
        along_x = [five(k, *[wide[t, z, 2 + o:2 + o + rows_b, :] for o in range(5)]) for t in every]
        done = lane_blur(k, along_x, every)
        for t in every:
            bb[t, z, 0:edge, :] = blank
            bb[t, z, edge:edge + rows_b, :] = done[t]
            bb[t, z, edge + rows_b:, :] = blank

    masks, z_mask = grid_masks(dims, counts)

    def square_z(t, z):
        slope = bb[t, z + 5, edge:edge + rows_b, :] - bb[t, z + 3, edge:edge + rows_b, :]
        return z_mask(z, slope * slope * masks[t])

    tensor(t1, every, rows_b, square_z, nz + 1)
    before = None
    for z in range(nz + 1):
        here = finish(t1, every, z, nx, own)
        if before is not None:
            scale = 0.5 * stiffness
            if z == nz:
                scale = jnp.where(at_z < counts[0] - 1, scale, 0.0)
            for t in own:
                cz[z - 1, :, cut(t)] = (before[t] + here[t]) * scale
        before = here

    def keep_z(i, w, d, h):
        fz[0, i], fz[1, i], fz[2, i] = w, d, h

    seg = eliminate(lambda i: v[i], lambda i: cz[i], nz, keep_z)
    for i, value in enumerate(seg if counts[0] > 2 else last_message(bit_of(at_z, 0), seg)):
        send_z[i] = value


def side_kernel(dims, counts, *refs):
    nz, nx, ny = dims
    nt = ny // lanes
    own, every = tuple(range(nt)), tuple(range(nt + 1))
    v, bb, fx, fy, cy_out, send_x, send_y, t1, dxs, vs, cxs, cys, ct, vt = refs
    at_x, at_y = lax.axis_index("gx"), lax.axis_index("gy")
    rows_b = nx + 8
    masks, z_mask = grid_masks(dims, counts)
    kt = taps(0.25 / (contrast * contrast))
    blank = jnp.zeros((edge, lanes), jnp.float32)
    for t in every:
        for z in range(nz):
            t1[t, z, rows_b:, :] = blank

    def square_x(t, z):
        slope = bb[t, z + 4, edge + 1:edge + 1 + rows_b, :] - bb[t, z + 4, edge - 1:edge - 1 + rows_b, :]
        return z_mask(z, slope * slope * masks[t])

    tensor(t1, every, rows_b, square_x, nz)
    for z in range(nz):
        here = finish(t1, every, z, rows_b, own)
        for t in own:
            dxs[t, z * rows_b:(z + 1) * rows_b, :] = here[t]
            vs[t, z * nx:(z + 1) * nx, :] = v[z, :, cut(t)]
    for t in own:
        here = dxs[t, pl.ds(0, nz, stride=rows_b), :]
        for x in range(nx):
            following = dxs[t, pl.ds(x + 1, nz, stride=rows_b), :]
            scale = 0.5 * stiffness
            if x == nx - 1:
                scale = jnp.where(at_x < counts[1] - 1, scale, 0.0)
            cxs[0, x, :, cut(t)] = (here + following) * scale
            cxs[1, x, :, cut(t)] = vs[t, pl.ds(x, nz, stride=nx), :]
            here = following

    def keep_x(i, w, d, h):
        fx[0, i], fx[1, i], fx[2, i] = w, d, h

    seg = eliminate(lambda i: cxs[1, i], lambda i: cxs[0, i], nx, keep_x)
    for i, value in enumerate(seg if counts[1] > 2 else last_message(bit_of(at_x, 0), seg)):
        send_x[i] = value

    def square_y_layer(z):
        tiles = [bb[t, z + 4, edge:edge + rows_b, :] for t in every]
        up, down = lane_shift(tiles, 1, every), lane_shift(tiles, -1, every)
        out = []
        for t in every:
            slope = up[t] - down[t]
            out.append(z_mask(z, slope * slope * masks[t]))
        return out

    window = [square_y_layer(z) for z in range(-2, 2)]
    for z in range(nz):
        window.append(square_y_layer(z + 2))
        for t in every:
            t1[t, z, 0:rows_b, :] = five(kt, *[layer[t] for layer in window])
        window.pop(0)
    for z in range(nz):
        here = finish(t1, every, z, nx, every)
        following = lane_shift(here, 1, own)
        for t in own:
            cys[t, z * nx:(z + 1) * nx, :] = (here[t] + following[t]) * (0.5 * stiffness)
    for t in own:
        ct[t * lanes:(t + 1) * lanes, :] = cys[t].T
        vt[t * lanes:(t + 1) * lanes, :] = vs[t].T
    closing = jnp.where(at_y < counts[2] - 1, 1.0, 0.0)
    ct[ny - 1:ny, :] = ct[ny - 1:ny, :] * closing

    steps = ny // 16
    segs = []
    for half in range(2):
        def at(ref, i, half=half):
            return ref[pl.ds(half * steps + i, 8, stride=2 * steps), :]

        def keep_y(i, w, d, h, half=half):
            fy[0, i, half], fy[1, i, half], fy[2, i, half] = w, d, h

        segs.append(eliminate(functools.partial(at, vt), functools.partial(at, ct), steps, keep_y))
    seg, coef = merge(segs[0], segs[1])
    for i in range(3):
        cy_out[0, i] = coef[i]
    for level in range(3):
        other = tuple(pltpu.roll(value, 8 - 2**level, axis=0) for value in seg)
        seg, coef = merge(seg, other)
        for i in range(3):
            cy_out[level + 1, i] = coef[i]
    seg = seg if counts[2] > 2 else last_message(bit_of(at_y, 0), seg)
    for i, value in enumerate(seg):
        send_y[i:i + 1, :] = value[0:1, :]


def summary(ref, axis, count):
    if axis == 2:
        return tuple(ref[i:i + 1, :] for i in range(count))
    return tuple(ref[i] for i in range(count))


def merge_kernel(level, depths, axes, *refs):
    refs = list(refs)
    groups = [[refs.pop(0) for _ in range(level + 2)] for _ in axes]
    for axis, group, out in zip(axes, groups, refs):
        position = lax.axis_index(("gz", "gx", "gy")[axis])
        own, *received = [summary(ref, axis, 6) for ref in group]
        seg, _ = climb(position, own, received)
        if depths[axis] == level + 2:
            seg = last_message(bit_of(position, level + 1), seg)
        for i, value in enumerate(seg):
            if axis == 2:
                out[i:i + 1, :] = value
            else:
                out[i] = value


def last_kernel(dims, depths, *refs):
    nz, nx, ny = dims
    nt = ny // lanes
    refs = list(refs)
    v, fz, fx, fy, cy = [refs.pop(0) for _ in range(5)]
    groups = [[refs.pop(0) for _ in range(depths[axis] + 1)] for axis in range(3)]
    out, acc, st, sx = refs
    fluxes = []
    for axis, group in enumerate(groups):
        position = lax.axis_index(("gz", "gx", "gy")[axis])
        if depths[axis] == 1:
            upper = bit_of(position, 0)
            mine, final = [summary(ref, axis, 2) for ref in group]
            (low_a, low_y), (high_a, high_g) = pick(upper, mine, final)
            flux = low_y * (high_a - low_a) / (1.0 + low_y * high_g)
            fluxes.append((jnp.where(upper, -flux, 0.0), jnp.where(upper, 0.0, flux)))
        else:
            own, *received = [summary(ref, axis, 6) for ref in group[:-1]]
            fluxes.append(end_fluxes(position, own, received, summary(group[-1], axis, 2)))

    left, right = fluxes[2]
    left = jnp.broadcast_to(left, (8, lanes))
    right = jnp.broadcast_to(right, (8, lanes))
    sub = lax.broadcasted_iota(jnp.int32, (8, lanes), 0)
    for level in (2, 1, 0):
        stride = 2**level
        const, by_left, by_right = [cy[level + 1, i] for i in range(3)]
        flux = const + by_right * right - by_left * left
        lower = sub % (2 * stride) == 0
        left, right = (jnp.where(lower, left, -pltpu.roll(flux, stride, axis=0)),
                       jnp.where(lower, flux, pltpu.roll(right, stride, axis=0)))
    flux = cy[0, 0] + cy[0, 2] * right - cy[0, 1] * left
    steps = ny // 16
    for half, (a, b) in enumerate(((left, flux), (-flux, right))):
        def factors(i, half=half):
            return fy[0, i, half], fy[1, i, half], fy[2, i, half]

        def emit(i, value, half=half):
            st[pl.ds(half * steps + i, 8, stride=2 * steps), :] = value

        substitute(factors, steps, a, b, emit)

    def emit_x(i, value):
        for t in range(nt):
            sx[t, pl.ds(i, nz, stride=nx), :] = value[:, t * lanes:(t + 1) * lanes]

    substitute(lambda i: (fx[0, i], fx[1, i], fx[2, i]), nx, *fluxes[1], emit_x)

    def emit_z(i, value):
        acc[i] = value

    substitute(lambda i: (fz[0, i], fz[1, i], fz[2, i]), nz, *fluxes[0], emit_z)
    for t in range(nt):
        cols = slice(t * lanes, (t + 1) * lanes)
        turned = st[cols, :].T
        for z in range(nz):
            rows = slice(z * nx, (z + 1) * nx)
            total = acc[z, :, cols] + sx[t, rows, :] + turned[rows, :]
            out[z, :, cols] = v[z, :, cols] + total * (1.0 / 3.0)


def partners(n, start):
    return [i ^ 1 if start == 0 else ((i - 1) ^ 1) + 1 if 0 < i < n - 1 else n - 1 - i for i in range(n)]


def permute(value, axes, move):
    sizes = [lax.axis_size(axis) for axis in axes]
    moves = []
    for source in itertools.product(*[range(size) for size in sizes]):
        index = lambda place: functools.reduce(lambda so_far, pair: so_far * pair[1] + pair[0], zip(place, sizes), 0)
        moves.append((index(source), index(move(*source))))
    return lax.ppermute(value, axes if len(axes) > 1 else axes[0], moves)


def swap_bit(value, axis, level):
    return permute(value, (axis,), lambda i: (i ^ (2**level),))


def swap_pair(value, axis, start):
    partner = partners(lax.axis_size(axis), start)
    return permute(value, (axis,), lambda i: (partner[i],))


def swap_z(value, start):
    n = lax.axis_size("gz")
    partner = partners(n, start)
    if start == 0:
        return swap_pair(value, "gz", 0)
    return permute(value, ("gy", "gz"), lambda y, z: (y, partner[z]) if 0 < z < n - 1 else (y ^ 1, z))


def swap_corner(value, x_start, y_start):
    of_x, of_y = partners(lax.axis_size("gx"), x_start), partners(lax.axis_size("gy"), y_start)
    return permute(value, ("gx", "gy"), lambda x, y: (of_x[x], of_y[y]))


def body(volume):
    dims = volume.shape
    nz, nx, ny = dims
    nt = ny // lanes
    names = ("gz", "gx", "gy")
    counts = tuple(lax.axis_size(name) for name in names)
    depths = tuple(count.bit_length() - 1 for count in counts)
    pairs = tuple(1 if count == 2 else 2 for count in counts)
    nb, rows_b = nz + 8, nx + 8
    assert all(2**d == n and d >= 1 for d, n in zip(depths, counts))
    assert nz == 8 and nz * nx == lanes and nx >= 8 and nb * nx % lanes == 0 and nb * halo <= lanes
    f32 = lambda *shape: jax.ShapeDtypeStruct(shape, jnp.float32)
    scratch = lambda *shape: pltpu.VMEM(shape, jnp.float32)

    def call(kernel, out_shape, scratch_shapes, *args):
        return pl.pallas_call(
            kernel, out_shape=out_shape, in_specs=[VMEM] * len(args), out_specs=[VMEM] * len(out_shape),
            scratch_shapes=scratch_shapes,
            compiler_params=pltpu.CompilerParams(vmem_limit_bytes=16 * 2**20),
        )(*args)

    volume, *z_sends = call(
        functools.partial(open_kernel, dims), [f32(*dims)] + [f32(halo, nx, ny)] * pairs[0], [], volume)
    z_received = [swap_z(value, e) for e, value in enumerate(z_sends)]
    ex, ey = range(pairs[1]), range(pairs[2])
    blurred_z, *sends = call(
        functools.partial(z_kernel, dims, counts, pairs),
        [f32(nt, nb, nx, lanes)] + [f32(nb * halo, ny) for e in ex] + [f32(edge, nb * nx) for f in ey]
        + [f32(edge, lanes) for e in ex for f in ey], [], volume, *z_received)
    x_received = [swap_pair(sends[e], "gx", e) for e in ex]
    y_received = [swap_pair(sends[pairs[1] + f], "gy", f) for f in reversed(ey)][::-1]
    corners = [swap_corner(sends[pairs[1] + pairs[2] + e * pairs[2] + f], e, f) for e in ex for f in ey]

    steps = ny // 16
    send_shape = lambda d: 6 if d > 1 else 2
    bb, fz, send_z = call(
        functools.partial(main_kernel, dims, counts, pairs),
        [f32(nt + 1, nb, rows_b + 2 * edge, lanes), f32(3, nz - 1, nx, ny), f32(send_shape(depths[0]), nx, ny)],
        [scratch(nt + 1, nb, nx + 2 * edge, lanes), scratch(nt + 1, nz + 1, rows_b + 8, lanes), scratch(nz, nx, ny)],
        volume, blurred_z, *x_received, *y_received, *corners)
    fx, fy, cy, send_x, send_y = call(
        functools.partial(side_kernel, dims, counts),
        [f32(3, nx - 1, nz, ny), f32(3, steps - 1, 2, 8, lanes), f32(4, 3, 8, lanes),
         f32(send_shape(depths[1]), nz, ny), f32(8, lanes)],
        [scratch(nt + 1, nz, rows_b + 8, lanes), scratch(nt, nz * rows_b, lanes), scratch(nt, lanes, lanes),
         scratch(2, nx, nz, ny), scratch(nt, lanes, lanes), scratch(ny, lanes), scratch(ny, lanes)],
        volume, bb)

    groups = [[send_z], [send_x], [send_y]]
    message = [send_z, send_x, send_y]
    for level in range(max(depths)):
        for axis in range(3):
            if level < depths[axis]:
                groups[axis].append(swap_bit(message[axis], names[axis], level))
        axes = [axis for axis in range(3) if depths[axis] > level + 1]
        if axes:
            shapes = []
            for axis in axes:
                count = 2 if depths[axis] == level + 2 else 6
                shapes.append(f32(8, lanes) if axis == 2 else f32(count, *((nx, ny) if axis == 0 else (nz, ny))))
            sent = call(functools.partial(merge_kernel, level, depths, axes), shapes, [],
                        *[ref for axis in axes for ref in groups[axis]])
            for axis, value in zip(axes, sent):
                message[axis] = value
    return call(
        functools.partial(last_kernel, dims, depths), [f32(*dims)],
        [scratch(*dims), scratch(ny, lanes), scratch(nt, lanes, lanes)],
        volume, fz, fx, fy, cy, *groups[0], *groups[1], *groups[2])[0]


def solution(mesh):
    return jax.shard_map(
        body,
        mesh=mesh,
        in_specs=(P("gz", "gx", "gy"),),
        out_specs=P("gz", "gx", "gy"),
        check_vma=False,
    )
```

```python
import functools
import itertools

import jax
import jax.numpy as jnp
from jax import lax
from jax.experimental import pallas as pl
from jax.experimental.pallas import tpu as pltpu
from jax.sharding import PartitionSpec as P


kernel_taps = (0.41111229, 0.8007374, 1.0, 0.8007374, 0.41111229)
time_step = 3000.0
contrast = 0.1
stiffness = 3.0 * time_step
halo = 6
lanes = 128
edge = 8
VMEM = pl.BlockSpec(memory_space=pltpu.VMEM)


def taps(scale=1.0):
    total = sum(kernel_taps)
    return tuple(scale * tap / total for tap in kernel_taps[:3])


def five(k, a, b, c, d, e):
    return k[0] * (a + e) + k[1] * (b + d) + k[2] * c


def lane_shift(tiles, k, wanted):
    count = len(tiles)
    rolled = [pltpu.roll(t, (-k) % lanes, axis=1) for t in tiles]
    lane = lax.broadcasted_iota(jnp.int32, tiles[0].shape, 1)
    out = []
    for t in wanted:
        if k > 0:
            out.append(jnp.where(lane < lanes - k, rolled[t], rolled[(t + 1) % count]))
        else:
            out.append(jnp.where(lane >= -k, rolled[t], rolled[(t - 1) % count]))
    return out


def lane_blur(k, tiles, wanted):
    s = {o: lane_shift(tiles, o, wanted) for o in (-2, -1, 1, 2)}
    return [five(k, s[-2][i], s[-1][i], tiles[t], s[1][i], s[2][i]) for i, t in enumerate(wanted)]


def merge(low, high):
    a0, an, g00, g0n, y = low
    b0, bn, h00, h0n, e = high
    w = y / (1.0 + y * h00)
    flux = w * (b0 - an)
    by_left = w * g0n
    by_right = w * h0n
    joined = (a0 + g0n * flux, bn - h0n * flux, g00 - g0n * by_left, by_left * h0n, e / (1.0 - e * (h0n * by_right)))
    return joined, (flux, by_left, by_right)


def pick(upper, own, other):
    low = tuple(jnp.where(upper, o, m) for m, o in zip(own, other))
    high = tuple(jnp.where(upper, m, o) for m, o in zip(own, other))
    return low, high


def last_message(upper, seg):
    a0, an, g00, _, y = seg
    return jnp.where(upper, a0, an), jnp.where(upper, g00, y)


def bit_of(position, level):
    return (position // (2**level)) % 2 == 1


def climb(position, own, received):
    coefs = []
    for level, other in enumerate(received):
        low, high = pick(bit_of(position, level), own, other)
        own, coef = merge(low, high)
        coefs.append(coef)
    return own, coefs


def end_fluxes(position, own, received, final):
    seg, coefs = climb(position, own, received)
    top = len(received)
    upper = bit_of(position, top)
    mine = last_message(upper, seg)
    (low_a, low_y), (high_a, high_g) = pick(upper, mine, final)
    flux = low_y * (high_a - low_a) / (1.0 + low_y * high_g)
    left = jnp.where(upper, -flux, 0.0)
    right = jnp.where(upper, 0.0, flux)
    for level in reversed(range(top)):
        const, by_left, by_right = coefs[level]
        flux = const + by_right * right - by_left * left
        upper = bit_of(position, level)
        left, right = jnp.where(upper, -flux, left), jnp.where(upper, right, flux)
    return left, right


def eliminate(v, c, count, keep):
    a0 = an = v(0)
    g00 = g0n = gnn = jnp.ones_like(an)
    for i in range(count - 1):
        face = c(i)
        w = face / (1.0 + face * (gnn + 1.0))
        following = v(i + 1)
        d = following - an
        keep(i, w, d, g0n)
        flux = w * d
        a0 = a0 + g0n * flux
        an = following - flux
        hw = g0n * w
        g00 = g00 - g0n * hw
        g0n = hw
        gnn = 1.0 - w
    face = c(count - 1)
    return a0, an, g00, g0n, face / (1.0 + face * gnn)


def substitute(factors, count, left, right, emit):
    above = right
    for i in reversed(range(count - 1)):
        w, d, h = factors(i)
        flux = w * (d + above - h * left)
        emit(i + 1, above - flux)
        above = flux
    emit(0, above + left)


def responses(factors, count, emit):
    base, by_left, by_right = 0.0, 0.0, 1.0
    for i in reversed(range(count - 1)):
        w, d, h = factors(i)
        flux = w * (d + base), w * (by_left - h), w * by_right
        emit(i + 1, base - flux[0], by_left - flux[1], by_right - flux[2])
        base, by_left, by_right = flux
    emit(0, base, by_left + 1.0, by_right)


def cut(t):
    return slice(t * lanes, (t + 1) * lanes)


def z_blur(load, store, count, weights):
    window = [load(i) for i in range(4)]
    for i in range(count):
        window.append(load(i + 4))
        store(i, five(weights, *window))
        window.pop(0)


def neighbours(position, count, refs, load):
    odd = position % 2 == 1
    first = load(refs[0])
    if len(refs) > 1:
        end = (position == 0) | (position == count - 1)
        second = jnp.where(end, 0.0, load(refs[1]))
    else:
        second = jnp.zeros_like(first)
    return jnp.where(odd, first, second), jnp.where(odd, second, first)


def open_kernel(dims, volume, kept, *sends):
    nz = dims[0]
    odd = lax.axis_index("gz") % 2 == 1
    for z in range(nz):
        kept[z] = volume[z]
    for z in range(halo):
        low, high = volume[z], volume[nz - halo + z]
        sends[0][z] = jnp.where(odd, low, high)
        if len(sends) > 1:
            sends[1][z] = jnp.where(odd, high, low)


def z_kernel(dims, counts, pairs, *refs):
    nz, nx, ny = dims
    nt, nb = ny // lanes, nz + 8
    v, zr = refs[0], refs[1:1 + pairs[0]]
    out, *sends = refs[1 + pairs[0]:]
    x_sends, y_sends = sends[:pairs[1]], sends[pairs[1]:pairs[1] + pairs[2]]
    corner_sends = sends[pairs[1] + pairs[2]:]
    at_z = lax.axis_index("gz")
    odd_x = lax.axis_index("gx") % 2 == 1
    odd_y = lax.axis_index("gy") % 2 == 1
    for t in range(nt):
        cols = cut(t)
        below = [neighbours(at_z, counts[0], zr, lambda ref: ref[z, :, cols])[0] for z in range(halo)]
        above = [neighbours(at_z, counts[0], zr, lambda ref: ref[z, :, cols])[1] for z in range(halo)]

        def load(z):
            if z < halo:
                return below[z]
            return v[z - halo, :, cols] if z < halo + nz else above[z - halo - nz]

        def store(i, value):
            out[t, i] = value
            low, high = value[:halo], value[nx - halo:]
            rows = slice(i * halo, (i + 1) * halo)
            x_sends[0][rows, cols] = jnp.where(odd_x, low, high)
            if len(x_sends) > 1:
                x_sends[1][rows, cols] = jnp.where(odd_x, high, low)

        z_blur(load, store, nb, taps())

    per = lanes // nx
    for chunk in range(nb // per):
        tiles = [out[t, chunk * per:(chunk + 1) * per].reshape(lanes, lanes) for t in (0, nt - 1)]
        for f, ref in enumerate(y_sends):
            ref[:, cut(chunk)] = strip(odd_y, f, *tiles)
    pad = jnp.zeros((lanes - nb * halo, lanes), jnp.float32)
    for ref, corner in zip(x_sends, corner_sends):
        corner[...] = strip(odd_y, 1, *[jnp.concatenate([ref[:, cut(t)], pad], axis=0) for t in (0, nt - 1)])


def strip(odd_y, f, first_tile, last_tile):
    first, last = first_tile.T[:edge, :], last_tile.T[lanes - edge:, :]
    return jnp.where(odd_y, last, first) if f else jnp.where(odd_y, first, last)


def pack_kernel(dims, *refs):
    nz, nx, ny = dims
    nt, nb = ny // lanes, nz + 8
    own, xr, out = refs[0], refs[1:-1], refs[-1]
    odd_y = lax.axis_index("gy") % 2 == 1
    out[:, :nb * nx] = own[...]
    pad = jnp.zeros((lanes - nb * halo, lanes), jnp.float32)
    for e, ref in enumerate(xr):
        tiles = [jnp.concatenate([ref[:, cut(t)], pad], axis=0) for t in (0, nt - 1)]
        begin = nb * nx + e * lanes
        out[:, begin:begin + lanes] = strip(odd_y, 0, *tiles)


def grid_masks(dims, counts):
    nz, nx, ny = dims
    nt = ny // lanes
    at_z, at_x, at_y = lax.axis_index("gz"), lax.axis_index("gx"), lax.axis_index("gy")
    rows_b = nx + 8
    xi = at_x * nx + lax.broadcasted_iota(jnp.int32, (rows_b, lanes), 0) - 4
    x_mask = jnp.where((xi >= 0) & (xi < nx * counts[1]), 1.0, 0.0)
    lane = lax.broadcasted_iota(jnp.int32, (rows_b, lanes), 1)
    not_first = (at_y > 0).astype(jnp.float32)
    not_last = (at_y < counts[2] - 1).astype(jnp.float32)
    masks = [x_mask] * nt + [x_mask * jnp.where(lane < lanes // 2, not_last, not_first)]

    def z_mask(z, value):
        if 0 <= z < nz:
            return value
        inside = (at_z > 0) if z < 0 else (at_z < counts[0] - 1)
        return value * inside.astype(jnp.float32)

    return masks, z_mask


def tensor(t1, every, rows_b, square, count):
    kt = taps(0.25 / (contrast * contrast))
    for t in every:
        window = [square(t, z) for z in range(-2, 2)]
        for i in range(count):
            window.append(square(t, i + 2))
            t1[t, i, 0:rows_b, :] = five(kt, *window)
            window.pop(0)


def finish(t1, every, z, rows, wanted):
    k = taps()
    along_x = [five(k, *[t1[t, z, 2 + o:2 + o + rows, :] for o in range(5)]) for t in every]
    return [1.0 / (1.0 + value) for value in lane_blur(k, along_x, wanted)]


def main_kernel(dims, counts, pairs, *refs):
    nz, nx, ny = dims
    nt = ny // lanes
    own, every = tuple(range(nt)), tuple(range(nt + 1))
    refs = list(refs)
    v, zb = refs.pop(0), refs.pop(0)
    xr = [refs.pop(0) for _ in range(pairs[1])]
    yr = [refs.pop(0) for _ in range(pairs[2])]
    far = [refs.pop(0) for _ in range(pairs[1] if pairs[2] > 1 else 0)]
    bb, fz, send_z, wide, t1, cz = refs
    at_z, at_x, at_y = lax.axis_index("gz"), lax.axis_index("gx"), lax.axis_index("gy")
    nb, rows_b = nz + 8, nx + 8
    k = taps()

    gap = jnp.zeros((lanes - 2 * edge, lanes), jnp.float32)

    def halo_tile(received, cols):
        low, high = neighbours(at_y, counts[2], received, lambda ref: ref[:, cols])
        return jnp.concatenate([high, gap, low], axis=0).T

    def sides(t, load, sources):
        for i in range(nb):
            rows = slice(i * halo, (i + 1) * halo)
            low, high = neighbours(at_x, counts[1], sources, lambda source: load(source, rows))
            wide[t, i, edge - halo:edge, :] = low
            wide[t, i, edge + nx:edge + nx + halo, :] = high

    for t in own:
        sides(t, lambda ref, rows: ref[rows, cut(t)], xr)
        for i in range(nb):
            wide[t, i, edge:edge + nx, :] = zb[t, i]
    corners = []
    for e in range(pairs[1]):
        begin = nb * nx + e * lanes
        corners.append(halo_tile([yr[0].at[:, begin:begin + lanes]] + far[e:e + 1], slice(None)))
    sides(nt, lambda tile, rows: tile[rows, :], corners)
    per = lanes // nx
    for chunk in range(nb // per):
        turned = halo_tile(yr, cut(chunk))
        for i in range(per):
            wide[nt, chunk * per + i, edge:edge + nx, :] = turned[i * nx:(i + 1) * nx, :]

    blank = jnp.zeros((edge, lanes), jnp.float32)
    for z in range(nb):
        along_x = [five(k, *[wide[t, z, 2 + o:2 + o + rows_b, :] for o in range(5)]) for t in every]
        done = lane_blur(k, along_x, every)
        for t in every:
            bb[t, z, 0:edge, :] = blank
            bb[t, z, edge:edge + rows_b, :] = done[t]
            bb[t, z, edge + rows_b:, :] = blank

    masks, z_mask = grid_masks(dims, counts)

    def square_z(t, z):
        slope = bb[t, z + 5, edge:edge + rows_b, :] - bb[t, z + 3, edge:edge + rows_b, :]
        return z_mask(z, slope * slope * masks[t])

    tensor(t1, every, rows_b, square_z, nz + 1)
    before = None
    for z in range(nz + 1):
        here = finish(t1, every, z, nx, own)
        if before is not None:
            scale = 0.5 * stiffness
            if z == nz:
                scale = jnp.where(at_z < counts[0] - 1, scale, 0.0)
            for t in own:
                cz[z - 1, :, cut(t)] = (before[t] + here[t]) * scale
        before = here

    def keep_z(i, w, d, h):
        fz[0, i], fz[1, i], fz[2, i] = w, d, h

    seg = eliminate(lambda i: v[i], lambda i: cz[i], nz, keep_z)
    for i, value in enumerate(seg if counts[0] > 2 else last_message(bit_of(at_z, 0), seg)):
        send_z[i] = value


def side_kernel(dims, counts, *refs):
    nz, nx, ny = dims
    nt = ny // lanes
    own, every = tuple(range(nt)), tuple(range(nt + 1))
    v, bb, fx, fy, cy_out, send_x, send_y, t1, dxs, vs, cxs, cys, ct, vt = refs
    at_x, at_y = lax.axis_index("gx"), lax.axis_index("gy")
    rows_b = nx + 8
    masks, z_mask = grid_masks(dims, counts)
    kt = taps(0.25 / (contrast * contrast))
    blank = jnp.zeros((edge, lanes), jnp.float32)
    for t in every:
        for z in range(nz):
            t1[t, z, rows_b:, :] = blank

    def square_x(t, z):
        slope = bb[t, z + 4, edge + 1:edge + 1 + rows_b, :] - bb[t, z + 4, edge - 1:edge - 1 + rows_b, :]
        return z_mask(z, slope * slope * masks[t])

    tensor(t1, every, rows_b, square_x, nz)
    for z in range(nz):
        here = finish(t1, every, z, rows_b, own)
        for t in own:
            dxs[t, z * rows_b:(z + 1) * rows_b, :] = here[t]
            vs[t, z * nx:(z + 1) * nx, :] = v[z, :, cut(t)]
    for t in own:
        here = dxs[t, pl.ds(0, nz, stride=rows_b), :]
        for x in range(nx):
            following = dxs[t, pl.ds(x + 1, nz, stride=rows_b), :]
            scale = 0.5 * stiffness
            if x == nx - 1:
                scale = jnp.where(at_x < counts[1] - 1, scale, 0.0)
            cxs[0, x, :, cut(t)] = (here + following) * scale
            cxs[1, x, :, cut(t)] = vs[t, pl.ds(x, nz, stride=nx), :]
            here = following

    def keep_x(i, w, d, h):
        fx[0, i], fx[1, i], fx[2, i] = w, d, h

    seg = eliminate(lambda i: cxs[1, i], lambda i: cxs[0, i], nx, keep_x)
    for i, value in enumerate(seg if counts[1] > 2 else last_message(bit_of(at_x, 0), seg)):
        send_x[i] = value

    def square_y_layer(z):
        tiles = [bb[t, z + 4, edge:edge + rows_b, :] for t in every]
        up, down = lane_shift(tiles, 1, every), lane_shift(tiles, -1, every)
        out = []
        for t in every:
            slope = up[t] - down[t]
            out.append(z_mask(z, slope * slope * masks[t]))
        return out

    window = [square_y_layer(z) for z in range(-2, 2)]
    for z in range(nz):
        window.append(square_y_layer(z + 2))
        for t in every:
            t1[t, z, 0:rows_b, :] = five(kt, *[layer[t] for layer in window])
        window.pop(0)
    for z in range(nz):
        here = finish(t1, every, z, nx, every)
        following = lane_shift(here, 1, own)
        for t in own:
            cys[t, z * nx:(z + 1) * nx, :] = (here[t] + following[t]) * (0.5 * stiffness)
    for t in own:
        ct[t * lanes:(t + 1) * lanes, :] = cys[t].T
        vt[t * lanes:(t + 1) * lanes, :] = vs[t].T
    closing = jnp.where(at_y < counts[2] - 1, 1.0, 0.0)
    ct[ny - 1:ny, :] = ct[ny - 1:ny, :] * closing

    steps = ny // 16
    segs = []
    for half in range(2):
        def at(ref, i, half=half):
            return ref[pl.ds(half * steps + i, 8, stride=2 * steps), :]

        def keep_y(i, w, d, h, half=half):
            fy[0, i, half], fy[1, i, half], fy[2, i, half] = w, d, h

        segs.append(eliminate(functools.partial(at, vt), functools.partial(at, ct), steps, keep_y))
    seg, coef = merge(segs[0], segs[1])
    for i in range(3):
        cy_out[0, i] = coef[i]
    for level in range(3):
        other = tuple(pltpu.roll(value, 8 - 2**level, axis=0) for value in seg)
        seg, coef = merge(seg, other)
        for i in range(3):
            cy_out[level + 1, i] = coef[i]
    seg = seg if counts[2] > 2 else last_message(bit_of(at_y, 0), seg)
    for i, value in enumerate(seg):
        send_y[i:i + 1, :] = value[0:1, :]


def summary(ref, axis, count):
    if axis == 2:
        return tuple(ref[i:i + 1, :] for i in range(count))
    return tuple(ref[i] for i in range(count))


def merge_kernel(level, depths, axes, *refs):
    refs = list(refs)
    groups = [[refs.pop(0) for _ in range(level + 2)] for _ in axes]
    for axis, group, out in zip(axes, groups, refs):
        position = lax.axis_index(("gz", "gx", "gy")[axis])
        own, *received = [summary(ref, axis, 5) for ref in group]
        seg, _ = climb(position, own, received)
        if depths[axis] == level + 2:
            seg = last_message(bit_of(position, level + 1), seg)
        for i, value in enumerate(seg):
            if axis == 2:
                out[i:i + 1, :] = value
            else:
                out[i] = value


def fluxes_of(axis, depths, group):
    position = lax.axis_index(("gz", "gx", "gy")[axis])
    if depths[axis] == 1:
        upper = bit_of(position, 0)
        mine, final = [summary(ref, axis, 2) for ref in group]
        (low_a, low_y), (high_a, high_g) = pick(upper, mine, final)
        flux = low_y * (high_a - low_a) / (1.0 + low_y * high_g)
        return jnp.where(upper, -flux, 0.0), jnp.where(upper, 0.0, flux)
    own, *received = [summary(ref, axis, 5) for ref in group[:-1]]
    return end_fluxes(position, own, received, summary(group[-1], axis, 2))


def solve_x(dims, factors, fluxes, target):
    nz, nx, ny = dims

    def emit(i, value):
        for t in range(ny // lanes):
            target[t, pl.ds(i, nz, stride=nx), :] = value[:, cut(t)]

    substitute(lambda i: (factors[0, i], factors[1, i], factors[2, i]), nx, *fluxes, emit)


def prepare_kernel(dims, depths, *refs):
    nz, nx, ny = dims
    refs = list(refs)
    v, fz, fx, fy, cy = [refs.pop(0) for _ in range(5)]
    group = [refs.pop(0) for _ in range(2 if depths[1] == 1 else 0)]
    base, by_z, by_y, sx = refs
    third = 1.0 / 3.0
    if group:
        solve_x(dims, fx, fluxes_of(1, depths, group), sx)

    sub = lax.broadcasted_iota(jnp.int32, (8, lanes), 0)
    zero = jnp.zeros((8, lanes), jnp.float32)
    left, right = (zero, zero + 1.0, zero), (zero, zero, zero + 1.0)

    def crossing(level):
        const, by_left, by_right = [cy[level, i] for i in range(3)]
        terms = [by_right * r - by_left * l for l, r in zip(left, right)]
        return [terms[0] + const] + terms[1:]

    for level in (2, 1, 0):
        stride = 2**level
        flux = crossing(level + 1)
        lower = sub % (2 * stride) == 0
        left, right = ([jnp.where(lower, l, -pltpu.roll(f, stride, axis=0)) for l, f in zip(left, flux)],
                       [jnp.where(lower, f, pltpu.roll(r, stride, axis=0)) for r, f in zip(right, flux)])
    flux = crossing(0)
    steps = ny // 16
    for half, (a, b) in enumerate(((left, flux), ([-f for f in flux], right))):
        a, b = [m * third for m in a], [m * third for m in b]

        def emit(i, own, by_left, by_right, half=half, a=a, b=b):
            at = pl.ds(half * steps + i, 8, stride=2 * steps)
            for m in range(3):
                value = by_left * a[m] + by_right * b[m]
                by_y[m, at, :] = value + own * third if m == 0 else value

        responses(lambda i, half=half: (fy[0, i, half], fy[1, i, half], fy[2, i, half]), steps, emit)

    def emit_z(i, own, by_left, by_right):
        total = own
        if group:
            total = total + jnp.concatenate([sx[t, i * nx:(i + 1) * nx, :] for t in range(ny // lanes)], axis=1)
        base[i] = v[i] + total * third
        by_z[0, i] = jnp.broadcast_to(by_left * third, (nx, ny))
        by_z[1, i] = jnp.broadcast_to(by_right * third, (nx, ny))

    responses(lambda i: (fz[0, i], fz[1, i], fz[2, i]), nz, emit_z)


def last_kernel(dims, depths, *refs):
    nz, nx, ny = dims
    nt = ny // lanes
    refs = list(refs)
    base, by_z, by_y, fx = [refs.pop(0) for _ in range(4)]
    groups = {axis: [refs.pop(0) for _ in range(depths[axis] + 1)] for axis in range(3) if axis != 1 or depths[1] > 1}
    out, st, sx = refs
    left, right = fluxes_of(2, depths, groups[2])
    for t in range(nt):
        st[t] = (by_y[0, cut(t), :] + by_y[1, cut(t), :] * left + by_y[2, cut(t), :] * right).T
    if 1 in groups:
        solve_x(dims, fx, fluxes_of(1, depths, groups[1]), sx)
    left, right = fluxes_of(0, depths, groups[0])
    for z in range(nz):
        total = base[z] + by_z[0, z] * left + by_z[1, z] * right
        rows = slice(z * nx, (z + 1) * nx)
        for t in range(nt):
            value = total[:, cut(t)] + st[t, rows, :]
            if 1 in groups:
                value = value + sx[t, rows, :] * (1.0 / 3.0)
            out[z, :, cut(t)] = value


def partners(n, start):
    return [i ^ 1 if start == 0 else ((i - 1) ^ 1) + 1 if 0 < i < n - 1 else n - 1 - i for i in range(n)]


def permute(value, axes, move):
    sizes = [lax.axis_size(axis) for axis in axes]
    moves = []
    for source in itertools.product(*[range(size) for size in sizes]):
        index = lambda place: functools.reduce(lambda so_far, pair: so_far * pair[1] + pair[0], zip(place, sizes), 0)
        moves.append((index(source), index(move(*source))))
    return lax.ppermute(value, axes if len(axes) > 1 else axes[0], moves)


def swap_bit(value, axis, level):
    return permute(value, (axis,), lambda i: (i ^ (2**level),))


def swap_pair(value, axis, start):
    partner = partners(lax.axis_size(axis), start)
    return permute(value, (axis,), lambda i: (partner[i],))


def swap_z(value, start):
    n = lax.axis_size("gz")
    partner = partners(n, start)
    if start == 0:
        return swap_pair(value, "gz", 0)
    return permute(value, ("gy", "gz"), lambda y, z: (y, partner[z]) if 0 < z < n - 1 else (y ^ 1, z))


def swap_corner(value, x_start, y_start):
    of_x, of_y = partners(lax.axis_size("gx"), x_start), partners(lax.axis_size("gy"), y_start)
    return permute(value, ("gx", "gy"), lambda x, y: (of_x[x], of_y[y]))


def body(volume):
    dims = volume.shape
    nz, nx, ny = dims
    nt = ny // lanes
    names = ("gz", "gx", "gy")
    counts = tuple(lax.axis_size(name) for name in names)
    depths = tuple(count.bit_length() - 1 for count in counts)
    pairs = tuple(1 if count == 2 else 2 for count in counts)
    nb, rows_b = nz + 8, nx + 8
    assert all(2**d == n and d >= 1 for d, n in zip(depths, counts))
    assert nz == 8 and nz * nx == lanes and nx >= 8 and nb * nx % lanes == 0 and nb * halo <= lanes
    f32 = lambda *shape: jax.ShapeDtypeStruct(shape, jnp.float32)
    scratch = lambda *shape: pltpu.VMEM(shape, jnp.float32)

    def call(kernel, out_shape, scratch_shapes, *args):
        return pl.pallas_call(
            kernel, out_shape=out_shape, in_specs=[VMEM] * len(args), out_specs=[VMEM] * len(out_shape),
            scratch_shapes=scratch_shapes,
            compiler_params=pltpu.CompilerParams(vmem_limit_bytes=16 * 2**20),
        )(*args)

    volume, *z_sends = call(
        functools.partial(open_kernel, dims), [f32(*dims)] + [f32(halo, nx, ny)] * pairs[0], [], volume)
    z_received = [swap_z(value, e) for e, value in enumerate(z_sends)]
    ex, ey = range(pairs[1]), range(pairs[2])
    far = ex if pairs[2] > 1 else []
    blurred_z, *sends = call(
        functools.partial(z_kernel, dims, counts, pairs),
        [f32(nt, nb, nx, lanes)] + [f32(nb * halo, ny) for e in ex] + [f32(edge, nb * nx) for f in ey]
        + [f32(edge, lanes) for e in far], [], volume, *z_received)
    x_received = [swap_pair(sends[e], "gx", e) for e in ex]
    y_sends = sends[pairs[1]:pairs[1] + pairs[2]]
    corners = [swap_corner(sends[pairs[1] + pairs[2] + e], e, 1) for e in far]
    y_received = [swap_pair(value, "gy", 1) for value in y_sends[1:]]
    y_sends[0], = call(functools.partial(pack_kernel, dims), [f32(edge, nb * nx + pairs[1] * lanes)], [],
                       y_sends[0], *x_received)
    y_received.insert(0, swap_pair(y_sends[0], "gy", 0))

    steps = ny // 16
    send_shape = lambda d: 5 if d > 1 else 2
    bb, fz, send_z = call(
        functools.partial(main_kernel, dims, counts, pairs),
        [f32(nt + 1, nb, rows_b + 2 * edge, lanes), f32(3, nz - 1, nx, ny), f32(send_shape(depths[0]), nx, ny)],
        [scratch(nt + 1, nb, nx + 2 * edge, lanes), scratch(nt + 1, nz + 1, rows_b + 8, lanes), scratch(nz, nx, ny)],
        volume, blurred_z, *x_received, *y_received, *corners)
    fx, fy, cy, send_x, send_y = call(
        functools.partial(side_kernel, dims, counts),
        [f32(3, nx - 1, nz, ny), f32(3, steps - 1, 2, 8, lanes), f32(4, 3, 8, lanes),
         f32(send_shape(depths[1]), nz, ny), f32(8, lanes)],
        [scratch(nt + 1, nz, rows_b + 8, lanes), scratch(nt, nz * rows_b, lanes), scratch(nt, lanes, lanes),
         scratch(2, nx, nz, ny), scratch(nt, lanes, lanes), scratch(ny, lanes), scratch(ny, lanes)],
        volume, bb)

    groups = [[send_z], [send_x], [send_y]]
    message = [send_z, send_x, send_y]
    for level in range(max(depths)):
        for axis in range(3):
            if level < depths[axis]:
                groups[axis].append(swap_bit(message[axis], names[axis], level))
        axes = [axis for axis in range(3) if depths[axis] > level + 1]
        if axes:
            shapes = []
            for axis in axes:
                count = 2 if depths[axis] == level + 2 else 5
                shapes.append(f32(8, lanes) if axis == 2 else f32(count, *((nx, ny) if axis == 0 else (nz, ny))))
            sent = call(functools.partial(merge_kernel, level, depths, axes), shapes, [],
                        *[ref for axis in axes for ref in groups[axis]])
            for axis, value in zip(axes, sent):
                message[axis] = value
    x_group = groups[1] if depths[1] == 1 else []
    base, by_z, by_y = call(
        functools.partial(prepare_kernel, dims, depths), [f32(*dims), f32(2, *dims), f32(3, ny, lanes)],
        [scratch(nt, lanes, lanes)], volume, fz, fx, fy, cy, *x_group)
    rest = groups[0] + ([] if x_group else groups[1]) + groups[2]
    return call(
        functools.partial(last_kernel, dims, depths), [f32(*dims)],
        [scratch(nt, lanes, lanes), scratch(nt, lanes, lanes)], base, by_z, by_y, fx, *rest)[0]


def solution(mesh):
    return jax.shard_map(
        body,
        mesh=mesh,
        in_specs=(P("gz", "gx", "gy"),),
        out_specs=P("gz", "gx", "gy"),
        check_vma=False,
    )
```

```python
import functools
import itertools

import jax
import jax.numpy as jnp
from jax import lax
from jax.experimental import pallas as pl
from jax.experimental.pallas import tpu as pltpu
from jax.sharding import PartitionSpec as P


kernel_taps = (0.41111229, 0.8007374, 1.0, 0.8007374, 0.41111229)
time_step = 3000.0
contrast = 0.1
stiffness = 3.0 * time_step
halo = 6
lanes = 128
edge = 8
VMEM = pl.BlockSpec(memory_space=pltpu.VMEM)


def taps(scale=1.0):
    total = sum(kernel_taps)
    return tuple(scale * tap / total for tap in kernel_taps[:3])


def five(k, a, b, c, d, e):
    return k[0] * (a + e) + k[1] * (b + d) + k[2] * c


def lane_shift(tiles, k, wanted):
    count = len(tiles)
    rolled = [pltpu.roll(t, (-k) % lanes, axis=1) for t in tiles]
    lane = lax.broadcasted_iota(jnp.int32, tiles[0].shape, 1)
    out = []
    for t in wanted:
        if k > 0:
            out.append(jnp.where(lane < lanes - k, rolled[t], rolled[(t + 1) % count]))
        else:
            out.append(jnp.where(lane >= -k, rolled[t], rolled[(t - 1) % count]))
    return out


def lane_blur(k, tiles, wanted):
    s = {o: lane_shift(tiles, o, wanted) for o in (-2, -1, 1, 2)}
    return [five(k, s[-2][i], s[-1][i], tiles[t], s[1][i], s[2][i]) for i, t in enumerate(wanted)]


def merge(low, high):
    a0, an, g00, g0n, y = low
    b0, bn, h00, h0n, e = high
    w = y / (1.0 + y * h00)
    flux = w * (b0 - an)
    by_left = w * g0n
    by_right = w * h0n
    joined = (a0 + g0n * flux, bn - h0n * flux, g00 - g0n * by_left, by_left * h0n, e / (1.0 - e * (h0n * by_right)))
    return joined, (flux, by_left, by_right)


def pick(upper, own, other):
    low = tuple(jnp.where(upper, o, m) for m, o in zip(own, other))
    high = tuple(jnp.where(upper, m, o) for m, o in zip(own, other))
    return low, high


def last_message(upper, seg):
    a0, an, g00, _, y = seg
    return jnp.where(upper, a0, an), jnp.where(upper, g00, y)


def bit_of(position, level):
    return (position // (2**level)) % 2 == 1


def climb(position, own, received):
    coefs = []
    for level, other in enumerate(received):
        low, high = pick(bit_of(position, level), own, other)
        own, coef = merge(low, high)
        coefs.append(coef)
    return own, coefs


def end_fluxes(position, own, received, final):
    seg, coefs = climb(position, own, received)
    top = len(received)
    upper = bit_of(position, top)
    mine = last_message(upper, seg)
    (low_a, low_y), (high_a, high_g) = pick(upper, mine, final)
    flux = low_y * (high_a - low_a) / (1.0 + low_y * high_g)
    left = jnp.where(upper, -flux, 0.0)
    right = jnp.where(upper, 0.0, flux)
    for level in reversed(range(top)):
        const, by_left, by_right = coefs[level]
        flux = const + by_right * right - by_left * left
        upper = bit_of(position, level)
        left, right = jnp.where(upper, -flux, left), jnp.where(upper, right, flux)
    return left, right


def eliminate(v, c, count, keep):
    a0 = an = v(0)
    g00 = g0n = gnn = jnp.ones_like(an)
    for i in range(count - 1):
        face = c(i)
        w = face / (1.0 + face * (gnn + 1.0))
        following = v(i + 1)
        d = following - an
        keep(i, w, d, g0n)
        flux = w * d
        a0 = a0 + g0n * flux
        an = following - flux
        hw = g0n * w
        g00 = g00 - g0n * hw
        g0n = hw
        gnn = 1.0 - w
    face = c(count - 1)
    return a0, an, g00, g0n, face / (1.0 + face * gnn)


def substitute(factors, count, left, right, emit):
    above = right
    for i in reversed(range(count - 1)):
        w, d, h = factors(i)
        flux = w * (d + above - h * left)
        emit(i + 1, above - flux)
        above = flux
    emit(0, above + left)


def responses(factors, count, emit):
    base, by_left, by_right = 0.0, 0.0, 1.0
    for i in reversed(range(count - 1)):
        w, d, h = factors(i)
        flux = w * (d + base), w * (by_left - h), w * by_right
        emit(i + 1, base - flux[0], by_left - flux[1], by_right - flux[2])
        base, by_left, by_right = flux
    emit(0, base, by_left + 1.0, by_right)


def cut(t):
    return slice(t * lanes, (t + 1) * lanes)


def z_blur(load, store, count, weights):
    window = [load(i) for i in range(4)]
    for i in range(count):
        window.append(load(i + 4))
        store(i, five(weights, *window))
        window.pop(0)


def neighbours(position, count, refs, load):
    odd = position % 2 == 1
    first = load(refs[0])
    if len(refs) > 1:
        end = (position == 0) | (position == count - 1)
        second = jnp.where(end, 0.0, load(refs[1]))
    else:
        second = jnp.zeros_like(first)
    return jnp.where(odd, first, second), jnp.where(odd, second, first)


def open_kernel(dims, volume, kept, *sends):
    nz = dims[0]
    odd = lax.axis_index("gz") % 2 == 1
    for z in range(nz):
        kept[z] = volume[z]
    for z in range(halo):
        low, high = volume[z], volume[nz - halo + z]
        sends[0][z] = jnp.where(odd, low, high)
        if len(sends) > 1:
            sends[1][z] = jnp.where(odd, high, low)


def z_kernel(dims, counts, pairs, *refs):
    nz, nx, ny = dims
    nt, nb = ny // lanes, nz + 8
    v, zr = refs[0], refs[1:1 + pairs[0]]
    out, *sends = refs[1 + pairs[0]:]
    x_sends, y_sends = sends[:pairs[1]], sends[pairs[1]:pairs[1] + pairs[2]]
    corner_sends = sends[pairs[1] + pairs[2]:]
    at_z = lax.axis_index("gz")
    odd_x = lax.axis_index("gx") % 2 == 1
    odd_y = lax.axis_index("gy") % 2 == 1
    for t in range(nt):
        cols = cut(t)
        below = [neighbours(at_z, counts[0], zr, lambda ref: ref[z, :, cols])[0] for z in range(halo)]
        above = [neighbours(at_z, counts[0], zr, lambda ref: ref[z, :, cols])[1] for z in range(halo)]

        def load(z):
            if z < halo:
                return below[z]
            return v[z - halo, :, cols] if z < halo + nz else above[z - halo - nz]

        def store(i, value):
            out[t, i] = value
            low, high = value[:halo], value[nx - halo:]
            rows = slice(i * halo, (i + 1) * halo)
            x_sends[0][rows, cols] = jnp.where(odd_x, low, high)
            if len(x_sends) > 1:
                x_sends[1][rows, cols] = jnp.where(odd_x, high, low)

        z_blur(load, store, nb, taps())

    per = lanes // nx
    for chunk in range(nb // per):
        tiles = [out[t, chunk * per:(chunk + 1) * per].reshape(lanes, lanes) for t in (0, nt - 1)]
        for f, ref in enumerate(y_sends):
            ref[:, cut(chunk)] = strip(odd_y, f, *tiles)
    pad = jnp.zeros((lanes - nb * halo, lanes), jnp.float32)
    for ref, corner in zip(x_sends, corner_sends):
        corner[...] = strip(odd_y, 1, *[jnp.concatenate([ref[:, cut(t)], pad], axis=0) for t in (0, nt - 1)])


def strip(odd_y, f, first_tile, last_tile):
    first, last = first_tile.T[:edge, :], last_tile.T[lanes - edge:, :]
    return jnp.where(odd_y, last, first) if f else jnp.where(odd_y, first, last)


def pack_kernel(dims, *refs):
    nz, nx, ny = dims
    nt, nb = ny // lanes, nz + 8
    own, xr, out = refs[0], refs[1:-1], refs[-1]
    odd_y = lax.axis_index("gy") % 2 == 1
    out[:, :nb * nx] = own[...]
    pad = jnp.zeros((lanes - nb * halo, lanes), jnp.float32)
    for e, ref in enumerate(xr):
        tiles = [jnp.concatenate([ref[:, cut(t)], pad], axis=0) for t in (0, nt - 1)]
        begin = nb * nx + e * lanes
        out[:, begin:begin + lanes] = strip(odd_y, 0, *tiles)


def grid_masks(dims, counts):
    nz, nx, ny = dims
    nt = ny // lanes
    at_z, at_x, at_y = lax.axis_index("gz"), lax.axis_index("gx"), lax.axis_index("gy")
    rows_b = nx + 8
    xi = at_x * nx + lax.broadcasted_iota(jnp.int32, (rows_b, lanes), 0) - 4
    x_mask = jnp.where((xi >= 0) & (xi < nx * counts[1]), 1.0, 0.0)
    lane = lax.broadcasted_iota(jnp.int32, (rows_b, lanes), 1)
    not_first = (at_y > 0).astype(jnp.float32)
    not_last = (at_y < counts[2] - 1).astype(jnp.float32)
    masks = [x_mask] * nt + [x_mask * jnp.where(lane < lanes // 2, not_last, not_first)]

    def z_mask(z, value):
        if 0 <= z < nz:
            return value
        inside = (at_z > 0) if z < 0 else (at_z < counts[0] - 1)
        return value * inside.astype(jnp.float32)

    return masks, z_mask


def tensor(t1, every, rows_b, square, count):
    kt = taps(0.25 / (contrast * contrast))
    for t in every:
        window = [square(t, z) for z in range(-2, 2)]
        for i in range(count):
            window.append(square(t, i + 2))
            t1[t, i, 0:rows_b, :] = five(kt, *window)
            window.pop(0)


def finish(t1, every, z, rows, wanted):
    k = taps()
    along_x = [five(k, *[t1[t, z, 2 + o:2 + o + rows, :] for o in range(5)]) for t in every]
    return [1.0 / (1.0 + value) for value in lane_blur(k, along_x, wanted)]


def finish_rows(t1, every, rows_b, first, nz, count, wanted):
    k = taps()
    windows = [[t1[t, pl.ds(first + 2 + o, nz, stride=rows_b), :] for o in range(4)] for t in every]
    for x in range(count):
        for t in every:
            windows[t].append(t1[t, pl.ds(first + 6 + x, nz, stride=rows_b), :])
        yield x, [1.0 / (1.0 + value) for value in lane_blur(k, [five(k, *window) for window in windows], wanted)]
        for window in windows:
            window.pop(0)


def main_kernel(dims, counts, pairs, *refs):
    nz, nx, ny = dims
    nt = ny // lanes
    own, every = tuple(range(nt)), tuple(range(nt + 1))
    refs = list(refs)
    v, zb = refs.pop(0), refs.pop(0)
    xr = [refs.pop(0) for _ in range(pairs[1])]
    yr = [refs.pop(0) for _ in range(pairs[2])]
    far = [refs.pop(0) for _ in range(pairs[1] if pairs[2] > 1 else 0)]
    bb, fz, send_z, wide, t1, cz = refs
    at_z, at_x, at_y = lax.axis_index("gz"), lax.axis_index("gx"), lax.axis_index("gy")
    nb, rows_b = nz + 8, nx + 8
    k = taps()

    gap = jnp.zeros((lanes - 2 * edge, lanes), jnp.float32)

    def halo_tile(received, cols):
        low, high = neighbours(at_y, counts[2], received, lambda ref: ref[:, cols])
        return jnp.concatenate([high, gap, low], axis=0).T

    def sides(t, load, sources):
        for i in range(nb):
            rows = slice(i * halo, (i + 1) * halo)
            low, high = neighbours(at_x, counts[1], sources, lambda source: load(source, rows))
            wide[t, i, edge - halo:edge, :] = low
            wide[t, i, edge + nx:edge + nx + halo, :] = high

    for t in own:
        sides(t, lambda ref, rows: ref[rows, cut(t)], xr)
        for i in range(nb):
            wide[t, i, edge:edge + nx, :] = zb[t, i]
    corners = []
    for e in range(pairs[1]):
        begin = nb * nx + e * lanes
        corners.append(halo_tile([yr[0].at[:, begin:begin + lanes]] + far[e:e + 1], slice(None)))
    sides(nt, lambda tile, rows: tile[rows, :], corners)
    per = lanes // nx
    for chunk in range(nb // per):
        turned = halo_tile(yr, cut(chunk))
        for i in range(per):
            wide[nt, chunk * per + i, edge:edge + nx, :] = turned[i * nx:(i + 1) * nx, :]

    blank = jnp.zeros((edge, lanes), jnp.float32)
    for z in range(nb):
        along_x = [five(k, *[wide[t, z, 2 + o:2 + o + rows_b, :] for o in range(5)]) for t in every]
        done = lane_blur(k, along_x, every)
        for t in every:
            bb[t, z, 0:edge, :] = blank
            bb[t, z, edge:edge + rows_b, :] = done[t]
            bb[t, z, edge + rows_b:, :] = blank

    masks, z_mask = grid_masks(dims, counts)

    def square_z(t, z):
        slope = bb[t, z + 5, edge:edge + rows_b, :] - bb[t, z + 3, edge:edge + rows_b, :]
        return z_mask(z, slope * slope * masks[t])

    tensor(t1, every, rows_b, square_z, nz + 1)
    before = None
    for z in range(nz + 1):
        here = finish(t1, every, z, nx, own)
        if before is not None:
            scale = 0.5 * stiffness
            if z == nz:
                scale = jnp.where(at_z < counts[0] - 1, scale, 0.0)
            for t in own:
                cz[z - 1, :, cut(t)] = (before[t] + here[t]) * scale
        before = here

    def keep_z(i, w, d, h):
        fz[0, i], fz[1, i], fz[2, i] = w, d, h

    seg = eliminate(lambda i: v[i], lambda i: cz[i], nz, keep_z)
    for i, value in enumerate(seg if counts[0] > 2 else last_message(bit_of(at_z, 0), seg)):
        send_z[i] = value


def side_kernel(dims, counts, *refs):
    nz, nx, ny = dims
    nt = ny // lanes
    own, every = tuple(range(nt)), tuple(range(nt + 1))
    v, bb, fx, fy, cy_out, send_x, send_y, t1, t2, vs, vx, cxs, cys, ct, vt = refs
    at_x, at_y = lax.axis_index("gx"), lax.axis_index("gy")
    rows_b = nx + 8
    masks, z_mask = grid_masks(dims, counts)
    kt = taps(0.25 / (contrast * contrast))

    def square_x(t, z):
        slope = bb[t, z + 4, edge + 1:edge + 1 + rows_b, :] - bb[t, z + 4, edge - 1:edge - 1 + rows_b, :]
        return z_mask(z, slope * slope * masks[t])

    for t in every:
        window = [square_x(t, z) for z in range(-2, 2)]
        for i in range(nz):
            window.append(square_x(t, i + 2))
            t1[t, i * rows_b:(i + 1) * rows_b, :] = five(kt, *window)
            window.pop(0)
    for t in own:
        for z in range(nz):
            vs[t, z * nx:(z + 1) * nx, :] = v[z, :, cut(t)]
        for x in range(nx):
            value = vs[t, pl.ds(x, nz, stride=nx), :]
            vx[t, x * nz:(x + 1) * nz, :] = value
            cxs[1, x, :, cut(t)] = value
    before = None
    for x, here in finish_rows(t1, every, rows_b, 0, nz, nx + 1, own):
        if before is not None:
            scale = 0.5 * stiffness
            if x == nx:
                scale = jnp.where(at_x < counts[1] - 1, scale, 0.0)
            for t in own:
                cxs[0, x - 1, :, cut(t)] = (before[t] + here[t]) * scale
        before = here

    def keep_x(i, w, d, h):
        fx[0, i], fx[1, i], fx[2, i] = w, d, h

    seg = eliminate(lambda i: cxs[1, i], lambda i: cxs[0, i], nx, keep_x)
    for i, value in enumerate(seg if counts[1] > 2 else last_message(bit_of(at_x, 0), seg)):
        send_x[i] = value

    def square_y_layer(z):
        tiles = [bb[t, z + 4, edge:edge + rows_b, :] for t in every]
        up, down = lane_shift(tiles, 1, every), lane_shift(tiles, -1, every)
        out = []
        for t in every:
            slope = up[t] - down[t]
            out.append(z_mask(z, slope * slope * masks[t]))
        return out

    window = [square_y_layer(z) for z in range(-2, 2)]
    for z in range(nz):
        window.append(square_y_layer(z + 2))
        for t in every:
            t2[t, z * rows_b:(z + 1) * rows_b, :] = five(kt, *[tiles[t] for tiles in window])
        window.pop(0)
    for x, here in finish_rows(t2, every, rows_b, 0, nz, nx, every):
        following = lane_shift(here, 1, own)
        for t in own:
            cys[t, x * nz:(x + 1) * nz, :] = (here[t] + following[t]) * (0.5 * stiffness)
    for t in own:
        ct[cut(t), :] = cys[t].T
        vt[cut(t), :] = vx[t].T
    closing = jnp.where(at_y < counts[2] - 1, 1.0, 0.0)
    ct[ny - 1:ny, :] = ct[ny - 1:ny, :] * closing

    steps = ny // 16
    segs = []
    for half in range(2):
        def at(ref, i, half=half):
            return ref[pl.ds(half * steps + i, 8, stride=2 * steps), :]

        def keep_y(i, w, d, h, half=half):
            fy[0, i, half], fy[1, i, half], fy[2, i, half] = w, d, h

        segs.append(eliminate(functools.partial(at, vt), functools.partial(at, ct), steps, keep_y))
    seg, coef = merge(segs[0], segs[1])
    for i in range(3):
        cy_out[0, i] = coef[i]
    for level in range(3):
        other = tuple(pltpu.roll(value, 8 - 2**level, axis=0) for value in seg)
        seg, coef = merge(seg, other)
        for i in range(3):
            cy_out[level + 1, i] = coef[i]
    seg = seg if counts[2] > 2 else last_message(bit_of(at_y, 0), seg)
    for i, value in enumerate(seg):
        send_y[i:i + 1, :] = value[0:1, :]


def summary(ref, axis, count):
    if axis == 2:
        return tuple(ref[i:i + 1, :] for i in range(count))
    return tuple(ref[i] for i in range(count))


def merge_kernel(level, depths, axes, *refs):
    refs = list(refs)
    groups = [[refs.pop(0) for _ in range(level + 2)] for _ in axes]
    for axis, group, out in zip(axes, groups, refs):
        position = lax.axis_index(("gz", "gx", "gy")[axis])
        own, *received = [summary(ref, axis, 5) for ref in group]
        seg, _ = climb(position, own, received)
        if depths[axis] == level + 2:
            seg = last_message(bit_of(position, level + 1), seg)
        for i, value in enumerate(seg):
            if axis == 2:
                out[i:i + 1, :] = value
            else:
                out[i] = value


def fluxes_of(axis, depths, group):
    position = lax.axis_index(("gz", "gx", "gy")[axis])
    if depths[axis] == 1:
        upper = bit_of(position, 0)
        mine, final = [summary(ref, axis, 2) for ref in group]
        (low_a, low_y), (high_a, high_g) = pick(upper, mine, final)
        flux = low_y * (high_a - low_a) / (1.0 + low_y * high_g)
        return jnp.where(upper, -flux, 0.0), jnp.where(upper, 0.0, flux)
    own, *received = [summary(ref, axis, 5) for ref in group[:-1]]
    return end_fluxes(position, own, received, summary(group[-1], axis, 2))


def solve_x(dims, factors, fluxes, target):
    nz, nx, ny = dims

    def emit(i, value):
        for t in range(ny // lanes):
            target[t, pl.ds(i, nz, stride=nx), :] = value[:, cut(t)]

    substitute(lambda i: (factors[0, i], factors[1, i], factors[2, i]), nx, *fluxes, emit)


def prepare_kernel(dims, depths, *refs):
    nz, nx, ny = dims
    refs = list(refs)
    v, fz, fx, fy, cy = [refs.pop(0) for _ in range(5)]
    group = [refs.pop(0) for _ in range(2 if depths[1] == 1 else 0)]
    base, by_z, by_y, sx = refs
    third = 1.0 / 3.0
    if group:
        solve_x(dims, fx, fluxes_of(1, depths, group), sx)

    sub = lax.broadcasted_iota(jnp.int32, (8, lanes), 0)
    zero = jnp.zeros((8, lanes), jnp.float32)
    left, right = (zero, zero + 1.0, zero), (zero, zero, zero + 1.0)

    def crossing(level):
        const, by_left, by_right = [cy[level, i] for i in range(3)]
        terms = [by_right * r - by_left * l for l, r in zip(left, right)]
        return [terms[0] + const] + terms[1:]

    for level in (2, 1, 0):
        stride = 2**level
        flux = crossing(level + 1)
        lower = sub % (2 * stride) == 0
        left, right = ([jnp.where(lower, l, -pltpu.roll(f, stride, axis=0)) for l, f in zip(left, flux)],
                       [jnp.where(lower, f, pltpu.roll(r, stride, axis=0)) for r, f in zip(right, flux)])
    flux = crossing(0)
    steps = ny // 16
    for half, (a, b) in enumerate(((left, flux), ([-f for f in flux], right))):
        a, b = [m * third for m in a], [m * third for m in b]

        def emit(i, own, by_left, by_right, half=half, a=a, b=b):
            at = pl.ds(half * steps + i, 8, stride=2 * steps)
            for m in range(3):
                value = by_left * a[m] + by_right * b[m]
                by_y[m, at, :] = value + own * third if m == 0 else value

        responses(lambda i, half=half: (fy[0, i, half], fy[1, i, half], fy[2, i, half]), steps, emit)

    def emit_z(i, own, by_left, by_right):
        total = own
        if group:
            total = total + jnp.concatenate([sx[t, i * nx:(i + 1) * nx, :] for t in range(ny // lanes)], axis=1)
        base[i] = v[i] + total * third
        by_z[0, i] = jnp.broadcast_to(by_left * third, (nx, ny))
        by_z[1, i] = jnp.broadcast_to(by_right * third, (nx, ny))

    responses(lambda i: (fz[0, i], fz[1, i], fz[2, i]), nz, emit_z)


def last_kernel(dims, depths, *refs):
    nz, nx, ny = dims
    nt = ny // lanes
    refs = list(refs)
    base, by_z, by_y, fx = [refs.pop(0) for _ in range(4)]
    groups = {axis: [refs.pop(0) for _ in range(depths[axis] + 1)] for axis in range(3) if axis != 1 or depths[1] > 1}
    out, st, sx = refs
    left, right = fluxes_of(2, depths, groups[2])
    for t in range(nt):
        st[t] = (by_y[0, cut(t), :] + by_y[1, cut(t), :] * left + by_y[2, cut(t), :] * right).T
    if 1 in groups:
        solve_x(dims, fx, fluxes_of(1, depths, groups[1]), sx)
    left, right = fluxes_of(0, depths, groups[0])
    for z in range(nz):
        total = base[z] + by_z[0, z] * left + by_z[1, z] * right
        rows = slice(z * nx, (z + 1) * nx)
        for t in range(nt):
            value = total[:, cut(t)] + st[t, pl.ds(z, nx, stride=nz), :]
            if 1 in groups:
                value = value + sx[t, rows, :] * (1.0 / 3.0)
            out[z, :, cut(t)] = value


def partners(n, start):
    return [i ^ 1 if start == 0 else ((i - 1) ^ 1) + 1 if 0 < i < n - 1 else n - 1 - i for i in range(n)]


def permute(value, axes, move):
    sizes = [lax.axis_size(axis) for axis in axes]
    moves = []
    for source in itertools.product(*[range(size) for size in sizes]):
        index = lambda place: functools.reduce(lambda so_far, pair: so_far * pair[1] + pair[0], zip(place, sizes), 0)
        moves.append((index(source), index(move(*source))))
    return lax.ppermute(value, axes if len(axes) > 1 else axes[0], moves)


def swap_bit(value, axis, level):
    return permute(value, (axis,), lambda i: (i ^ (2**level),))


def swap_pair(value, axis, start):
    partner = partners(lax.axis_size(axis), start)
    return permute(value, (axis,), lambda i: (partner[i],))


def swap_z(value, start):
    n = lax.axis_size("gz")
    partner = partners(n, start)
    if start == 0:
        return swap_pair(value, "gz", 0)
    return permute(value, ("gy", "gz"), lambda y, z: (y, partner[z]) if 0 < z < n - 1 else (y ^ 1, z))


def swap_corner(value, x_start, y_start):
    of_x, of_y = partners(lax.axis_size("gx"), x_start), partners(lax.axis_size("gy"), y_start)
    return permute(value, ("gx", "gy"), lambda x, y: (of_x[x], of_y[y]))


def body(volume):
    dims = volume.shape
    nz, nx, ny = dims
    nt = ny // lanes
    names = ("gz", "gx", "gy")
    counts = tuple(lax.axis_size(name) for name in names)
    depths = tuple(count.bit_length() - 1 for count in counts)
    pairs = tuple(1 if count == 2 else 2 for count in counts)
    nb, rows_b = nz + 8, nx + 8
    assert all(2**d == n and d >= 1 for d, n in zip(depths, counts))
    assert nz == 8 and nz * nx == lanes and nx >= 8 and nb * nx % lanes == 0 and nb * halo <= lanes
    f32 = lambda *shape: jax.ShapeDtypeStruct(shape, jnp.float32)
    scratch = lambda *shape: pltpu.VMEM(shape, jnp.float32)

    def call(kernel, out_shape, scratch_shapes, *args):
        return pl.pallas_call(
            kernel, out_shape=out_shape, in_specs=[VMEM] * len(args), out_specs=[VMEM] * len(out_shape),
            scratch_shapes=scratch_shapes,
            compiler_params=pltpu.CompilerParams(vmem_limit_bytes=16 * 2**20),
        )(*args)

    volume, *z_sends = call(
        functools.partial(open_kernel, dims), [f32(*dims)] + [f32(halo, nx, ny)] * pairs[0], [], volume)
    z_received = [swap_z(value, e) for e, value in enumerate(z_sends)]
    ex, ey = range(pairs[1]), range(pairs[2])
    far = ex if pairs[2] > 1 else []
    blurred_z, *sends = call(
        functools.partial(z_kernel, dims, counts, pairs),
        [f32(nt, nb, nx, lanes)] + [f32(nb * halo, ny) for e in ex] + [f32(edge, nb * nx) for f in ey]
        + [f32(edge, lanes) for e in far], [], volume, *z_received)
    x_received = [swap_pair(sends[e], "gx", e) for e in ex]
    y_sends = sends[pairs[1]:pairs[1] + pairs[2]]
    corners = [swap_corner(sends[pairs[1] + pairs[2] + e], e, 1) for e in far]
    y_received = [swap_pair(value, "gy", 1) for value in y_sends[1:]]
    y_sends[0], = call(functools.partial(pack_kernel, dims), [f32(edge, nb * nx + pairs[1] * lanes)], [],
                       y_sends[0], *x_received)
    y_received.insert(0, swap_pair(y_sends[0], "gy", 0))

    steps = ny // 16
    send_shape = lambda d: 5 if d > 1 else 2
    bb, fz, send_z = call(
        functools.partial(main_kernel, dims, counts, pairs),
        [f32(nt + 1, nb, rows_b + 2 * edge, lanes), f32(3, nz - 1, nx, ny), f32(send_shape(depths[0]), nx, ny)],
        [scratch(nt + 1, nb, nx + 2 * edge, lanes), scratch(nt + 1, nz + 1, rows_b + 8, lanes), scratch(nz, nx, ny)],
        volume, blurred_z, *x_received, *y_received, *corners)
    fx, fy, cy, send_x, send_y = call(
        functools.partial(side_kernel, dims, counts),
        [f32(3, nx - 1, nz, ny), f32(3, steps - 1, 2, 8, lanes), f32(4, 3, 8, lanes),
         f32(send_shape(depths[1]), nz, ny), f32(8, lanes)],
        [scratch(nt + 1, nz * rows_b, lanes)] * 2 + [scratch(nt, lanes, lanes)] * 2
        + [scratch(2, nx, nz, ny), scratch(nt, lanes, lanes), scratch(ny, lanes), scratch(ny, lanes)],
        volume, bb)

    groups = [[send_z], [send_x], [send_y]]
    message = [send_z, send_x, send_y]
    for level in range(max(depths)):
        for axis in range(3):
            if level < depths[axis]:
                groups[axis].append(swap_bit(message[axis], names[axis], level))
        axes = [axis for axis in range(3) if depths[axis] > level + 1]
        if axes:
            shapes = []
            for axis in axes:
                count = 2 if depths[axis] == level + 2 else 5
                shapes.append(f32(8, lanes) if axis == 2 else f32(count, *((nx, ny) if axis == 0 else (nz, ny))))
            sent = call(functools.partial(merge_kernel, level, depths, axes), shapes, [],
                        *[ref for axis in axes for ref in groups[axis]])
            for axis, value in zip(axes, sent):
                message[axis] = value
    x_group = groups[1] if depths[1] == 1 else []
    base, by_z, by_y = call(
        functools.partial(prepare_kernel, dims, depths), [f32(*dims), f32(2, *dims), f32(3, ny, lanes)],
        [scratch(nt, lanes, lanes)], volume, fz, fx, fy, cy, *x_group)
    rest = groups[0] + ([] if x_group else groups[1]) + groups[2]
    return call(
        functools.partial(last_kernel, dims, depths), [f32(*dims)],
        [scratch(nt, lanes, lanes), scratch(nt, lanes, lanes)], base, by_z, by_y, fx, *rest)[0]


def solution(mesh):
    return jax.shard_map(
        body,
        mesh=mesh,
        in_specs=(P("gz", "gx", "gy"),),
        out_specs=P("gz", "gx", "gy"),
        check_vma=False,
    )
```

```python
import functools
import itertools

import jax
import jax.numpy as jnp
from jax import lax
from jax.experimental import pallas as pl
from jax.experimental.pallas import tpu as pltpu
from jax.sharding import PartitionSpec as P


kernel_taps = (0.41111229, 0.8007374, 1.0, 0.8007374, 0.41111229)
time_step = 3000.0
contrast = 0.1
stiffness = 3.0 * time_step
halo = 6
lanes = 128
edge = 8
VMEM = pl.BlockSpec(memory_space=pltpu.VMEM)


def taps(scale=1.0):
    total = sum(kernel_taps)
    return tuple(scale * tap / total for tap in kernel_taps[:3])


def five(k, a, b, c, d, e):
    return k[0] * (a + e) + k[1] * (b + d) + k[2] * c


def lane_shift(tiles, k, wanted):
    count = len(tiles)
    rolled = [pltpu.roll(t, (-k) % lanes, axis=1) for t in tiles]
    lane = lax.broadcasted_iota(jnp.int32, tiles[0].shape, 1)
    out = []
    for t in wanted:
        if k > 0:
            out.append(jnp.where(lane < lanes - k, rolled[t], rolled[(t + 1) % count]))
        else:
            out.append(jnp.where(lane >= -k, rolled[t], rolled[(t - 1) % count]))
    return out


def lane_blur(k, tiles, wanted):
    s = {o: lane_shift(tiles, o, wanted) for o in (-2, -1, 1, 2)}
    return [five(k, s[-2][i], s[-1][i], tiles[t], s[1][i], s[2][i]) for i, t in enumerate(wanted)]


def merge(low, high):
    a0, an, g00, g0n, y = low
    b0, bn, h00, h0n, e = high
    w = y / (1.0 + y * h00)
    flux = w * (b0 - an)
    by_left = w * g0n
    by_right = w * h0n
    joined = (a0 + g0n * flux, bn - h0n * flux, g00 - g0n * by_left, by_left * h0n, e / (1.0 - e * (h0n * by_right)))
    return joined, (flux, by_left, by_right)


def pick(upper, own, other):
    low = tuple(jnp.where(upper, o, m) for m, o in zip(own, other))
    high = tuple(jnp.where(upper, m, o) for m, o in zip(own, other))
    return low, high


def last_message(upper, seg):
    a0, an, g00, _, y = seg
    return jnp.where(upper, a0, an), jnp.where(upper, g00, y)


def bit_of(position, level):
    return (position // (2**level)) % 2 == 1


def climb(position, own, received):
    coefs = []
    for level, other in enumerate(received):
        low, high = pick(bit_of(position, level), own, other)
        own, coef = merge(low, high)
        coefs.append(coef)
    return own, coefs


def end_fluxes(position, own, received, final):
    seg, coefs = climb(position, own, received)
    top = len(received)
    upper = bit_of(position, top)
    mine = last_message(upper, seg)
    (low_a, low_y), (high_a, high_g) = pick(upper, mine, final)
    flux = low_y * (high_a - low_a) / (1.0 + low_y * high_g)
    left = jnp.where(upper, -flux, 0.0)
    right = jnp.where(upper, 0.0, flux)
    for level in reversed(range(top)):
        const, by_left, by_right = coefs[level]
        flux = const + by_right * right - by_left * left
        upper = bit_of(position, level)
        left, right = jnp.where(upper, -flux, left), jnp.where(upper, right, flux)
    return left, right


def eliminate(v, c, count, keep):
    a0 = an = v(0)
    g00 = g0n = gnn = jnp.ones_like(an)
    for i in range(count - 1):
        face = c(i)
        w = face / (1.0 + face * (gnn + 1.0))
        following = v(i + 1)
        d = following - an
        keep(i, w, d, g0n)
        flux = w * d
        a0 = a0 + g0n * flux
        an = following - flux
        hw = g0n * w
        g00 = g00 - g0n * hw
        g0n = hw
        gnn = 1.0 - w
    face = c(count - 1)
    return a0, an, g00, g0n, face / (1.0 + face * gnn)


def substitute(factors, count, left, right, emit):
    above = right
    for i in reversed(range(count - 1)):
        w, d, h = factors(i)
        flux = w * (d + above - h * left)
        emit(i + 1, above - flux)
        above = flux
    emit(0, above + left)


def responses(factors, count, emit):
    base, by_left, by_right = 0.0, 0.0, 1.0
    for i in reversed(range(count - 1)):
        w, d, h = factors(i)
        flux = w * (d + base), w * (by_left - h), w * by_right
        emit(i + 1, base - flux[0], by_left - flux[1], by_right - flux[2])
        base, by_left, by_right = flux
    emit(0, base, by_left + 1.0, by_right)


def cut(t):
    return slice(t * lanes, (t + 1) * lanes)


def z_blur(load, store, count, weights):
    window = [load(i) for i in range(4)]
    for i in range(count):
        window.append(load(i + 4))
        store(i, five(weights, *window))
        window.pop(0)


def neighbours(position, count, refs, load):
    odd = position % 2 == 1
    first = load(refs[0])
    if len(refs) > 1:
        end = (position == 0) | (position == count - 1)
        second = jnp.where(end, 0.0, load(refs[1]))
    else:
        second = jnp.zeros_like(first)
    return jnp.where(odd, first, second), jnp.where(odd, second, first)


def open_kernel(dims, volume, kept):
    for z in range(dims[0]):
        kept[z] = volume[z]


def z_kernel(dims, counts, pairs, *refs):
    nz, nx, ny = dims
    nt, nb = ny // lanes, nz + 8
    v, zr = refs[0], refs[1:1 + pairs[0]]
    out, *sends = refs[1 + pairs[0]:]
    x_sends, y_sends = sends[:pairs[1]], sends[pairs[1]:pairs[1] + pairs[2]]
    corner_sends = sends[pairs[1] + pairs[2]:]
    at_z = lax.axis_index("gz")
    odd_x = lax.axis_index("gx") % 2 == 1
    odd_y = lax.axis_index("gy") % 2 == 1
    for t in range(nt):
        cols = cut(t)
        below = [neighbours(at_z, counts[0], zr, lambda ref: ref[nz - halo + z, :, cols])[0] for z in range(halo)]
        above = [neighbours(at_z, counts[0], zr, lambda ref: ref[z, :, cols])[1] for z in range(halo)]

        def load(z):
            if z < halo:
                return below[z]
            return v[z - halo, :, cols] if z < halo + nz else above[z - halo - nz]

        def store(i, value):
            out[t, i] = value
            low, high = value[:halo], value[nx - halo:]
            rows = slice(i * halo, (i + 1) * halo)
            x_sends[0][rows, cols] = jnp.where(odd_x, low, high)
            if len(x_sends) > 1:
                x_sends[1][rows, cols] = jnp.where(odd_x, high, low)

        z_blur(load, store, nb, taps())

    per = lanes // nx
    for chunk in range(nb // per):
        tiles = [out[t, chunk * per:(chunk + 1) * per].reshape(lanes, lanes) for t in (0, nt - 1)]
        for f, ref in enumerate(y_sends):
            ref[:, cut(chunk)] = strip(odd_y, f, *tiles)
    pad = jnp.zeros((lanes - nb * halo, lanes), jnp.float32)
    for ref, corner in zip(x_sends, corner_sends):
        corner[...] = strip(odd_y, 1, *[jnp.concatenate([ref[:, cut(t)], pad], axis=0) for t in (0, nt - 1)])


def strip(odd_y, f, first_tile, last_tile):
    first, last = first_tile.T[:edge, :], last_tile.T[lanes - edge:, :]
    return jnp.where(odd_y, last, first) if f else jnp.where(odd_y, first, last)


def pack_kernel(dims, *refs):
    nz, nx, ny = dims
    nt, nb = ny // lanes, nz + 8
    own, xr, out = refs[0], refs[1:-1], refs[-1]
    odd_y = lax.axis_index("gy") % 2 == 1
    out[:, :nb * nx] = own[...]
    pad = jnp.zeros((lanes - nb * halo, lanes), jnp.float32)
    for e, ref in enumerate(xr):
        tiles = [jnp.concatenate([ref[:, cut(t)], pad], axis=0) for t in (0, nt - 1)]
        begin = nb * nx + e * lanes
        out[:, begin:begin + lanes] = strip(odd_y, 0, *tiles)


def grid_masks(dims, counts):
    nz, nx, ny = dims
    nt = ny // lanes
    at_z, at_x, at_y = lax.axis_index("gz"), lax.axis_index("gx"), lax.axis_index("gy")
    rows_b = nx + 8
    xi = at_x * nx + lax.broadcasted_iota(jnp.int32, (rows_b, lanes), 0) - 4
    x_mask = jnp.where((xi >= 0) & (xi < nx * counts[1]), 1.0, 0.0)
    lane = lax.broadcasted_iota(jnp.int32, (rows_b, lanes), 1)
    not_first = (at_y > 0).astype(jnp.float32)
    not_last = (at_y < counts[2] - 1).astype(jnp.float32)
    masks = [x_mask] * nt + [x_mask * jnp.where(lane < lanes // 2, not_last, not_first)]

    def z_mask(z, value):
        if 0 <= z < nz:
            return value
        inside = (at_z > 0) if z < 0 else (at_z < counts[0] - 1)
        return value * inside.astype(jnp.float32)

    return masks, z_mask


def tensor(t1, every, rows_b, square, count):
    kt = taps(0.25 / (contrast * contrast))
    for t in every:
        window = [square(t, z) for z in range(-2, 2)]
        for i in range(count):
            window.append(square(t, i + 2))
            t1[t, i, 0:rows_b, :] = five(kt, *window)
            window.pop(0)


def finish(t1, every, z, rows, wanted):
    k = taps()
    along_x = [five(k, *[t1[t, z, 2 + o:2 + o + rows, :] for o in range(5)]) for t in every]
    return [1.0 / (1.0 + value) for value in lane_blur(k, along_x, wanted)]


def finish_rows(t1, every, rows_b, first, nz, count, wanted):
    k = taps()
    windows = [[t1[t, pl.ds(first + 2 + o, nz, stride=rows_b), :] for o in range(4)] for t in every]
    for x in range(count):
        for t in every:
            windows[t].append(t1[t, pl.ds(first + 6 + x, nz, stride=rows_b), :])
        yield x, [1.0 / (1.0 + value) for value in lane_blur(k, [five(k, *window) for window in windows], wanted)]
        for window in windows:
            window.pop(0)


def main_kernel(dims, counts, pairs, *refs):
    nz, nx, ny = dims
    nt = ny // lanes
    own, every = tuple(range(nt)), tuple(range(nt + 1))
    refs = list(refs)
    v, zb = refs.pop(0), refs.pop(0)
    xr = [refs.pop(0) for _ in range(pairs[1])]
    yr = [refs.pop(0) for _ in range(pairs[2])]
    far = [refs.pop(0) for _ in range(pairs[1] if pairs[2] > 1 else 0)]
    bb, fz, send_z, wide, t1, cz = refs
    at_z, at_x, at_y = lax.axis_index("gz"), lax.axis_index("gx"), lax.axis_index("gy")
    nb, rows_b = nz + 8, nx + 8
    k = taps()

    gap = jnp.zeros((lanes - 2 * edge, lanes), jnp.float32)

    def halo_tile(received, cols):
        low, high = neighbours(at_y, counts[2], received, lambda ref: ref[:, cols])
        return jnp.concatenate([high, gap, low], axis=0).T

    def sides(t, load, sources):
        for i in range(nb):
            rows = slice(i * halo, (i + 1) * halo)
            low, high = neighbours(at_x, counts[1], sources, lambda source: load(source, rows))
            wide[t, i, edge - halo:edge, :] = low
            wide[t, i, edge + nx:edge + nx + halo, :] = high

    for t in own:
        sides(t, lambda ref, rows: ref[rows, cut(t)], xr)
        for i in range(nb):
            wide[t, i, edge:edge + nx, :] = zb[t, i]
    corners = []
    for e in range(pairs[1]):
        begin = nb * nx + e * lanes
        corners.append(halo_tile([yr[0].at[:, begin:begin + lanes]] + far[e:e + 1], slice(None)))
    sides(nt, lambda tile, rows: tile[rows, :], corners)
    per = lanes // nx
    for chunk in range(nb // per):
        turned = halo_tile(yr, cut(chunk))
        for i in range(per):
            wide[nt, chunk * per + i, edge:edge + nx, :] = turned[i * nx:(i + 1) * nx, :]

    blank = jnp.zeros((edge, lanes), jnp.float32)
    for z in range(nb):
        along_x = [five(k, *[wide[t, z, 2 + o:2 + o + rows_b, :] for o in range(5)]) for t in every]
        done = lane_blur(k, along_x, every)
        for t in every:
            bb[t, z, 0:edge, :] = blank
            bb[t, z, edge:edge + rows_b, :] = done[t]
            bb[t, z, edge + rows_b:, :] = blank

    masks, z_mask = grid_masks(dims, counts)

    def square_z(t, z):
        slope = bb[t, z + 5, edge:edge + rows_b, :] - bb[t, z + 3, edge:edge + rows_b, :]
        return z_mask(z, slope * slope * masks[t])

    tensor(t1, every, rows_b, square_z, nz + 1)
    before = None
    for z in range(nz + 1):
        here = finish(t1, every, z, nx, own)
        if before is not None:
            scale = 0.5 * stiffness
            if z == nz:
                scale = jnp.where(at_z < counts[0] - 1, scale, 0.0)
            for t in own:
                cz[z - 1, :, cut(t)] = (before[t] + here[t]) * scale
        before = here

    def keep_z(i, w, d, h):
        fz[0, i], fz[1, i], fz[2, i] = w, d, h

    seg = eliminate(lambda i: v[i], lambda i: cz[i], nz, keep_z)
    for i, value in enumerate(seg if counts[0] > 2 else last_message(bit_of(at_z, 0), seg)):
        send_z[i] = value


def side_kernel(dims, counts, *refs):
    nz, nx, ny = dims
    nt = ny // lanes
    own, every = tuple(range(nt)), tuple(range(nt + 1))
    v, bb, fx, fy, cy_out, send_x, send_y, t1, t2, vs, vx, cxs, cys, ct, vt = refs
    at_x, at_y = lax.axis_index("gx"), lax.axis_index("gy")
    rows_b = nx + 8
    masks, z_mask = grid_masks(dims, counts)
    kt = taps(0.25 / (contrast * contrast))

    def square_x(t, z):
        slope = bb[t, z + 4, edge + 1:edge + 1 + rows_b, :] - bb[t, z + 4, edge - 1:edge - 1 + rows_b, :]
        return z_mask(z, slope * slope * masks[t])

    for t in every:
        window = [square_x(t, z) for z in range(-2, 2)]
        for i in range(nz):
            window.append(square_x(t, i + 2))
            t1[t, i * rows_b:(i + 1) * rows_b, :] = five(kt, *window)
            window.pop(0)
    for t in own:
        for z in range(nz):
            vs[t, z * nx:(z + 1) * nx, :] = v[z, :, cut(t)]
        for x in range(nx):
            value = vs[t, pl.ds(x, nz, stride=nx), :]
            vx[t, x * nz:(x + 1) * nz, :] = value
            cxs[1, x, :, cut(t)] = value
    before = None
    for x, here in finish_rows(t1, every, rows_b, 0, nz, nx + 1, own):
        if before is not None:
            scale = 0.5 * stiffness
            if x == nx:
                scale = jnp.where(at_x < counts[1] - 1, scale, 0.0)
            for t in own:
                cxs[0, x - 1, :, cut(t)] = (before[t] + here[t]) * scale
        before = here

    def keep_x(i, w, d, h):
        fx[0, i], fx[1, i], fx[2, i] = w, d, h

    seg = eliminate(lambda i: cxs[1, i], lambda i: cxs[0, i], nx, keep_x)
    for i, value in enumerate(seg if counts[1] > 2 else last_message(bit_of(at_x, 0), seg)):
        send_x[i] = value

    def square_y_layer(z):
        tiles = [bb[t, z + 4, edge:edge + rows_b, :] for t in every]
        up, down = lane_shift(tiles, 1, every), lane_shift(tiles, -1, every)
        out = []
        for t in every:
            slope = up[t] - down[t]
            out.append(z_mask(z, slope * slope * masks[t]))
        return out

    window = [square_y_layer(z) for z in range(-2, 2)]
    for z in range(nz):
        window.append(square_y_layer(z + 2))
        for t in every:
            t2[t, z * rows_b:(z + 1) * rows_b, :] = five(kt, *[tiles[t] for tiles in window])
        window.pop(0)
    for x, here in finish_rows(t2, every, rows_b, 0, nz, nx, every):
        following = lane_shift(here, 1, own)
        for t in own:
            cys[t, x * nz:(x + 1) * nz, :] = (here[t] + following[t]) * (0.5 * stiffness)
    for t in own:
        ct[cut(t), :] = cys[t].T
        vt[cut(t), :] = vx[t].T
    closing = jnp.where(at_y < counts[2] - 1, 1.0, 0.0)
    ct[ny - 1:ny, :] = ct[ny - 1:ny, :] * closing

    steps = ny // 16
    segs = []
    for half in range(2):
        def at(ref, i, half=half):
            return ref[pl.ds(half * steps + i, 8, stride=2 * steps), :]

        def keep_y(i, w, d, h, half=half):
            fy[0, i, half], fy[1, i, half], fy[2, i, half] = w, d, h

        segs.append(eliminate(functools.partial(at, vt), functools.partial(at, ct), steps, keep_y))
    seg, coef = merge(segs[0], segs[1])
    for i in range(3):
        cy_out[0, i] = coef[i]
    for level in range(3):
        other = tuple(pltpu.roll(value, 8 - 2**level, axis=0) for value in seg)
        seg, coef = merge(seg, other)
        for i in range(3):
            cy_out[level + 1, i] = coef[i]
    seg = seg if counts[2] > 2 else last_message(bit_of(at_y, 0), seg)
    for i, value in enumerate(seg):
        send_y[i:i + 1, :] = value[0:1, :]


def summary(ref, axis, count):
    if axis == 2:
        return tuple(ref[i:i + 1, :] for i in range(count))
    return tuple(ref[i] for i in range(count))


def merge_kernel(level, depths, axes, *refs):
    refs = list(refs)
    groups = [[refs.pop(0) for _ in range(level + 2)] for _ in axes]
    for axis, group, out in zip(axes, groups, refs):
        position = lax.axis_index(("gz", "gx", "gy")[axis])
        own, *received = [summary(ref, axis, 5) for ref in group]
        seg, _ = climb(position, own, received)
        if depths[axis] == level + 2:
            seg = last_message(bit_of(position, level + 1), seg)
        for i, value in enumerate(seg):
            if axis == 2:
                out[i:i + 1, :] = value
            else:
                out[i] = value


def fluxes_of(axis, depths, group):
    position = lax.axis_index(("gz", "gx", "gy")[axis])
    if depths[axis] == 1:
        upper = bit_of(position, 0)
        mine, final = [summary(ref, axis, 2) for ref in group]
        (low_a, low_y), (high_a, high_g) = pick(upper, mine, final)
        flux = low_y * (high_a - low_a) / (1.0 + low_y * high_g)
        return jnp.where(upper, -flux, 0.0), jnp.where(upper, 0.0, flux)
    own, *received = [summary(ref, axis, 5) for ref in group[:-1]]
    return end_fluxes(position, own, received, summary(group[-1], axis, 2))


def solve_x(dims, factors, fluxes, target):
    nz, nx, ny = dims

    def emit(i, value):
        for t in range(ny // lanes):
            target[t, pl.ds(i, nz, stride=nx), :] = value[:, cut(t)]

    substitute(lambda i: (factors[0, i], factors[1, i], factors[2, i]), nx, *fluxes, emit)


def prepare_kernel(dims, depths, *refs):
    nz, nx, ny = dims
    refs = list(refs)
    v, fz, fx, fy, cy = [refs.pop(0) for _ in range(5)]
    group = [refs.pop(0) for _ in range(2 if depths[1] == 1 else 0)]
    base, by_z, by_y, sx = refs
    third = 1.0 / 3.0
    if group:
        solve_x(dims, fx, fluxes_of(1, depths, group), sx)

    sub = lax.broadcasted_iota(jnp.int32, (8, lanes), 0)
    zero = jnp.zeros((8, lanes), jnp.float32)
    left, right = (zero, zero + 1.0, zero), (zero, zero, zero + 1.0)

    def crossing(level):
        const, by_left, by_right = [cy[level, i] for i in range(3)]
        terms = [by_right * r - by_left * l for l, r in zip(left, right)]
        return [terms[0] + const] + terms[1:]

    for level in (2, 1, 0):
        stride = 2**level
        flux = crossing(level + 1)
        lower = sub % (2 * stride) == 0
        left, right = ([jnp.where(lower, l, -pltpu.roll(f, stride, axis=0)) for l, f in zip(left, flux)],
                       [jnp.where(lower, f, pltpu.roll(r, stride, axis=0)) for r, f in zip(right, flux)])
    flux = crossing(0)
    steps = ny // 16
    for half, (a, b) in enumerate(((left, flux), ([-f for f in flux], right))):
        a, b = [m * third for m in a], [m * third for m in b]

        def emit(i, own, by_left, by_right, half=half, a=a, b=b):
            at = pl.ds(half * steps + i, 8, stride=2 * steps)
            for m in range(3):
                value = by_left * a[m] + by_right * b[m]
                by_y[m, at, :] = value + own * third if m == 0 else value

        responses(lambda i, half=half: (fy[0, i, half], fy[1, i, half], fy[2, i, half]), steps, emit)

    def emit_z(i, own, by_left, by_right):
        total = own
        if group:
            total = total + jnp.concatenate([sx[t, i * nx:(i + 1) * nx, :] for t in range(ny // lanes)], axis=1)
        base[i] = v[i] + total * third
        by_z[0, i] = jnp.broadcast_to(by_left * third, (nx, ny))
        by_z[1, i] = jnp.broadcast_to(by_right * third, (nx, ny))

    responses(lambda i: (fz[0, i], fz[1, i], fz[2, i]), nz, emit_z)


def last_kernel(dims, depths, *refs):
    nz, nx, ny = dims
    nt = ny // lanes
    refs = list(refs)
    base, by_z, by_y, fx = [refs.pop(0) for _ in range(4)]
    groups = {axis: [refs.pop(0) for _ in range(depths[axis] + 1)] for axis in range(3) if axis != 1 or depths[1] > 1}
    out, st, sx = refs
    left, right = fluxes_of(2, depths, groups[2])
    for t in range(nt):
        st[t] = (by_y[0, cut(t), :] + by_y[1, cut(t), :] * left + by_y[2, cut(t), :] * right).T
    if 1 in groups:
        solve_x(dims, fx, fluxes_of(1, depths, groups[1]), sx)
    left, right = fluxes_of(0, depths, groups[0])
    for z in range(nz):
        total = base[z] + by_z[0, z] * left + by_z[1, z] * right
        rows = slice(z * nx, (z + 1) * nx)
        for t in range(nt):
            value = total[:, cut(t)] + st[t, pl.ds(z, nx, stride=nz), :]
            if 1 in groups:
                value = value + sx[t, rows, :] * (1.0 / 3.0)
            out[z, :, cut(t)] = value


def partners(n, start):
    return [i ^ 1 if start == 0 else ((i - 1) ^ 1) + 1 if 0 < i < n - 1 else n - 1 - i for i in range(n)]


def permute(value, axes, move):
    sizes = [lax.axis_size(axis) for axis in axes]
    moves = []
    for source in itertools.product(*[range(size) for size in sizes]):
        index = lambda place: functools.reduce(lambda so_far, pair: so_far * pair[1] + pair[0], zip(place, sizes), 0)
        moves.append((index(source), index(move(*source))))
    return lax.ppermute(value, axes if len(axes) > 1 else axes[0], moves)


def swap_bit(value, axis, level):
    return permute(value, (axis,), lambda i: (i ^ (2**level),))


def swap_pair(value, axis, start):
    n = lax.axis_size(axis)
    partner = partners(n, start)
    if axis == "gy" and start == 1:
        move = lambda y, z: (partner[y], z) if 0 < y < n - 1 else (y, z ^ 1)
        return permute(value, ("gy", "gz"), move)
    return permute(value, (axis,), lambda i: (partner[i],))


def swap_z(value, start):
    n = lax.axis_size("gz")
    partner = partners(n, start)
    if start == 0:
        return swap_pair(value, "gz", 0)
    return permute(value, ("gy", "gz"), lambda y, z: (y, partner[z]) if 0 < z < n - 1 else (y ^ 1, z))


def swap_corner(value, x_start, y_start):
    of_x, of_y = partners(lax.axis_size("gx"), x_start), partners(lax.axis_size("gy"), y_start)
    return permute(value, ("gx", "gy"), lambda x, y: (of_x[x], of_y[y] if 0 < y < len(of_y) - 1 else y))


def body(volume):
    dims = volume.shape
    nz, nx, ny = dims
    nt = ny // lanes
    names = ("gz", "gx", "gy")
    counts = tuple(lax.axis_size(name) for name in names)
    depths = tuple(count.bit_length() - 1 for count in counts)
    pairs = tuple(1 if count == 2 else 2 for count in counts)
    nb, rows_b = nz + 8, nx + 8
    assert all(2**d == n and d >= 1 for d, n in zip(depths, counts))
    assert nz == 8 and nz * nx == lanes and nx >= 8 and nb * nx % lanes == 0 and nb * halo <= lanes
    f32 = lambda *shape: jax.ShapeDtypeStruct(shape, jnp.float32)
    scratch = lambda *shape: pltpu.VMEM(shape, jnp.float32)

    def call(kernel, out_shape, scratch_shapes, *args):
        return pl.pallas_call(
            kernel, out_shape=out_shape, in_specs=[VMEM] * len(args), out_specs=[VMEM] * len(out_shape),
            scratch_shapes=scratch_shapes,
            compiler_params=pltpu.CompilerParams(vmem_limit_bytes=16 * 2**20),
        )(*args)

    z_received = [swap_z(volume, e) for e in range(pairs[0])]
    volume, = call(functools.partial(open_kernel, dims), [f32(*dims)], [], volume)
    ex, ey = range(pairs[1]), range(pairs[2])
    far = ex if pairs[2] > 1 else []
    blurred_z, *sends = call(
        functools.partial(z_kernel, dims, counts, pairs),
        [f32(nt, nb, nx, lanes)] + [f32(nb * halo, ny) for e in ex] + [f32(edge, nb * nx) for f in ey]
        + [f32(edge, lanes) for e in far], [], volume, *z_received)
    x_received = [swap_pair(sends[e], "gx", e) for e in ex]
    y_sends = sends[pairs[1]:pairs[1] + pairs[2]]
    corners = [swap_corner(sends[pairs[1] + pairs[2] + e], e, 1) for e in far]
    y_received = [swap_pair(value, "gy", 1) for value in y_sends[1:]]
    y_sends[0], = call(functools.partial(pack_kernel, dims), [f32(edge, nb * nx + pairs[1] * lanes)], [],
                       y_sends[0], *x_received)
    y_received.insert(0, swap_pair(y_sends[0], "gy", 0))

    steps = ny // 16
    send_shape = lambda d: 5 if d > 1 else 2
    bb, fz, send_z = call(
        functools.partial(main_kernel, dims, counts, pairs),
        [f32(nt + 1, nb, rows_b + 2 * edge, lanes), f32(3, nz - 1, nx, ny), f32(send_shape(depths[0]), nx, ny)],
        [scratch(nt + 1, nb, nx + 2 * edge, lanes), scratch(nt + 1, nz + 1, rows_b + 8, lanes), scratch(nz, nx, ny)],
        volume, blurred_z, *x_received, *y_received, *corners)
    fx, fy, cy, send_x, send_y = call(
        functools.partial(side_kernel, dims, counts),
        [f32(3, nx - 1, nz, ny), f32(3, steps - 1, 2, 8, lanes), f32(4, 3, 8, lanes),
         f32(send_shape(depths[1]), nz, ny), f32(8, lanes)],
        [scratch(nt + 1, nz * rows_b, lanes)] * 2 + [scratch(nt, lanes, lanes)] * 2
        + [scratch(2, nx, nz, ny), scratch(nt, lanes, lanes), scratch(ny, lanes), scratch(ny, lanes)],
        volume, bb)

    groups = [[send_z], [send_x], [send_y]]
    message = [send_z, send_x, send_y]
    for level in range(max(depths)):
        for axis in range(3):
            if level < depths[axis]:
                groups[axis].append(swap_bit(message[axis], names[axis], level))
        axes = [axis for axis in range(3) if depths[axis] > level + 1]
        if axes:
            shapes = []
            for axis in axes:
                count = 2 if depths[axis] == level + 2 else 5
                shapes.append(f32(8, lanes) if axis == 2 else f32(count, *((nx, ny) if axis == 0 else (nz, ny))))
            sent = call(functools.partial(merge_kernel, level, depths, axes), shapes, [],
                        *[ref for axis in axes for ref in groups[axis]])
            for axis, value in zip(axes, sent):
                message[axis] = value
    x_group = groups[1] if depths[1] == 1 else []
    base, by_z, by_y = call(
        functools.partial(prepare_kernel, dims, depths), [f32(*dims), f32(2, *dims), f32(3, ny, lanes)],
        [scratch(nt, lanes, lanes)], volume, fz, fx, fy, cy, *x_group)
    rest = groups[0] + ([] if x_group else groups[1]) + groups[2]
    return call(
        functools.partial(last_kernel, dims, depths), [f32(*dims)],
        [scratch(nt, lanes, lanes), scratch(nt, lanes, lanes)], base, by_z, by_y, fx, *rest)[0]


def solution(mesh):
    return jax.shard_map(
        body,
        mesh=mesh,
        in_specs=(P("gz", "gx", "gy"),),
        out_specs=P("gz", "gx", "gy"),
        check_vma=False,
    )
```
